256 devices in a mesh: dp: 16 (over x_hi, y, core), tensor: 16 (over z, x_lo).
Axes of the slice: x: 4 (x_hi: 2, x_lo: 2; x = x_hi * 2 + x_lo), y: 4, z: 8, core: 2. Of those that a mesh axis runs over, the one named last changes fastest.
Arguments:
- out_grad: bfloat16 [8192, 4096], P('dp', 'tensor'), may hold values from -6 to 6
- gate_act: bfloat16 [8192, 14336], P('dp', 'tensor'), may hold values from -8 to 8
- up_act: bfloat16 [8192, 14336], P('dp', 'tensor'), may hold values from -6 to 6
- w_down: bfloat16 [4096, 14336], P('dp', 'tensor'), may hold values from -0.09375 to 0.09375
Outputs:
- gate_grad: bfloat16 [8192, 14336], P('dp', 'tensor')
- up_grad: bfloat16 [8192, 14336], P('dp', 'tensor')
- down_grad: bfloat16 [4096, 14336], P('dp', 'tensor')
The draws below stay inside these ranges and needn't reach their ends.
All inputs are finite; a program needn't handle non-finite values.
Results may differ from the reference program's by a relative error of at most 0.0049.
Values may be sent and summed in bfloat16 or wider, within the bound.
A program may use at most 128 MiB of HBM per device.

```python
import math
import jax
import jax.numpy as jnp
from jax import lax

D = 4096
FF = 14336
SEQ = 512
TOKENS = 8192
N_DP = 16


def levels(key, shape, split, smallest, high):
    factor_of = 1.0
    for position, shards_of in split:
        draws = jax.random.uniform(jax.random.fold_in(jax.random.fold_in(key, 6), position), (shards_of,), jnp.float32, smallest / len(split), high / len(split))
        factor_of = factor_of * jnp.repeat(jnp.exp(draws), shape[position] // shards_of).reshape((-1,) + (1,) * (len(shape) - 1 - position))
    return factor_of


def bell_draw(stream_key, dims, deviation, reach, split=(), kind=jnp.bfloat16):
    entries = jax.random.normal(stream_key, dims, jnp.float32) * deviation
    if len(split) > 0:
        entries = levels(stream_key, dims, split, -0.22, 0.18) * entries
    return jnp.clip(entries, min=-reach, max=reach).astype(kind)


def setup_inputs(seed: int = 0) -> dict:
    streams_of = jax.random.split(jax.random.key(seed), 5)
    out_grad = bell_draw(streams_of[0], (TOKENS, D), 1.0, 6.0, ((0, 16), (1, 16)))
    gate_act = bell_draw(streams_of[1], (TOKENS, FF), 2.0, 8.0, ((0, 16), (1, 16)))
    up_act = bell_draw(streams_of[2], (TOKENS, FF), 1.0, 6.0, ((0, 16), (1, 16)))
    w_down = bell_draw(streams_of[3], (D, FF), D ** -0.5, 0.09375, ((0, 16), (1, 16)))
    return dict(out_grad=out_grad, gate_act=gate_act, up_act=up_act, w_down=w_down)


def reference(out_grad, gate_act, up_act, w_down):
    grad_blocks = out_grad.reshape(N_DP, SEQ, D)
    gate_blocks = gate_act.reshape(N_DP, SEQ, FF)
    up_blocks = up_act.reshape(N_DP, SEQ, FF)

    def one_batch(running, inputs):
        grad_rows, gate_rows, up_rows = inputs
        gate_wide = gate_rows.astype(jnp.float32)
        up_wide = up_rows.astype(jnp.float32)
        sigmoid_gate = jax.nn.sigmoid(gate_wide)
        activated = gate_wide * sigmoid_gate
        hidden = (activated * up_wide).astype(jnp.bfloat16)
        hidden_grad = jnp.dot(grad_rows, w_down, preferred_element_type=jnp.float32)
        gate_out = (hidden_grad * up_wide * sigmoid_gate * (1.0 + gate_wide * (1.0 - sigmoid_gate))).astype(jnp.bfloat16)
        up_out = (hidden_grad * activated).astype(jnp.bfloat16)
        running = running + lax.dot_general(grad_rows, hidden, (((0,), (0,)), ((), ())), preferred_element_type=jnp.float32)
        return (running, (gate_out, up_out))
    start_sum = jnp.zeros((D, FF), jnp.float32)
    summed, outputs = lax.scan(one_batch, start_sum, (grad_blocks, gate_blocks, up_blocks))
    gate_grad = outputs[0].reshape(TOKENS, FF)
    up_grad = outputs[1].reshape(TOKENS, FF)
    down_grad = (summed * (1.0 / math.sqrt(TOKENS))).astype(jnp.bfloat16)
    return (gate_grad, up_grad, down_grad)
```

```python
import math

import jax
import jax.numpy as jnp
import numpy as np
from jax import lax
from jax.sharding import Mesh
from jax.sharding import PartitionSpec as P


def body(out_grad, gate_act, up_act, w_down):
    seq_rows = gate_act.shape[0]
    n_chip = lax.axis_size("chip")
    n_core = lax.axis_size("core")
    width = w_down.shape[0]
    grad_scale = 1.0 / math.sqrt(seq_rows * n_chip * n_core)
    gate_wide = gate_act.astype(jnp.float32)
    up_wide = up_act.astype(jnp.float32)
    sigmoid_gate = jax.nn.sigmoid(gate_wide)
    activated = gate_wide * sigmoid_gate
    hidden = (activated * up_wide).astype(jnp.bfloat16)

    rows_all = lax.all_gather(out_grad, "tensor", axis=1, tiled=True)
    rows4 = rows_all.reshape(seq_rows, n_chip, n_core, width)
    w_chips = lax.all_gather(w_down, "chip", axis=0, tiled=False)
    w_full = lax.all_gather(w_chips, "core", axis=0, tiled=False)
    hidden_grad = jnp.einsum(
        "trck,crkf->tf", rows4, w_full, preferred_element_type=jnp.float32
    )

    rows_pair = lax.all_to_all(rows4, "core", 2, 0, tiled=True)
    hidden_pair = lax.all_gather(hidden, "core", axis=0, tiled=True)
    partial = jnp.einsum(
        "trk,tf->rkf",
        rows_pair.reshape(n_core * seq_rows, n_chip, width),
        hidden_pair,
        preferred_element_type=jnp.float32,
    )
    summed = lax.psum_scatter(partial, "chip", scatter_dimension=0, tiled=False)

    gate_grad = (
        hidden_grad * up_wide * sigmoid_gate * (1.0 + gate_wide * (1.0 - sigmoid_gate))
    ).astype(jnp.bfloat16)
    up_grad = (hidden_grad * activated).astype(jnp.bfloat16)
    down_grad = (summed * grad_scale).astype(jnp.bfloat16)
    return (gate_grad, up_grad, down_grad)


def solution(mesh):
    n_dp = mesh.shape["dp"]
    n_tensor = mesh.shape["tensor"]
    devices = np.asarray(mesh.devices).reshape(n_dp // 2, 2, n_tensor)
    split = Mesh(devices, ("chip", "core", "tensor"))
    placed = P(("chip", "core"), "tensor")
    return jax.shard_map(
        body,
        mesh=split,
        in_specs=(placed, placed, placed, placed),
        out_specs=(placed, placed, placed),
        check_vma=False,
    )
```

```python
import math

import jax
import jax.numpy as jnp
import numpy as np
from jax import lax
from jax.experimental import pallas as pl
from jax.experimental.pallas import tpu as pltpu
from jax.sharding import Mesh
from jax.sharding import PartitionSpec as P

MESH = pl.DeviceIdType.MESH
ANY = pl.BlockSpec(memory_space=pl.ANY)


def _where():
    return lax.axis_index("chip"), lax.axis_index("core"), lax.axis_index("tensor")


def _gather_kernel(n_chip, n_core, n_ten, og_ref, w_ref, rows_out, w_out,
                   r_send, r_recv, w_send, w_recv, own_sem):
    chip, core, ten = _where()
    barrier = pltpu.get_barrier_semaphore()
    for k in range(1, n_ten):
        pl.semaphore_signal(barrier, inc=1, device_id=(chip, core, (ten + k) % n_ten),
                            device_id_type=MESH)
    for k in range(1, n_chip):
        pl.semaphore_signal(barrier, inc=1, device_id=((chip + k) % n_chip, core, ten),
                            device_id_type=MESH)
    pl.semaphore_wait(barrier, (n_ten - 1) + (n_chip - 1))

    rows_slot = rows_out.at[ten % n_core, ten // n_core]
    own_r = pltpu.make_async_copy(og_ref, rows_slot, own_sem.at[0])
    own_w = pltpu.make_async_copy(w_ref, w_out.at[chip], own_sem.at[1])
    own_r.start()
    own_w.start()
    copies = []
    for k in range(1, n_ten):
        cp = pltpu.make_async_remote_copy(
            og_ref, rows_slot, r_send.at[k], r_recv.at[k],
            device_id=(chip, core, (ten + k) % n_ten), device_id_type=MESH)
        cp.start()
        copies.append(cp)
    for k in range(1, n_chip):
        cp = pltpu.make_async_remote_copy(
            w_ref, w_out.at[chip], w_send.at[k], w_recv.at[k],
            device_id=((chip + k) % n_chip, core, ten), device_id_type=MESH)
        cp.start()
        copies.append(cp)
    own_r.wait()
    own_w.wait()
    for cp in copies:
        cp.wait_send()
        cp.wait_recv()


def _pair_kernel(n_core, w_ref, rows_ref, hid_ref, w_other, rows_other, hid_other,
                 send, recv):
    chip, core, ten = _where()
    other = (chip, 1 - core, ten)
    barrier = pltpu.get_barrier_semaphore()
    pl.semaphore_signal(barrier, inc=1, device_id=other, device_id_type=MESH)
    pl.semaphore_wait(barrier, 1)
    copies = [
        pltpu.make_async_remote_copy(w_ref, w_other, send.at[0], recv.at[0],
                                     device_id=other, device_id_type=MESH),
        pltpu.make_async_remote_copy(rows_ref.at[1 - core], rows_other, send.at[1],
                                     recv.at[1], device_id=other, device_id_type=MESH),
        pltpu.make_async_remote_copy(hid_ref, hid_other, send.at[2], recv.at[2],
                                     device_id=other, device_id_type=MESH),
    ]
    for cp in copies:
        cp.start()
    for cp in copies:
        cp.wait_send()
        cp.wait_recv()


def _scatter_kernel(n_chip, part_ref, recv_out, send, recv, own_sem):
    chip, core, ten = _where()
    barrier = pltpu.get_barrier_semaphore()
    for k in range(1, n_chip):
        pl.semaphore_signal(barrier, inc=1, device_id=((chip + k) % n_chip, core, ten),
                            device_id_type=MESH)
    pl.semaphore_wait(barrier, n_chip - 1)
    own = pltpu.make_async_copy(part_ref.at[chip], recv_out.at[chip], own_sem.at[0])
    own.start()
    copies = []
    for k in range(1, n_chip):
        dest = (chip + k) % n_chip
        cp = pltpu.make_async_remote_copy(
            part_ref.at[dest], recv_out.at[chip], send.at[k], recv.at[k],
            device_id=(dest, core, ten), device_id_type=MESH)
        cp.start()
        copies.append(cp)
    own.wait()
    for cp in copies:
        cp.wait_send()
        cp.wait_recv()


def _params(cid):
    return pltpu.CompilerParams(collective_id=cid, has_side_effects=True)


def body(out_grad, gate_act, up_act, w_down):
    seq_rows, ff = gate_act.shape
    width = w_down.shape[0]
    n_chip = lax.axis_size("chip")
    n_core = lax.axis_size("core")
    n_ten = lax.axis_size("tensor")
    core = lax.axis_index("core")
    grad_scale = 1.0 / math.sqrt(seq_rows * n_chip * n_core)
    gate_wide = gate_act.astype(jnp.float32)
    up_wide = up_act.astype(jnp.float32)
    sigmoid_gate = jax.nn.sigmoid(gate_wide)
    activated = gate_wide * sigmoid_gate
    hidden = (activated * up_wide).astype(jnp.bfloat16)

    rows_g, w_own = pl.pallas_call(
        lambda *refs: _gather_kernel(n_chip, n_core, n_ten, *refs),
        out_shape=(
            jax.ShapeDtypeStruct((n_core, n_chip, seq_rows, out_grad.shape[1]), out_grad.dtype),
            jax.ShapeDtypeStruct((n_chip, width, ff), w_down.dtype),
        ),
        in_specs=[ANY, ANY],
        out_specs=(ANY, ANY),
        scratch_shapes=[pltpu.SemaphoreType.DMA((n_ten,)), pltpu.SemaphoreType.DMA((n_ten,)),
                        pltpu.SemaphoreType.DMA((n_chip,)), pltpu.SemaphoreType.DMA((n_chip,)),
                        pltpu.SemaphoreType.DMA((2,))],
        compiler_params=_params(0),
    )(out_grad, w_down)

    w_other, rows_other, hidden_other = pl.pallas_call(
        lambda *refs: _pair_kernel(n_core, *refs),
        out_shape=(
            jax.ShapeDtypeStruct(w_own.shape, w_own.dtype),
            jax.ShapeDtypeStruct(rows_g.shape[1:], rows_g.dtype),
            jax.ShapeDtypeStruct(hidden.shape, hidden.dtype),
        ),
        in_specs=[ANY, ANY, ANY],
        out_specs=(ANY, ANY, ANY),
        scratch_shapes=[pltpu.SemaphoreType.DMA((3,)), pltpu.SemaphoreType.DMA((3,))],
        compiler_params=_params(1),
    )(w_own, rows_g, hidden)

    rows_mine = lax.dynamic_index_in_dim(rows_g, core, 0, keepdims=False)
    rows_theirs = lax.dynamic_index_in_dim(rows_g, 1 - core, 0, keepdims=False)
    hidden_grad = jnp.einsum(
        "rtk,rkf->tf", rows_mine, w_own, preferred_element_type=jnp.float32
    ) + jnp.einsum("rtk,rkf->tf", rows_theirs, w_other, preferred_element_type=jnp.float32)

    partial = jnp.einsum(
        "rtk,tf->rkf", rows_mine, hidden, preferred_element_type=jnp.float32
    ) + jnp.einsum("rtk,tf->rkf", rows_other, hidden_other, preferred_element_type=jnp.float32)

    received = pl.pallas_call(
        lambda *refs: _scatter_kernel(n_chip, *refs),
        out_shape=jax.ShapeDtypeStruct(partial.shape, partial.dtype),
        in_specs=[ANY],
        out_specs=ANY,
        scratch_shapes=[pltpu.SemaphoreType.DMA((n_chip,)), pltpu.SemaphoreType.DMA((n_chip,)),
                        pltpu.SemaphoreType.DMA((1,))],
        compiler_params=_params(2),
    )(partial)
    summed = jnp.sum(received, axis=0)

    gate_grad = (
        hidden_grad * up_wide * sigmoid_gate * (1.0 + gate_wide * (1.0 - sigmoid_gate))
    ).astype(jnp.bfloat16)
    up_grad = (hidden_grad * activated).astype(jnp.bfloat16)
    down_grad = (summed * grad_scale).astype(jnp.bfloat16)
    return (gate_grad, up_grad, down_grad)


def solution(mesh):
    n_dp = mesh.shape["dp"]
    n_tensor = mesh.shape["tensor"]
    devices = np.asarray(mesh.devices).reshape(n_dp // 2, 2, n_tensor)
    split = Mesh(devices, ("chip", "core", "tensor"))
    placed = P(("chip", "core"), "tensor")
    return jax.shard_map(
        body,
        mesh=split,
        in_specs=(placed, placed, placed, placed),
        out_specs=(placed, placed, placed),
        check_vma=False,
    )
```

```python
import math

import jax
import jax.numpy as jnp
import numpy as np
from jax import lax
from jax.experimental import pallas as pl
from jax.experimental.pallas import tpu as pltpu
from jax.sharding import Mesh
from jax.sharding import PartitionSpec as P

MESH = pl.DeviceIdType.MESH
ANY = pl.BlockSpec(memory_space=pl.ANY)


def _where():
    return lax.axis_index("chip"), lax.axis_index("core"), lax.axis_index("tensor")


def _gather_kernel(n_chip, n_lo, og_ref, w_ref, rows_out, w_out,
                   x_send, x_recv, r_send, r_recv, l_send, l_recv, w_send, w_recv, own_sem):
    chip, core, ten = _where()
    n_plane = rows_out.shape[0]
    plane, lo = ten // n_lo, ten % n_lo
    right = ((plane + 1) % n_plane) * n_lo + lo
    left = ((plane + n_plane - 1) % n_plane) * n_lo + lo
    side = plane * n_lo + (1 - lo)
    barrier = pltpu.get_barrier_semaphore()
    for t in (right, left, side):
        pl.semaphore_signal(barrier, inc=1, device_id=(chip, core, t), device_id_type=MESH)
    for k in range(1, n_chip):
        pl.semaphore_signal(barrier, inc=1, device_id=((chip + k) % n_chip, core, ten),
                            device_id_type=MESH)
    pl.semaphore_wait(barrier, 3 + (n_chip - 1))

    own_r = pltpu.make_async_copy(og_ref, rows_out.at[plane, lo], own_sem.at[0])
    own_w = pltpu.make_async_copy(w_ref, w_out.at[chip], own_sem.at[1])
    own_r.start()
    own_w.start()
    w_copies = []
    for k in range(1, n_chip):
        cp = pltpu.make_async_remote_copy(
            w_ref, w_out.at[chip], w_send.at[k], w_recv.at[k],
            device_id=((chip + k) % n_chip, core, ten), device_id_type=MESH)
        cp.start()
        w_copies.append(cp)
    side_cp = pltpu.make_async_remote_copy(
        og_ref, rows_out.at[plane, lo], x_send.at[0], x_recv.at[0],
        device_id=(chip, core, side), device_id_type=MESH)
    side_cp.start()
    own_r.wait()
    side_cp.wait_send()
    side_cp.wait_recv()

    n_right = n_plane // 2
    n_left = n_plane - 1 - n_right
    ring = []
    for s in range(max(n_right, n_left)):
        if s < n_right:
            src_plane = (plane + n_plane - s) % n_plane
            cp = pltpu.make_async_remote_copy(
                rows_out.at[src_plane], rows_out.at[src_plane], r_send.at[s], r_recv.at[s],
                device_id=(chip, core, right), device_id_type=MESH)
            ring.append(("r", s, cp))
        if s < n_left:
            src_plane = (plane + s) % n_plane
            cp = pltpu.make_async_remote_copy(
                rows_out.at[src_plane], rows_out.at[src_plane], l_send.at[s], l_recv.at[s],
                device_id=(chip, core, left), device_id_type=MESH)
            ring.append(("l", s, cp))
    by = {(d, s): cp for d, s, cp in ring}
    for s in range(max(n_right, n_left)):
        for d, n in (("r", n_right), ("l", n_left)):
            if s < n:
                if s > 0:
                    by[(d, s - 1)].wait_recv()
                by[(d, s)].start()
    for d, n in (("r", n_right), ("l", n_left)):
        if n > 0:
            by[(d, n - 1)].wait_recv()
        for s in range(n):
            by[(d, s)].wait_send()
    own_w.wait()
    for cp in w_copies:
        cp.wait_send()
        cp.wait_recv()


def _pair_kernel(w_ref, rows_ref, hid_ref, w_other, rows_other, hid_other,
                 send, recv, r_send, r_recv):
    chip, core, ten = _where()
    other = (chip, 1 - core, ten)
    barrier = pltpu.get_barrier_semaphore()
    pl.semaphore_signal(barrier, inc=1, device_id=other, device_id_type=MESH)
    pl.semaphore_wait(barrier, 1)
    copies = [
        pltpu.make_async_remote_copy(w_ref, w_other, send.at[0], recv.at[0],
                                     device_id=other, device_id_type=MESH),
        pltpu.make_async_remote_copy(hid_ref, hid_other, send.at[1], recv.at[1],
                                     device_id=other, device_id_type=MESH),
    ]
    for r in range(rows_ref.shape[0]):
        copies.append(pltpu.make_async_remote_copy(
            rows_ref.at[r, 1 - core], rows_other.at[r], r_send.at[r], r_recv.at[r],
            device_id=other, device_id_type=MESH))
    for cp in copies:
        cp.start()
    for cp in copies:
        cp.wait_send()
        cp.wait_recv()


def _scatter_kernel(n_chip, part_ref, recv_out, send, recv, own_sem):
    chip, core, ten = _where()
    barrier = pltpu.get_barrier_semaphore()
    for k in range(1, n_chip):
        pl.semaphore_signal(barrier, inc=1, device_id=((chip + k) % n_chip, core, ten),
                            device_id_type=MESH)
    pl.semaphore_wait(barrier, n_chip - 1)
    own = pltpu.make_async_copy(part_ref.at[chip], recv_out.at[chip], own_sem.at[0])
    own.start()
    copies = []
    for k in range(1, n_chip):
        dest = (chip + k) % n_chip
        cp = pltpu.make_async_remote_copy(
            part_ref.at[dest], recv_out.at[chip], send.at[k], recv.at[k],
            device_id=(dest, core, ten), device_id_type=MESH)
        cp.start()
        copies.append(cp)
    own.wait()
    for cp in copies:
        cp.wait_send()
        cp.wait_recv()


def _params(cid):
    return pltpu.CompilerParams(collective_id=cid, has_side_effects=True)


def body(out_grad, gate_act, up_act, w_down):
    seq_rows, ff = gate_act.shape
    width = w_down.shape[0]
    n_chip = lax.axis_size("chip")
    n_core = lax.axis_size("core")
    n_ten = lax.axis_size("tensor")
    core = lax.axis_index("core")
    grad_scale = 1.0 / math.sqrt(seq_rows * n_chip * n_core)
    gate_wide = gate_act.astype(jnp.float32)
    up_wide = up_act.astype(jnp.float32)
    sigmoid_gate = jax.nn.sigmoid(gate_wide)
    activated = gate_wide * sigmoid_gate
    hidden = (activated * up_wide).astype(jnp.bfloat16)

    n_lo = n_core
    n_plane = n_ten // n_lo
    rows_g, w_own = pl.pallas_call(
        lambda *refs: _gather_kernel(n_chip, n_lo, *refs),
        out_shape=(
            jax.ShapeDtypeStruct((n_plane, n_lo, seq_rows, out_grad.shape[1]), out_grad.dtype),
            jax.ShapeDtypeStruct((n_chip, width, ff), w_down.dtype),
        ),
        in_specs=[ANY, ANY],
        out_specs=(ANY, ANY),
        scratch_shapes=[pltpu.SemaphoreType.DMA((1,)), pltpu.SemaphoreType.DMA((1,)),
                        pltpu.SemaphoreType.DMA((n_plane,)), pltpu.SemaphoreType.DMA((n_plane,)),
                        pltpu.SemaphoreType.DMA((n_plane,)), pltpu.SemaphoreType.DMA((n_plane,)),
                        pltpu.SemaphoreType.DMA((n_chip,)), pltpu.SemaphoreType.DMA((n_chip,)),
                        pltpu.SemaphoreType.DMA((2,))],
        compiler_params=_params(0),
    )(out_grad, w_down)

    w_other, rows_other, hidden_other = pl.pallas_call(
        _pair_kernel,
        out_shape=(
            jax.ShapeDtypeStruct(w_own.shape, w_own.dtype),
            jax.ShapeDtypeStruct((n_plane,) + rows_g.shape[2:], rows_g.dtype),
            jax.ShapeDtypeStruct(hidden.shape, hidden.dtype),
        ),
        in_specs=[ANY, ANY, ANY],
        out_specs=(ANY, ANY, ANY),
        scratch_shapes=[pltpu.SemaphoreType.DMA((2,)), pltpu.SemaphoreType.DMA((2,)),
                        pltpu.SemaphoreType.DMA((n_plane,)), pltpu.SemaphoreType.DMA((n_plane,))],
        compiler_params=_params(1),
    )(w_own, rows_g, hidden)

    rows_mine = lax.dynamic_index_in_dim(rows_g, core, 1, keepdims=False)
    rows_theirs = lax.dynamic_index_in_dim(rows_g, 1 - core, 1, keepdims=False)
    hidden_grad = jnp.einsum(
        "rtk,rkf->tf", rows_mine, w_own, preferred_element_type=jnp.float32
    ) + jnp.einsum("rtk,rkf->tf", rows_theirs, w_other, preferred_element_type=jnp.float32)

    partial = jnp.einsum(
        "rtk,tf->rkf", rows_mine, hidden, preferred_element_type=jnp.float32
    ) + jnp.einsum("rtk,tf->rkf", rows_other, hidden_other, preferred_element_type=jnp.float32)

    received = pl.pallas_call(
        lambda *refs: _scatter_kernel(n_chip, *refs),
        out_shape=jax.ShapeDtypeStruct(partial.shape, jnp.bfloat16),
        in_specs=[ANY],
        out_specs=ANY,
        scratch_shapes=[pltpu.SemaphoreType.DMA((n_chip,)), pltpu.SemaphoreType.DMA((n_chip,)),
                        pltpu.SemaphoreType.DMA((1,))],
        compiler_params=_params(2),
    )(partial.astype(jnp.bfloat16))
    summed = jnp.sum(received.astype(jnp.float32), axis=0)

    gate_grad = (
        hidden_grad * up_wide * sigmoid_gate * (1.0 + gate_wide * (1.0 - sigmoid_gate))
    ).astype(jnp.bfloat16)
    up_grad = (hidden_grad * activated).astype(jnp.bfloat16)
    down_grad = (summed * grad_scale).astype(jnp.bfloat16)
    return (gate_grad, up_grad, down_grad)


def solution(mesh):
    n_dp = mesh.shape["dp"]
    n_tensor = mesh.shape["tensor"]
    devices = np.asarray(mesh.devices).reshape(n_dp // 2, 2, n_tensor)
    split = Mesh(devices, ("chip", "core", "tensor"))
    placed = P(("chip", "core"), "tensor")
    return jax.shard_map(
        body,
        mesh=split,
        in_specs=(placed, placed, placed, placed),
        out_specs=(placed, placed, placed),
        check_vma=False,
    )
```

```python
import math

import jax
import jax.numpy as jnp
import numpy as np
from jax import lax
from jax.experimental import pallas as pl
from jax.experimental.pallas import tpu as pltpu
from jax.sharding import Mesh
from jax.sharding import PartitionSpec as P

MESH = pl.DeviceIdType.MESH
ANY = pl.BlockSpec(memory_space=pl.ANY)


def _where():
    return lax.axis_index("chip"), lax.axis_index("core"), lax.axis_index("tensor")


def _w_kernel(n_chip, w_ref, w_out, w_send, w_recv, own_sem):
    chip, core, ten = _where()
    barrier = pltpu.get_barrier_semaphore()
    for k in range(1, n_chip):
        pl.semaphore_signal(barrier, inc=1, device_id=((chip + k) % n_chip, core, ten),
                            device_id_type=MESH)
    pl.semaphore_wait(barrier, n_chip - 1)
    own_w = pltpu.make_async_copy(w_ref, w_out.at[chip], own_sem.at[0])
    own_w.start()
    w_copies = []
    for k in range(1, n_chip):
        cp = pltpu.make_async_remote_copy(
            w_ref, w_out.at[chip], w_send.at[k], w_recv.at[k],
            device_id=((chip + k) % n_chip, core, ten), device_id_type=MESH)
        cp.start()
        w_copies.append(cp)
    own_w.wait()
    for cp in w_copies:
        cp.wait_send()
        cp.wait_recv()


def _rows_kernel(n_lo, og_ref, rows_out, x_send, x_recv, r_send, r_recv, l_send, l_recv,
                 own_sem):
    chip, core, ten = _where()
    n_plane = rows_out.shape[0]
    plane, lo = ten // n_lo, ten % n_lo
    right = ((plane + 1) % n_plane) * n_lo + lo
    left = ((plane + n_plane - 1) % n_plane) * n_lo + lo
    side = plane * n_lo + (1 - lo)
    barrier = pltpu.get_barrier_semaphore()
    for t in (right, left, side):
        pl.semaphore_signal(barrier, inc=1, device_id=(chip, core, t), device_id_type=MESH)
    pl.semaphore_wait(barrier, 3)

    own_r = pltpu.make_async_copy(og_ref, rows_out.at[plane, lo], own_sem.at[0])
    own_r.start()
    side_cp = pltpu.make_async_remote_copy(
        og_ref, rows_out.at[plane, lo], x_send.at[0], x_recv.at[0],
        device_id=(chip, core, side), device_id_type=MESH)
    side_cp.start()
    own_r.wait()
    side_cp.wait_send()
    side_cp.wait_recv()

    n_right = n_plane // 2
    n_left = n_plane - 1 - n_right
    ring = []
    for s in range(max(n_right, n_left)):
        if s < n_right:
            src_plane = (plane + n_plane - s) % n_plane
            cp = pltpu.make_async_remote_copy(
                rows_out.at[src_plane], rows_out.at[src_plane], r_send.at[s], r_recv.at[s],
                device_id=(chip, core, right), device_id_type=MESH)
            ring.append(("r", s, cp))
        if s < n_left:
            src_plane = (plane + s) % n_plane
            cp = pltpu.make_async_remote_copy(
                rows_out.at[src_plane], rows_out.at[src_plane], l_send.at[s], l_recv.at[s],
                device_id=(chip, core, left), device_id_type=MESH)
            ring.append(("l", s, cp))
    by = {(d, s): cp for d, s, cp in ring}
    for s in range(max(n_right, n_left)):
        for d, n in (("r", n_right), ("l", n_left)):
            if s < n:
                if s > 0:
                    by[(d, s - 1)].wait_recv()
                by[(d, s)].start()
    for d, n in (("r", n_right), ("l", n_left)):
        if n > 0:
            by[(d, n - 1)].wait_recv()
        for s in range(n):
            by[(d, s)].wait_send()


def _pair_kernel(w_ref, rows_ref, hid_ref, w_other, rows_other, hid_other,
                 send, recv, r_send, r_recv):
    chip, core, ten = _where()
    other = (chip, 1 - core, ten)
    barrier = pltpu.get_barrier_semaphore()
    pl.semaphore_signal(barrier, inc=1, device_id=other, device_id_type=MESH)
    pl.semaphore_wait(barrier, 1)
    copies = [
        pltpu.make_async_remote_copy(w_ref, w_other, send.at[0], recv.at[0],
                                     device_id=other, device_id_type=MESH),
        pltpu.make_async_remote_copy(hid_ref, hid_other, send.at[1], recv.at[1],
                                     device_id=other, device_id_type=MESH),
    ]
    for r in range(rows_ref.shape[0]):
        copies.append(pltpu.make_async_remote_copy(
            rows_ref.at[r, 1 - core], rows_other.at[r], r_send.at[r], r_recv.at[r],
            device_id=other, device_id_type=MESH))
    for cp in copies:
        cp.start()
    for cp in copies:
        cp.wait_send()
        cp.wait_recv()


def _scatter_kernel(n_chip, part_ref, recv_out, send, recv, own_sem):
    chip, core, ten = _where()
    barrier = pltpu.get_barrier_semaphore()
    for k in range(1, n_chip):
        pl.semaphore_signal(barrier, inc=1, device_id=((chip + k) % n_chip, core, ten),
                            device_id_type=MESH)
    pl.semaphore_wait(barrier, n_chip - 1)
    own = pltpu.make_async_copy(part_ref.at[chip], recv_out.at[chip], own_sem.at[0])
    own.start()
    copies = []
    for k in range(1, n_chip):
        dest = (chip + k) % n_chip
        cp = pltpu.make_async_remote_copy(
            part_ref.at[dest], recv_out.at[chip], send.at[k], recv.at[k],
            device_id=(dest, core, ten), device_id_type=MESH)
        cp.start()
        copies.append(cp)
    own.wait()
    for cp in copies:
        cp.wait_send()
        cp.wait_recv()


def _params(cid):
    return pltpu.CompilerParams(collective_id=cid, has_side_effects=True)


def body(out_grad, gate_act, up_act, w_down):
    seq_rows, ff = gate_act.shape
    width = w_down.shape[0]
    n_chip = lax.axis_size("chip")
    n_core = lax.axis_size("core")
    n_ten = lax.axis_size("tensor")
    core = lax.axis_index("core")
    grad_scale = 1.0 / math.sqrt(seq_rows * n_chip * n_core)
    gate_wide = gate_act.astype(jnp.float32)
    up_wide = up_act.astype(jnp.float32)
    sigmoid_gate = jax.nn.sigmoid(gate_wide)
    activated = gate_wide * sigmoid_gate
    hidden = (activated * up_wide).astype(jnp.bfloat16)

    n_lo = n_core
    n_plane = n_ten // n_lo
    rows_g = pl.pallas_call(
        lambda *refs: _rows_kernel(n_lo, *refs),
        out_shape=jax.ShapeDtypeStruct(
            (n_plane, n_lo, seq_rows, out_grad.shape[1]), out_grad.dtype),
        in_specs=[ANY],
        out_specs=ANY,
        scratch_shapes=[pltpu.SemaphoreType.DMA((1,)), pltpu.SemaphoreType.DMA((1,)),
                        pltpu.SemaphoreType.DMA((n_plane,)), pltpu.SemaphoreType.DMA((n_plane,)),
                        pltpu.SemaphoreType.DMA((n_plane,)), pltpu.SemaphoreType.DMA((n_plane,)),
                        pltpu.SemaphoreType.DMA((1,))],
        compiler_params=_params(0),
    )(out_grad)
    w_own = pl.pallas_call(
        lambda *refs: _w_kernel(n_chip, *refs),
        out_shape=jax.ShapeDtypeStruct((n_chip, width, ff), w_down.dtype),
        in_specs=[ANY],
        out_specs=ANY,
        scratch_shapes=[pltpu.SemaphoreType.DMA((n_chip,)), pltpu.SemaphoreType.DMA((n_chip,)),
                        pltpu.SemaphoreType.DMA((1,))],
        compiler_params=_params(3),
    )(w_down)

    w_other, rows_other, hidden_other = pl.pallas_call(
        _pair_kernel,
        out_shape=(
            jax.ShapeDtypeStruct(w_own.shape, w_own.dtype),
            jax.ShapeDtypeStruct((n_plane,) + rows_g.shape[2:], rows_g.dtype),
            jax.ShapeDtypeStruct(hidden.shape, hidden.dtype),
        ),
        in_specs=[ANY, ANY, ANY],
        out_specs=(ANY, ANY, ANY),
        scratch_shapes=[pltpu.SemaphoreType.DMA((2,)), pltpu.SemaphoreType.DMA((2,)),
                        pltpu.SemaphoreType.DMA((n_plane,)), pltpu.SemaphoreType.DMA((n_plane,))],
        compiler_params=_params(1),
    )(w_own, rows_g, hidden)

    rows_mine = lax.dynamic_index_in_dim(rows_g, core, 1, keepdims=False)
    rows_theirs = lax.dynamic_index_in_dim(rows_g, 1 - core, 1, keepdims=False)
    hidden_grad = jnp.einsum(
        "rtk,rkf->tf", rows_mine, w_own, preferred_element_type=jnp.float32
    ) + jnp.einsum("rtk,rkf->tf", rows_theirs, w_other, preferred_element_type=jnp.float32)

    partial = jnp.einsum(
        "rtk,tf->rkf", rows_mine, hidden, preferred_element_type=jnp.float32
    ) + jnp.einsum("rtk,tf->rkf", rows_other, hidden_other, preferred_element_type=jnp.float32)

    received = pl.pallas_call(
        lambda *refs: _scatter_kernel(n_chip, *refs),
        out_shape=jax.ShapeDtypeStruct(partial.shape, jnp.bfloat16),
        in_specs=[ANY],
        out_specs=ANY,
        scratch_shapes=[pltpu.SemaphoreType.DMA((n_chip,)), pltpu.SemaphoreType.DMA((n_chip,)),
                        pltpu.SemaphoreType.DMA((1,))],
        compiler_params=_params(2),
    )(partial.astype(jnp.bfloat16))
    summed = jnp.sum(received.astype(jnp.float32), axis=0)

    gate_grad = (
        hidden_grad * up_wide * sigmoid_gate * (1.0 + gate_wide * (1.0 - sigmoid_gate))
    ).astype(jnp.bfloat16)
    up_grad = (hidden_grad * activated).astype(jnp.bfloat16)
    down_grad = (summed * grad_scale).astype(jnp.bfloat16)
    return (gate_grad, up_grad, down_grad)


def solution(mesh):
    n_dp = mesh.shape["dp"]
    n_tensor = mesh.shape["tensor"]
    devices = np.asarray(mesh.devices).reshape(n_dp // 2, 2, n_tensor)
    split = Mesh(devices, ("chip", "core", "tensor"))
    placed = P(("chip", "core"), "tensor")
    return jax.shard_map(
        body,
        mesh=split,
        in_specs=(placed, placed, placed, placed),
        out_specs=(placed, placed, placed),
        check_vma=False,
    )
```

```python
import math

import jax
import jax.numpy as jnp
import numpy as np
from jax import lax
from jax.experimental import pallas as pl
from jax.experimental.pallas import tpu as pltpu
from jax.sharding import Mesh
from jax.sharding import PartitionSpec as P

MESH = pl.DeviceIdType.MESH
ANY = pl.BlockSpec(memory_space=pl.ANY)


def _where():
    return lax.axis_index("chip"), lax.axis_index("core"), lax.axis_index("tensor")


def _gather_kernel(n_chip, n_lo, og_ref, w_ref, rows_out, w_out, x_send, x_recv,
                   r_send, r_recv, l_send, l_recv, w_send, w_recv, own_sem):
    chip, core, ten = _where()
    n_plane = rows_out.shape[0]
    plane, lo = ten // n_lo, ten % n_lo
    right = ((plane + 1) % n_plane) * n_lo + lo
    left = ((plane + n_plane - 1) % n_plane) * n_lo + lo
    side = plane * n_lo + (1 - lo)
    barrier = pltpu.get_barrier_semaphore()
    for t in (right, left, side):
        pl.semaphore_signal(barrier, inc=1, device_id=(chip, core, t), device_id_type=MESH)
    for k in range(1, n_chip):
        pl.semaphore_signal(barrier, inc=1, device_id=((chip + k) % n_chip, core, ten),
                            device_id_type=MESH)
    pl.semaphore_wait(barrier, 3 + (n_chip - 1))

    side_cp = pltpu.make_async_remote_copy(
        og_ref, rows_out.at[plane, lo], x_send.at[0], x_recv.at[0],
        device_id=(chip, core, side), device_id_type=MESH)
    side_cp.start()
    own_r = pltpu.make_async_copy(og_ref, rows_out.at[plane, lo], own_sem.at[0])
    own_w = pltpu.make_async_copy(w_ref, w_out.at[chip], own_sem.at[1])
    own_r.start()
    own_w.start()
    own_r.wait()
    side_cp.wait_send()
    side_cp.wait_recv()

    n_steps = n_plane // 2
    ring = {}
    for s in range(n_steps):
        for d, sends, recvs, to, src_plane, half in (
            ("r", r_send, r_recv, right, (plane + n_plane - s) % n_plane, 0),
            ("l", l_send, l_recv, left, (plane + s) % n_plane, 1),
        ):
            block = rows_out.at[src_plane]
            if s == n_steps - 1:
                block = rows_out.at[src_plane, half]
            ring[(d, s)] = pltpu.make_async_remote_copy(
                block, block, sends.at[s], recvs.at[s],
                device_id=(chip, core, to), device_id_type=MESH)
    for d in ("r", "l"):
        ring[(d, 0)].start()
    w_copies = []
    for k in range(1, n_chip):
        cp = pltpu.make_async_remote_copy(
            w_ref, w_out.at[chip], w_send.at[k], w_recv.at[k],
            device_id=((chip + k) % n_chip, core, ten), device_id_type=MESH)
        cp.start()
        w_copies.append(cp)
    for s in range(1, n_steps):
        for d in ("r", "l"):
            ring[(d, s - 1)].wait_recv()
            ring[(d, s)].start()
    for d in ("r", "l"):
        ring[(d, n_steps - 1)].wait_recv()
        for s in range(n_steps):
            ring[(d, s)].wait_send()
    own_w.wait()
    for cp in w_copies:
        cp.wait_send()
        cp.wait_recv()


def _pair_kernel(w_ref, rows_ref, hid_ref, w_other, rows_other, hid_other,
                 send, recv, r_send, r_recv):
    chip, core, ten = _where()
    other = (chip, 1 - core, ten)
    barrier = pltpu.get_barrier_semaphore()
    pl.semaphore_signal(barrier, inc=1, device_id=other, device_id_type=MESH)
    pl.semaphore_wait(barrier, 1)
    copies = [
        pltpu.make_async_remote_copy(w_ref, w_other, send.at[0], recv.at[0],
                                     device_id=other, device_id_type=MESH),
        pltpu.make_async_remote_copy(hid_ref, hid_other, send.at[1], recv.at[1],
                                     device_id=other, device_id_type=MESH),
    ]
    for r in range(rows_ref.shape[0]):
        copies.append(pltpu.make_async_remote_copy(
            rows_ref.at[r, 1 - core], rows_other.at[r], r_send.at[r], r_recv.at[r],
            device_id=other, device_id_type=MESH))
    for cp in copies:
        cp.start()
    for cp in copies:
        cp.wait_send()
        cp.wait_recv()


def _scatter_kernel(n_chip, part_ref, recv_out, send, recv, own_sem):
    chip, core, ten = _where()
    barrier = pltpu.get_barrier_semaphore()
    for k in range(1, n_chip):
        pl.semaphore_signal(barrier, inc=1, device_id=((chip + k) % n_chip, core, ten),
                            device_id_type=MESH)
    pl.semaphore_wait(barrier, n_chip - 1)
    own = pltpu.make_async_copy(part_ref.at[chip], recv_out.at[chip], own_sem.at[0])
    own.start()
    copies = []
    for k in range(1, n_chip):
        dest = (chip + k) % n_chip
        cp = pltpu.make_async_remote_copy(
            part_ref.at[dest], recv_out.at[chip], send.at[k], recv.at[k],
            device_id=(dest, core, ten), device_id_type=MESH)
        cp.start()
        copies.append(cp)
    own.wait()
    for cp in copies:
        cp.wait_send()
        cp.wait_recv()


def _params(cid):
    return pltpu.CompilerParams(collective_id=cid, has_side_effects=True)


def body(out_grad, gate_act, up_act, w_down):
    seq_rows, ff = gate_act.shape
    width = w_down.shape[0]
    n_chip = lax.axis_size("chip")
    n_core = lax.axis_size("core")
    n_ten = lax.axis_size("tensor")
    core = lax.axis_index("core")
    grad_scale = 1.0 / math.sqrt(seq_rows * n_chip * n_core)
    gate_wide = gate_act.astype(jnp.float32)
    up_wide = up_act.astype(jnp.float32)
    sigmoid_gate = jax.nn.sigmoid(gate_wide)
    activated = gate_wide * sigmoid_gate
    hidden = (activated * up_wide).astype(jnp.bfloat16)

    n_lo = n_core
    n_plane = n_ten // n_lo
    rows_g, w_own = pl.pallas_call(
        lambda *refs: _gather_kernel(n_chip, n_lo, *refs),
        out_shape=(
            jax.ShapeDtypeStruct((n_plane, n_lo, seq_rows, out_grad.shape[1]), out_grad.dtype),
            jax.ShapeDtypeStruct((n_chip, width, ff), w_down.dtype),
        ),
        in_specs=[ANY, ANY],
        out_specs=(ANY, ANY),
        scratch_shapes=[pltpu.SemaphoreType.DMA((1,)), pltpu.SemaphoreType.DMA((1,)),
                        pltpu.SemaphoreType.DMA((n_plane // 2,)),
                        pltpu.SemaphoreType.DMA((n_plane // 2,)),
                        pltpu.SemaphoreType.DMA((n_plane // 2,)),
                        pltpu.SemaphoreType.DMA((n_plane // 2,)),
                        pltpu.SemaphoreType.DMA((n_chip,)), pltpu.SemaphoreType.DMA((n_chip,)),
                        pltpu.SemaphoreType.DMA((2,))],
        compiler_params=_params(0),
    )(out_grad, w_down)

    w_other, rows_other, hidden_other = pl.pallas_call(
        _pair_kernel,
        out_shape=(
            jax.ShapeDtypeStruct(w_own.shape, w_own.dtype),
            jax.ShapeDtypeStruct((n_plane,) + rows_g.shape[2:], rows_g.dtype),
            jax.ShapeDtypeStruct(hidden.shape, hidden.dtype),
        ),
        in_specs=[ANY, ANY, ANY],
        out_specs=(ANY, ANY, ANY),
        scratch_shapes=[pltpu.SemaphoreType.DMA((2,)), pltpu.SemaphoreType.DMA((2,)),
                        pltpu.SemaphoreType.DMA((n_plane,)), pltpu.SemaphoreType.DMA((n_plane,))],
        compiler_params=_params(1),
    )(w_own, rows_g, hidden)

    rows_mine = lax.dynamic_index_in_dim(rows_g, core, 1, keepdims=False)
    rows_theirs = lax.dynamic_index_in_dim(rows_g, 1 - core, 1, keepdims=False)
    hidden_grad = jnp.einsum(
        "rtk,rkf->tf", rows_mine, w_own, preferred_element_type=jnp.float32
    ) + jnp.einsum("rtk,rkf->tf", rows_theirs, w_other, preferred_element_type=jnp.float32)

    partial = jnp.einsum(
        "rtk,tf->rkf", rows_mine, hidden, preferred_element_type=jnp.float32
    ) + jnp.einsum("rtk,tf->rkf", rows_other, hidden_other, preferred_element_type=jnp.float32)

    received = pl.pallas_call(
        lambda *refs: _scatter_kernel(n_chip, *refs),
        out_shape=jax.ShapeDtypeStruct(partial.shape, jnp.bfloat16),
        in_specs=[ANY],
        out_specs=ANY,
        scratch_shapes=[pltpu.SemaphoreType.DMA((n_chip,)), pltpu.SemaphoreType.DMA((n_chip,)),
                        pltpu.SemaphoreType.DMA((1,))],
        compiler_params=_params(2),
    )(partial.astype(jnp.bfloat16))
    summed = jnp.sum(received.astype(jnp.float32), axis=0)

    gate_grad = (
        hidden_grad * up_wide * sigmoid_gate * (1.0 + gate_wide * (1.0 - sigmoid_gate))
    ).astype(jnp.bfloat16)
    up_grad = (hidden_grad * activated).astype(jnp.bfloat16)
    down_grad = (summed * grad_scale).astype(jnp.bfloat16)
    return (gate_grad, up_grad, down_grad)


def solution(mesh):
    n_dp = mesh.shape["dp"]
    n_tensor = mesh.shape["tensor"]
    devices = np.asarray(mesh.devices).reshape(n_dp // 2, 2, n_tensor)
    split = Mesh(devices, ("chip", "core", "tensor"))
    placed = P(("chip", "core"), "tensor")
    return jax.shard_map(
        body,
        mesh=split,
        in_specs=(placed, placed, placed, placed),
        out_specs=(placed, placed, placed),
        check_vma=False,
    )
```

```python
import math

import jax
import jax.numpy as jnp
import numpy as np
from jax import lax
from jax.experimental import pallas as pl
from jax.experimental.pallas import tpu as pltpu
from jax.sharding import Mesh
from jax.sharding import PartitionSpec as P

MESH = pl.DeviceIdType.MESH
ANY = pl.BlockSpec(memory_space=pl.ANY)


def _where():
    return lax.axis_index("chip"), lax.axis_index("core"), lax.axis_index("tensor")


def _gather_kernel(n_chip, n_lo, og_ref, w_ref, hid_ref, rows_out, w_out, rows_other,
                   w_other, hid_other, x_send, x_recv, r_send, r_recv, l_send, l_recv,
                   w_send, w_recv, f_send, f_recv, fw_send, fw_recv, fr_send, fr_recv, own_sem):
    chip, core, ten = _where()
    n_plane = rows_out.shape[0]
    plane, lo = ten // n_lo, ten % n_lo
    right = ((plane + 1) % n_plane) * n_lo + lo
    left = ((plane + n_plane - 1) % n_plane) * n_lo + lo
    side = plane * n_lo + (1 - lo)
    other = (chip, 1 - core, ten)
    barrier = pltpu.get_barrier_semaphore()
    for t in (right, left, side):
        pl.semaphore_signal(barrier, inc=1, device_id=(chip, core, t), device_id_type=MESH)
    for k in range(1, n_chip):
        pl.semaphore_signal(barrier, inc=1, device_id=((chip + k) % n_chip, core, ten),
                            device_id_type=MESH)
    pl.semaphore_signal(barrier, inc=1, device_id=other, device_id_type=MESH)
    pl.semaphore_wait(barrier, 3 + (n_chip - 1) + 1)

    side_cp = pltpu.make_async_remote_copy(
        og_ref, rows_out.at[plane, lo], x_send.at[0], x_recv.at[0],
        device_id=(chip, core, side), device_id_type=MESH)
    side_cp.start()
    own_r = pltpu.make_async_copy(og_ref, rows_out.at[plane, lo], own_sem.at[0])
    own_w = pltpu.make_async_copy(w_ref, w_out.at[chip], own_sem.at[1])
    own_r.start()
    own_w.start()
    hid_cp = pltpu.make_async_remote_copy(hid_ref, hid_other, f_send.at[0], f_recv.at[0],
                                          device_id=other, device_id_type=MESH)
    hid_cp.start()
    forwards = [hid_cp]

    def fwd_w(k):
        r = (chip + n_chip - k) % n_chip
        src = w_ref if k == 0 else w_out.at[r]
        cp = pltpu.make_async_remote_copy(src, w_other.at[r], fw_send.at[k], fw_recv.at[k],
                                          device_id=other, device_id_type=MESH)
        cp.start()
        forwards.append(cp)

    def fwd_rows(d):
        p = (plane + d) % n_plane
        cp = pltpu.make_async_remote_copy(rows_out.at[p, 1 - core], rows_other.at[p],
                                          fr_send.at[d], fr_recv.at[d],
                                          device_id=other, device_id_type=MESH)
        cp.start()
        forwards.append(cp)

    fwd_w(0)
    own_r.wait()
    side_cp.wait_send()
    side_cp.wait_recv()
    fwd_rows(0)

    n_steps = n_plane // 2
    ring = {}
    for s in range(n_steps):
        for d, sends, recvs, to, src_plane, half in (
            ("r", r_send, r_recv, right, (plane + n_plane - s) % n_plane, 0),
            ("l", l_send, l_recv, left, (plane + s) % n_plane, 1),
        ):
            block = rows_out.at[src_plane]
            if s == n_steps - 1:
                block = rows_out.at[src_plane, half]
            ring[(d, s)] = pltpu.make_async_remote_copy(
                block, block, sends.at[s], recvs.at[s],
                device_id=(chip, core, to), device_id_type=MESH)
    for d in ("r", "l"):
        ring[(d, 0)].start()
    w_copies = []
    for k in range(1, n_chip):
        cp = pltpu.make_async_remote_copy(
            w_ref, w_out.at[chip], w_send.at[k], w_recv.at[k],
            device_id=((chip + k) % n_chip, core, ten), device_id_type=MESH)
        cp.start()
        w_copies.append(cp)
    for s in range(1, n_steps):
        for d in ("r", "l"):
            ring[(d, s - 1)].wait_recv()
            ring[(d, s)].start()
        fwd_rows(n_plane - s)
        fwd_rows(s)
    for d in ("r", "l"):
        ring[(d, n_steps - 1)].wait_recv()
        for s in range(n_steps):
            ring[(d, s)].wait_send()
    fwd_rows(n_steps)
    for k in range(1, n_chip):
        w_copies[k - 1].wait_recv()
        fwd_w(k)
    own_w.wait()
    for cp in w_copies:
        cp.wait_send()
    for cp in forwards:
        cp.wait_send()
        cp.wait_recv()


def _scatter_kernel(n_chip, part_ref, recv_out, send, recv, own_sem):
    chip, core, ten = _where()
    barrier = pltpu.get_barrier_semaphore()
    for k in range(1, n_chip):
        pl.semaphore_signal(barrier, inc=1, device_id=((chip + k) % n_chip, core, ten),
                            device_id_type=MESH)
    pl.semaphore_wait(barrier, n_chip - 1)
    own = pltpu.make_async_copy(part_ref.at[chip], recv_out.at[chip], own_sem.at[0])
    own.start()
    copies = []
    for k in range(1, n_chip):
        dest = (chip + k) % n_chip
        cp = pltpu.make_async_remote_copy(
            part_ref.at[dest], recv_out.at[chip], send.at[k], recv.at[k],
            device_id=(dest, core, ten), device_id_type=MESH)
        cp.start()
        copies.append(cp)
    own.wait()
    for cp in copies:
        cp.wait_send()
        cp.wait_recv()


def _params(cid):
    return pltpu.CompilerParams(collective_id=cid, has_side_effects=True)


def body(out_grad, gate_act, up_act, w_down):
    seq_rows, ff = gate_act.shape
    width = w_down.shape[0]
    n_chip = lax.axis_size("chip")
    n_core = lax.axis_size("core")
    n_ten = lax.axis_size("tensor")
    core = lax.axis_index("core")
    grad_scale = 1.0 / math.sqrt(seq_rows * n_chip * n_core)
    gate_wide = gate_act.astype(jnp.float32)
    up_wide = up_act.astype(jnp.float32)
    sigmoid_gate = jax.nn.sigmoid(gate_wide)
    activated = gate_wide * sigmoid_gate
    hidden = (activated * up_wide).astype(jnp.bfloat16)

    n_lo = n_core
    n_plane = n_ten // n_lo
    rows_g, w_own, rows_other, w_other, hidden_other = pl.pallas_call(
        lambda *refs: _gather_kernel(n_chip, n_lo, *refs),
        out_shape=(
            jax.ShapeDtypeStruct((n_plane, n_lo, seq_rows, out_grad.shape[1]), out_grad.dtype),
            jax.ShapeDtypeStruct((n_chip, width, ff), w_down.dtype),
            jax.ShapeDtypeStruct((n_plane, seq_rows, out_grad.shape[1]), out_grad.dtype),
            jax.ShapeDtypeStruct((n_chip, width, ff), w_down.dtype),
            jax.ShapeDtypeStruct(hidden.shape, hidden.dtype),
        ),
        in_specs=[ANY, ANY, ANY],
        out_specs=(ANY, ANY, ANY, ANY, ANY),
        scratch_shapes=[pltpu.SemaphoreType.DMA((1,)), pltpu.SemaphoreType.DMA((1,)),
                        pltpu.SemaphoreType.DMA((n_plane // 2,)),
                        pltpu.SemaphoreType.DMA((n_plane // 2,)),
                        pltpu.SemaphoreType.DMA((n_plane // 2,)),
                        pltpu.SemaphoreType.DMA((n_plane // 2,)),
                        pltpu.SemaphoreType.DMA((n_chip,)), pltpu.SemaphoreType.DMA((n_chip,)),
                        pltpu.SemaphoreType.DMA((1,)), pltpu.SemaphoreType.DMA((1,)),
                        pltpu.SemaphoreType.DMA((n_chip,)), pltpu.SemaphoreType.DMA((n_chip,)),
                        pltpu.SemaphoreType.DMA((n_plane,)), pltpu.SemaphoreType.DMA((n_plane,)),
                        pltpu.SemaphoreType.DMA((2,))],
        compiler_params=_params(0),
    )(out_grad, w_down, hidden)

    rows_mine = lax.dynamic_index_in_dim(rows_g, core, 1, keepdims=False)
    rows_theirs = lax.dynamic_index_in_dim(rows_g, 1 - core, 1, keepdims=False)
    hidden_grad = jnp.einsum(
        "rtk,rkf->tf", rows_mine, w_own, preferred_element_type=jnp.float32
    ) + jnp.einsum("rtk,rkf->tf", rows_theirs, w_other, preferred_element_type=jnp.float32)

    partial = jnp.einsum(
        "rtk,tf->rkf", rows_mine, hidden, preferred_element_type=jnp.float32
    ) + jnp.einsum("rtk,tf->rkf", rows_other, hidden_other, preferred_element_type=jnp.float32)

    received = pl.pallas_call(
        lambda *refs: _scatter_kernel(n_chip, *refs),
        out_shape=jax.ShapeDtypeStruct(partial.shape, jnp.bfloat16),
        in_specs=[ANY],
        out_specs=ANY,
        scratch_shapes=[pltpu.SemaphoreType.DMA((n_chip,)), pltpu.SemaphoreType.DMA((n_chip,)),
                        pltpu.SemaphoreType.DMA((1,))],
        compiler_params=_params(2),
    )(partial.astype(jnp.bfloat16))
    summed = jnp.sum(received.astype(jnp.float32), axis=0)

    gate_grad = (
        hidden_grad * up_wide * sigmoid_gate * (1.0 + gate_wide * (1.0 - sigmoid_gate))
    ).astype(jnp.bfloat16)
    up_grad = (hidden_grad * activated).astype(jnp.bfloat16)
    down_grad = (summed * grad_scale).astype(jnp.bfloat16)
    return (gate_grad, up_grad, down_grad)


def solution(mesh):
    n_dp = mesh.shape["dp"]
    n_tensor = mesh.shape["tensor"]
    devices = np.asarray(mesh.devices).reshape(n_dp // 2, 2, n_tensor)
    split = Mesh(devices, ("chip", "core", "tensor"))
    placed = P(("chip", "core"), "tensor")
    return jax.shard_map(
        body,
        mesh=split,
        in_specs=(placed, placed, placed, placed),
        out_specs=(placed, placed, placed),
        check_vma=False,
    )
```

```python
import math

import jax
import jax.numpy as jnp
import numpy as np
from jax import lax
from jax.experimental import pallas as pl
from jax.experimental.pallas import tpu as pltpu
from jax.sharding import Mesh
from jax.sharding import PartitionSpec as P

MESH = pl.DeviceIdType.MESH
ANY = pl.BlockSpec(memory_space=pl.ANY)


def _where():
    return lax.axis_index("chip"), lax.axis_index("core"), lax.axis_index("tensor")


def _gather_kernel(n_chip, n_lo, og_ref, w_ref, hid_ref, rows_out, w_out, rows_other,
                   w_other, hid_other, x_send, x_recv, r_send, r_recv, l_send, l_recv,
                   w_send, w_recv, f_send, f_recv, fw_send, fw_recv, fr_send, fr_recv, own_sem):
    chip, core, ten = _where()
    n_plane = rows_out.shape[0]
    plane, lo = ten // n_lo, ten % n_lo
    right = ((plane + 1) % n_plane) * n_lo + lo
    left = ((plane + n_plane - 1) % n_plane) * n_lo + lo
    side = plane * n_lo + (1 - lo)
    other = (chip, 1 - core, ten)
    barrier = pltpu.get_barrier_semaphore()
    for t in (right, left, side):
        pl.semaphore_signal(barrier, inc=1, device_id=(chip, core, t), device_id_type=MESH)
    for k in range(1, n_chip):
        pl.semaphore_signal(barrier, inc=1, device_id=((chip + k) % n_chip, core, ten),
                            device_id_type=MESH)
    pl.semaphore_signal(barrier, inc=1, device_id=other, device_id_type=MESH)
    pl.semaphore_wait(barrier, 3 + (n_chip - 1) + 1)

    side_cp = pltpu.make_async_remote_copy(
        og_ref, rows_out.at[plane, lo], x_send.at[0], x_recv.at[0],
        device_id=(chip, core, side), device_id_type=MESH)
    side_cp.start()
    own_r = pltpu.make_async_copy(og_ref, rows_out.at[plane, lo], own_sem.at[0])
    own_w = pltpu.make_async_copy(w_ref, w_out.at[chip], own_sem.at[1])
    own_r.start()
    own_w.start()
    hid_cp = pltpu.make_async_remote_copy(hid_ref, hid_other, f_send.at[0], f_recv.at[0],
                                          device_id=other, device_id_type=MESH)
    hid_cp.start()
    forwards = [hid_cp]

    def fwd_w(k):
        r = (chip + n_chip - k) % n_chip
        src = w_ref if k == 0 else w_out.at[r]
        cp = pltpu.make_async_remote_copy(src, w_other.at[r], fw_send.at[k], fw_recv.at[k],
                                          device_id=other, device_id_type=MESH)
        cp.start()
        forwards.append(cp)

    def fwd_rows(d):
        p = (plane + d) % n_plane
        cp = pltpu.make_async_remote_copy(rows_out.at[p, 1 - core], rows_other.at[p],
                                          fr_send.at[d], fr_recv.at[d],
                                          device_id=other, device_id_type=MESH)
        cp.start()
        forwards.append(cp)

    fwd_w(0)
    own_r.wait()
    side_cp.wait_send()
    side_cp.wait_recv()
    fwd_rows(0)

    n_steps = n_plane // 2
    ring = {}
    for s in range(n_steps):
        for d, sends, recvs, to, src_plane, half in (
            ("r", r_send, r_recv, right, (plane + n_plane - s) % n_plane, 0),
            ("l", l_send, l_recv, left, (plane + s) % n_plane, 1),
        ):
            block = rows_out.at[src_plane]
            if s == n_steps - 1:
                block = rows_out.at[src_plane, half]
            ring[(d, s)] = pltpu.make_async_remote_copy(
                block, block, sends.at[s], recvs.at[s],
                device_id=(chip, core, to), device_id_type=MESH)
    for d in ("r", "l"):
        ring[(d, 0)].start()
    w_copies = []
    for k in range(1, n_chip):
        cp = pltpu.make_async_remote_copy(
            w_ref, w_out.at[chip], w_send.at[k], w_recv.at[k],
            device_id=((chip + k) % n_chip, core, ten), device_id_type=MESH)
        cp.start()
        w_copies.append(cp)
    for s in range(1, n_steps):
        for d in ("r", "l"):
            ring[(d, s - 1)].wait_recv()
            ring[(d, s)].start()
        fwd_rows(n_plane - s)
        fwd_rows(s)
    for d in ("r", "l"):
        ring[(d, n_steps - 1)].wait_recv()
        for s in range(n_steps):
            ring[(d, s)].wait_send()
    fwd_rows(n_steps)
    for k in range(1, n_chip):
        w_copies[k - 1].wait_recv()
        fwd_w(k)
    own_w.wait()
    for cp in w_copies:
        cp.wait_send()
    for cp in forwards:
        cp.wait_send()
        cp.wait_recv()


def _scatter_kernel(n_chip, tile, part_ref, rows_ref, w_ref, wo_ref, gate_ref, up_ref,
                    recv_out, gate_out, up_out, send, recv, own_sem):
    chip, core, ten = _where()
    barrier = pltpu.get_barrier_semaphore()
    for k in range(1, n_chip):
        pl.semaphore_signal(barrier, inc=1, device_id=((chip + k) % n_chip, core, ten),
                            device_id_type=MESH)
    pl.semaphore_wait(barrier, n_chip - 1)
    own = pltpu.make_async_copy(part_ref.at[chip], recv_out.at[chip], own_sem.at[0])
    own.start()
    copies = []
    for k in range(1, n_chip):
        dest = (chip + k) % n_chip
        cp = pltpu.make_async_remote_copy(
            part_ref.at[dest], recv_out.at[chip], send.at[k], recv.at[k],
            device_id=(dest, core, ten), device_id_type=MESH)
        cp.start()
        copies.append(cp)

    def one_tile(i, carry):
        rows = pl.ds(pl.multiple_of(i * tile, tile), tile)
        acc = jnp.zeros((tile, gate_ref.shape[1]), jnp.float32)
        for r in range(w_ref.shape[0]):
            acc += jnp.dot(rows_ref[r, core, rows, :], w_ref[r],
                           preferred_element_type=jnp.float32)
            acc += jnp.dot(rows_ref[r, 1 - core, rows, :], wo_ref[r],
                           preferred_element_type=jnp.float32)
        gate_wide = gate_ref[rows, :].astype(jnp.float32)
        up_wide = up_ref[rows, :].astype(jnp.float32)
        sigmoid_gate = jax.nn.sigmoid(gate_wide)
        activated = gate_wide * sigmoid_gate
        gate_out[rows, :] = (
            acc * up_wide * sigmoid_gate * (1.0 + gate_wide * (1.0 - sigmoid_gate))
        ).astype(gate_out.dtype)
        up_out[rows, :] = (acc * activated).astype(up_out.dtype)
        return carry

    lax.fori_loop(0, gate_ref.shape[0] // tile, one_tile, 0)

    own.wait()
    for cp in copies:
        cp.wait_send()
        cp.wait_recv()


def _params(cid):
    return pltpu.CompilerParams(collective_id=cid, has_side_effects=True)


def body(out_grad, gate_act, up_act, w_down):
    seq_rows, ff = gate_act.shape
    width = w_down.shape[0]
    n_chip = lax.axis_size("chip")
    n_core = lax.axis_size("core")
    n_ten = lax.axis_size("tensor")
    core = lax.axis_index("core")
    grad_scale = 1.0 / math.sqrt(seq_rows * n_chip * n_core)
    gate_wide = gate_act.astype(jnp.float32)
    up_wide = up_act.astype(jnp.float32)
    sigmoid_gate = jax.nn.sigmoid(gate_wide)
    activated = gate_wide * sigmoid_gate
    hidden = (activated * up_wide).astype(jnp.bfloat16)

    n_lo = n_core
    n_plane = n_ten // n_lo
    rows_g, w_own, rows_other, w_other, hidden_other = pl.pallas_call(
        lambda *refs: _gather_kernel(n_chip, n_lo, *refs),
        out_shape=(
            jax.ShapeDtypeStruct((n_plane, n_lo, seq_rows, out_grad.shape[1]), out_grad.dtype),
            jax.ShapeDtypeStruct((n_chip, width, ff), w_down.dtype),
            jax.ShapeDtypeStruct((n_plane, seq_rows, out_grad.shape[1]), out_grad.dtype),
            jax.ShapeDtypeStruct((n_chip, width, ff), w_down.dtype),
            jax.ShapeDtypeStruct(hidden.shape, hidden.dtype),
        ),
        in_specs=[ANY, ANY, ANY],
        out_specs=(ANY, ANY, ANY, ANY, ANY),
        scratch_shapes=[pltpu.SemaphoreType.DMA((1,)), pltpu.SemaphoreType.DMA((1,)),
                        pltpu.SemaphoreType.DMA((n_plane // 2,)),
                        pltpu.SemaphoreType.DMA((n_plane // 2,)),
                        pltpu.SemaphoreType.DMA((n_plane // 2,)),
                        pltpu.SemaphoreType.DMA((n_plane // 2,)),
                        pltpu.SemaphoreType.DMA((n_chip,)), pltpu.SemaphoreType.DMA((n_chip,)),
                        pltpu.SemaphoreType.DMA((1,)), pltpu.SemaphoreType.DMA((1,)),
                        pltpu.SemaphoreType.DMA((n_chip,)), pltpu.SemaphoreType.DMA((n_chip,)),
                        pltpu.SemaphoreType.DMA((n_plane,)), pltpu.SemaphoreType.DMA((n_plane,)),
                        pltpu.SemaphoreType.DMA((2,))],
        compiler_params=_params(0),
    )(out_grad, w_down, hidden)

    rows_mine = lax.dynamic_index_in_dim(rows_g, core, 1, keepdims=False)
    partial = jnp.einsum(
        "rtk,tf->rkf", rows_mine, hidden, preferred_element_type=jnp.float32
    ) + jnp.einsum("rtk,tf->rkf", rows_other, hidden_other, preferred_element_type=jnp.float32)

    vmem = pl.BlockSpec(memory_space=pltpu.VMEM)
    received, gate_grad, up_grad = pl.pallas_call(
        lambda *refs: _scatter_kernel(n_chip, min(128, seq_rows), *refs),
        out_shape=(
            jax.ShapeDtypeStruct(partial.shape, jnp.bfloat16),
            jax.ShapeDtypeStruct(gate_act.shape, jnp.bfloat16),
            jax.ShapeDtypeStruct(up_act.shape, jnp.bfloat16),
        ),
        in_specs=[ANY, vmem, vmem, vmem, vmem, vmem],
        out_specs=(ANY, vmem, vmem),
        scratch_shapes=[pltpu.SemaphoreType.DMA((n_chip,)), pltpu.SemaphoreType.DMA((n_chip,)),
                        pltpu.SemaphoreType.DMA((1,))],
        compiler_params=_params(2),
    )(partial.astype(jnp.bfloat16), rows_g, w_own, w_other, gate_act, up_act)
    summed = jnp.sum(received.astype(jnp.float32), axis=0)
    down_grad = (summed * grad_scale).astype(jnp.bfloat16)
    return (gate_grad, up_grad, down_grad)


def solution(mesh):
    n_dp = mesh.shape["dp"]
    n_tensor = mesh.shape["tensor"]
    devices = np.asarray(mesh.devices).reshape(n_dp // 2, 2, n_tensor)
    split = Mesh(devices, ("chip", "core", "tensor"))
    placed = P(("chip", "core"), "tensor")
    return jax.shard_map(
        body,
        mesh=split,
        in_specs=(placed, placed, placed, placed),
        out_specs=(placed, placed, placed),
        check_vma=False,
    )
```

```python
import math

import jax
import jax.numpy as jnp
import numpy as np
from jax import lax
from jax.experimental import pallas as pl
from jax.experimental.pallas import tpu as pltpu
from jax.sharding import Mesh
from jax.sharding import PartitionSpec as P

MESH = pl.DeviceIdType.MESH
ANY = pl.BlockSpec(memory_space=pl.ANY)


def _where():
    return lax.axis_index("chip"), lax.axis_index("core"), lax.axis_index("tensor")


def _gather_kernel(n_chip, n_lo, og_ref, w_ref, hid_ref, rows_out, w_out, rows_other,
                   w_other, hid_other, x_send, x_recv, r_send, r_recv, l_send, l_recv,
                   w_send, w_recv, f_send, f_recv, fw_send, fw_recv, fr_send, fr_recv, own_sem):
    chip, core, ten = _where()
    n_plane = rows_out.shape[0]
    plane, lo = ten // n_lo, ten % n_lo
    right = ((plane + 1) % n_plane) * n_lo + lo
    left = ((plane + n_plane - 1) % n_plane) * n_lo + lo
    side = plane * n_lo + (1 - lo)
    other = (chip, 1 - core, ten)
    barrier = pltpu.get_barrier_semaphore()
    for t in (right, left, side):
        pl.semaphore_signal(barrier, inc=1, device_id=(chip, core, t), device_id_type=MESH)
    for k in range(1, n_chip):
        pl.semaphore_signal(barrier, inc=1, device_id=((chip + k) % n_chip, core, ten),
                            device_id_type=MESH)
    pl.semaphore_signal(barrier, inc=1, device_id=other, device_id_type=MESH)
    pl.semaphore_wait(barrier, 3 + (n_chip - 1) + 1)

    side_cp = pltpu.make_async_remote_copy(
        og_ref, rows_out.at[plane, lo], x_send.at[0], x_recv.at[0],
        device_id=(chip, core, side), device_id_type=MESH)
    side_cp.start()
    own_r = pltpu.make_async_copy(og_ref, rows_out.at[plane, lo], own_sem.at[0])
    own_w = pltpu.make_async_copy(w_ref, w_out.at[chip], own_sem.at[1])
    own_r.start()
    own_w.start()
    hid_cp = pltpu.make_async_remote_copy(hid_ref, hid_other, f_send.at[0], f_recv.at[0],
                                          device_id=other, device_id_type=MESH)
    hid_cp.start()
    forwards = [hid_cp]

    def fwd_w(k):
        r = (chip + n_chip - k) % n_chip
        src = w_ref if k == 0 else w_out.at[r]
        cp = pltpu.make_async_remote_copy(src, w_other.at[r], fw_send.at[k], fw_recv.at[k],
                                          device_id=other, device_id_type=MESH)
        cp.start()
        forwards.append(cp)

    def fwd_rows(d):
        p = (plane + d) % n_plane
        cp = pltpu.make_async_remote_copy(rows_out.at[p, 1 - core], rows_other.at[p],
                                          fr_send.at[d], fr_recv.at[d],
                                          device_id=other, device_id_type=MESH)
        cp.start()
        forwards.append(cp)

    fwd_w(0)
    own_r.wait()
    side_cp.wait_send()
    side_cp.wait_recv()
    fwd_rows(0)

    n_steps = n_plane // 2
    ring = {}
    for s in range(n_steps):
        for d, sends, recvs, to, src_plane, half in (
            ("r", r_send, r_recv, right, (plane + n_plane - s) % n_plane, 0),
            ("l", l_send, l_recv, left, (plane + s) % n_plane, 1),
        ):
            block = rows_out.at[src_plane]
            if s == n_steps - 1:
                block = rows_out.at[src_plane, half]
            ring[(d, s)] = pltpu.make_async_remote_copy(
                block, block, sends.at[s], recvs.at[s],
                device_id=(chip, core, to), device_id_type=MESH)
    for d in ("r", "l"):
        ring[(d, 0)].start()
    w_copies = []
    for k in range(1, n_chip):
        cp = pltpu.make_async_remote_copy(
            w_ref, w_out.at[chip], w_send.at[k], w_recv.at[k],
            device_id=((chip + k) % n_chip, core, ten), device_id_type=MESH)
        cp.start()
        w_copies.append(cp)
    for s in range(1, n_steps):
        for d in ("r", "l"):
            ring[(d, s - 1)].wait_recv()
            ring[(d, s)].start()
        fwd_rows(n_plane - s)
        fwd_rows(s)
    for d in ("r", "l"):
        ring[(d, n_steps - 1)].wait_recv()
        for s in range(n_steps):
            ring[(d, s)].wait_send()
    fwd_rows(n_steps)
    for k in range(1, n_chip):
        w_copies[k - 1].wait_recv()
        fwd_w(k)
    own_w.wait()
    for cp in w_copies:
        cp.wait_send()
    for cp in forwards:
        cp.wait_send()
        cp.wait_recv()


def _scatter_kernel(n_chip, tile, part_ref, rows_hbm, w_hbm, wo_hbm, gate_hbm, up_hbm,
                    recv_out, gate_out, up_out, send, recv, own_sem,
                    rows_ref, w_ref, wo_ref, gate_ref, up_ref, load_sem):
    chip, core, ten = _where()
    barrier = pltpu.get_barrier_semaphore()
    for k in range(1, n_chip):
        pl.semaphore_signal(barrier, inc=1, device_id=((chip + k) % n_chip, core, ten),
                            device_id_type=MESH)
    pl.semaphore_wait(barrier, n_chip - 1)
    own = pltpu.make_async_copy(part_ref.at[chip], recv_out.at[chip], own_sem.at[0])
    own.start()
    copies = []
    for k in range(1, n_chip):
        dest = (chip + k) % n_chip
        cp = pltpu.make_async_remote_copy(
            part_ref.at[dest], recv_out.at[chip], send.at[k], recv.at[k],
            device_id=(dest, core, ten), device_id_type=MESH)
        cp.start()
        copies.append(cp)
    loads = [pltpu.make_async_copy(src, dst, load_sem.at[i]) for i, (src, dst) in enumerate(
        ((rows_hbm, rows_ref), (w_hbm, w_ref), (wo_hbm, wo_ref), (gate_hbm, gate_ref),
         (up_hbm, up_ref)))]
    for ld in loads:
        ld.start()
    for ld in loads:
        ld.wait()

    def one_tile(i, carry):
        rows = pl.ds(pl.multiple_of(i * tile, tile), tile)
        acc = jnp.zeros((tile, gate_ref.shape[1]), jnp.float32)
        for r in range(w_ref.shape[0]):
            acc += jnp.dot(rows_ref[r, core, rows, :], w_ref[r],
                           preferred_element_type=jnp.float32)
            acc += jnp.dot(rows_ref[r, 1 - core, rows, :], wo_ref[r],
                           preferred_element_type=jnp.float32)
        gate_wide = gate_ref[rows, :].astype(jnp.float32)
        up_wide = up_ref[rows, :].astype(jnp.float32)
        sigmoid_gate = jax.nn.sigmoid(gate_wide)
        activated = gate_wide * sigmoid_gate
        gate_out[rows, :] = (
            acc * up_wide * sigmoid_gate * (1.0 + gate_wide * (1.0 - sigmoid_gate))
        ).astype(gate_out.dtype)
        up_out[rows, :] = (acc * activated).astype(up_out.dtype)
        return carry

    lax.fori_loop(0, gate_ref.shape[0] // tile, one_tile, 0)

    own.wait()
    for cp in copies:
        cp.wait_send()
        cp.wait_recv()


def _params(cid):
    return pltpu.CompilerParams(collective_id=cid, has_side_effects=True)


def body(out_grad, gate_act, up_act, w_down):
    seq_rows, ff = gate_act.shape
    width = w_down.shape[0]
    n_chip = lax.axis_size("chip")
    n_core = lax.axis_size("core")
    n_ten = lax.axis_size("tensor")
    core = lax.axis_index("core")
    grad_scale = 1.0 / math.sqrt(seq_rows * n_chip * n_core)
    gate_wide = gate_act.astype(jnp.float32)
    up_wide = up_act.astype(jnp.float32)
    sigmoid_gate = jax.nn.sigmoid(gate_wide)
    activated = gate_wide * sigmoid_gate
    hidden = (activated * up_wide).astype(jnp.bfloat16)

    n_lo = n_core
    n_plane = n_ten // n_lo
    rows_g, w_own, rows_other, w_other, hidden_other = pl.pallas_call(
        lambda *refs: _gather_kernel(n_chip, n_lo, *refs),
        out_shape=(
            jax.ShapeDtypeStruct((n_plane, n_lo, seq_rows, out_grad.shape[1]), out_grad.dtype),
            jax.ShapeDtypeStruct((n_chip, width, ff), w_down.dtype),
            jax.ShapeDtypeStruct((n_plane, seq_rows, out_grad.shape[1]), out_grad.dtype),
            jax.ShapeDtypeStruct((n_chip, width, ff), w_down.dtype),
            jax.ShapeDtypeStruct(hidden.shape, hidden.dtype),
        ),
        in_specs=[ANY, ANY, ANY],
        out_specs=(ANY, ANY, ANY, ANY, ANY),
        scratch_shapes=[pltpu.SemaphoreType.DMA((1,)), pltpu.SemaphoreType.DMA((1,)),
                        pltpu.SemaphoreType.DMA((n_plane // 2,)),
                        pltpu.SemaphoreType.DMA((n_plane // 2,)),
                        pltpu.SemaphoreType.DMA((n_plane // 2,)),
                        pltpu.SemaphoreType.DMA((n_plane // 2,)),
                        pltpu.SemaphoreType.DMA((n_chip,)), pltpu.SemaphoreType.DMA((n_chip,)),
                        pltpu.SemaphoreType.DMA((1,)), pltpu.SemaphoreType.DMA((1,)),
                        pltpu.SemaphoreType.DMA((n_chip,)), pltpu.SemaphoreType.DMA((n_chip,)),
                        pltpu.SemaphoreType.DMA((n_plane,)), pltpu.SemaphoreType.DMA((n_plane,)),
                        pltpu.SemaphoreType.DMA((2,))],
        compiler_params=_params(0),
    )(out_grad, w_down, hidden)

    rows_mine = lax.dynamic_index_in_dim(rows_g, core, 1, keepdims=False)
    partial = jnp.einsum(
        "rtk,tf->rkf", rows_mine, hidden, preferred_element_type=jnp.float32
    ) + jnp.einsum("rtk,tf->rkf", rows_other, hidden_other, preferred_element_type=jnp.float32)

    vmem = pl.BlockSpec(memory_space=pltpu.VMEM)
    received, gate_grad, up_grad = pl.pallas_call(
        lambda *refs: _scatter_kernel(n_chip, min(128, seq_rows), *refs),
        out_shape=(
            jax.ShapeDtypeStruct(partial.shape, jnp.bfloat16),
            jax.ShapeDtypeStruct(gate_act.shape, jnp.bfloat16),
            jax.ShapeDtypeStruct(up_act.shape, jnp.bfloat16),
        ),
        in_specs=[ANY, ANY, ANY, ANY, ANY, ANY],
        out_specs=(ANY, vmem, vmem),
        scratch_shapes=[pltpu.SemaphoreType.DMA((n_chip,)), pltpu.SemaphoreType.DMA((n_chip,)),
                        pltpu.SemaphoreType.DMA((1,)),
                        pltpu.VMEM(rows_g.shape, rows_g.dtype),
                        pltpu.VMEM(w_own.shape, w_own.dtype),
                        pltpu.VMEM(w_other.shape, w_other.dtype),
                        pltpu.VMEM(gate_act.shape, gate_act.dtype),
                        pltpu.VMEM(up_act.shape, up_act.dtype),
                        pltpu.SemaphoreType.DMA((5,))],
        compiler_params=_params(2),
    )(partial.astype(jnp.bfloat16), rows_g, w_own, w_other, gate_act, up_act)
    summed = jnp.sum(received.astype(jnp.float32), axis=0)
    down_grad = (summed * grad_scale).astype(jnp.bfloat16)
    return (gate_grad, up_grad, down_grad)


def solution(mesh):
    n_dp = mesh.shape["dp"]
    n_tensor = mesh.shape["tensor"]
    devices = np.asarray(mesh.devices).reshape(n_dp // 2, 2, n_tensor)
    split = Mesh(devices, ("chip", "core", "tensor"))
    placed = P(("chip", "core"), "tensor")
    return jax.shard_map(
        body,
        mesh=split,
        in_specs=(placed, placed, placed, placed),
        out_specs=(placed, placed, placed),
        check_vma=False,
    )
```

```python
import math

import jax
import jax.numpy as jnp
import numpy as np
from jax import lax
from jax.experimental import pallas as pl
from jax.experimental.pallas import tpu as pltpu
from jax.sharding import Mesh
from jax.sharding import PartitionSpec as P

MESH = pl.DeviceIdType.MESH
ANY = pl.BlockSpec(memory_space=pl.ANY)


def _where():
    return lax.axis_index("chip"), lax.axis_index("core"), lax.axis_index("tensor")


def _gather_kernel(n_chip, n_lo, og_ref, w_ref, hid_ref, rows_out, w_out, rows_other,
                   w_other, hid_other, part_out, x_send, x_recv, r_send, r_recv, l_send, l_recv,
                   w_send, w_recv, f_send, f_recv, fw_send, fw_recv, fr_send, fr_recv,
                   own_sem, rows_v, ro_v, hid_v, ho_v, load_sem):
    chip, core, ten = _where()
    n_plane = rows_out.shape[0]
    plane, lo = ten // n_lo, ten % n_lo
    right = ((plane + 1) % n_plane) * n_lo + lo
    left = ((plane + n_plane - 1) % n_plane) * n_lo + lo
    side = plane * n_lo + (1 - lo)
    other = (chip, 1 - core, ten)
    barrier = pltpu.get_barrier_semaphore()
    for t in (right, left, side):
        pl.semaphore_signal(barrier, inc=1, device_id=(chip, core, t), device_id_type=MESH)
    for k in range(1, n_chip):
        pl.semaphore_signal(barrier, inc=1, device_id=((chip + k) % n_chip, core, ten),
                            device_id_type=MESH)
    pl.semaphore_signal(barrier, inc=1, device_id=other, device_id_type=MESH)
    pl.semaphore_wait(barrier, 3 + (n_chip - 1) + 1)

    side_cp = pltpu.make_async_remote_copy(
        og_ref, rows_out.at[plane, lo], x_send.at[0], x_recv.at[0],
        device_id=(chip, core, side), device_id_type=MESH)
    side_cp.start()
    own_r = pltpu.make_async_copy(og_ref, rows_out.at[plane, lo], own_sem.at[0])
    own_w = pltpu.make_async_copy(w_ref, w_out.at[chip], own_sem.at[1])
    own_r.start()
    own_w.start()
    hid_cp = pltpu.make_async_remote_copy(hid_ref, hid_other, f_send.at[0], f_recv.at[0],
                                          device_id=other, device_id_type=MESH)
    hid_cp.start()
    forwards = [hid_cp]

    def fwd_w(k):
        r = (chip + n_chip - k) % n_chip
        src = w_ref if k == 0 else w_out.at[r]
        cp = pltpu.make_async_remote_copy(src, w_other.at[r], fw_send.at[k], fw_recv.at[k],
                                          device_id=other, device_id_type=MESH)
        cp.start()
        forwards.append(cp)

    def fwd_rows(d):
        p = (plane + d) % n_plane
        cp = pltpu.make_async_remote_copy(rows_out.at[p, 1 - core], rows_other.at[p],
                                          fr_send.at[d], fr_recv.at[d],
                                          device_id=other, device_id_type=MESH)
        cp.start()
        forwards.append(cp)

    fwd_w(0)
    own_r.wait()
    side_cp.wait_send()
    side_cp.wait_recv()
    fwd_rows(0)

    n_steps = n_plane // 2
    ring = {}
    for s in range(n_steps):
        for d, sends, recvs, to, src_plane, half in (
            ("r", r_send, r_recv, right, (plane + n_plane - s) % n_plane, 0),
            ("l", l_send, l_recv, left, (plane + s) % n_plane, 1),
        ):
            block = rows_out.at[src_plane]
            if s == n_steps - 1:
                block = rows_out.at[src_plane, half]
            ring[(d, s)] = pltpu.make_async_remote_copy(
                block, block, sends.at[s], recvs.at[s],
                device_id=(chip, core, to), device_id_type=MESH)
    for d in ("r", "l"):
        ring[(d, 0)].start()
    w_copies = []
    for k in range(1, n_chip):
        cp = pltpu.make_async_remote_copy(
            w_ref, w_out.at[chip], w_send.at[k], w_recv.at[k],
            device_id=((chip + k) % n_chip, core, ten), device_id_type=MESH)
        cp.start()
        w_copies.append(cp)
    for s in range(1, n_steps):
        for d in ("r", "l"):
            ring[(d, s - 1)].wait_recv()
            ring[(d, s)].start()
        fwd_rows(n_plane - s)
        fwd_rows(s)
    for d in ("r", "l"):
        ring[(d, n_steps - 1)].wait_recv()
        for s in range(n_steps):
            ring[(d, s)].wait_send()
    fwd_rows(n_steps)

    loads = [pltpu.make_async_copy(rows_out.at[r, core], rows_v.at[r], load_sem.at[r])
             for r in range(n_plane)]
    loads.append(pltpu.make_async_copy(hid_ref, hid_v, load_sem.at[n_plane]))
    for ld in loads:
        ld.start()
    for cp in forwards:
        cp.wait_recv()
    later = [pltpu.make_async_copy(rows_other, ro_v, load_sem.at[n_plane + 1]),
             pltpu.make_async_copy(hid_other, ho_v, load_sem.at[n_plane + 2])]
    for ld in later:
        ld.start()
    for ld in loads + later:
        ld.wait()
    for r in range(n_plane):
        part = lax.dot_general(rows_v[r], hid_v[...], (((0,), (0,)), ((), ())),
                               preferred_element_type=jnp.float32)
        part += lax.dot_general(ro_v[r], ho_v[...], (((0,), (0,)), ((), ())),
                                preferred_element_type=jnp.float32)
        part_out[r] = part.astype(part_out.dtype)

    n_before = len(forwards)
    for k in range(1, n_chip):
        w_copies[k - 1].wait_recv()
        fwd_w(k)
    own_w.wait()
    for cp in w_copies:
        cp.wait_send()
    for i, cp in enumerate(forwards):
        cp.wait_send()
        if i >= n_before:
            cp.wait_recv()


def _scatter_kernel(n_chip, tile, part_ref, rows_hbm, w_hbm, wo_hbm, gate_hbm, up_hbm,
                    recv_out, gate_out, up_out, send, recv, own_sem,
                    rows_ref, w_ref, wo_ref, gate_ref, up_ref, load_sem):
    chip, core, ten = _where()
    barrier = pltpu.get_barrier_semaphore()
    for k in range(1, n_chip):
        pl.semaphore_signal(barrier, inc=1, device_id=((chip + k) % n_chip, core, ten),
                            device_id_type=MESH)
    pl.semaphore_wait(barrier, n_chip - 1)
    own = pltpu.make_async_copy(part_ref.at[chip], recv_out.at[chip], own_sem.at[0])
    own.start()
    copies = []
    for k in range(1, n_chip):
        dest = (chip + k) % n_chip
        cp = pltpu.make_async_remote_copy(
            part_ref.at[dest], recv_out.at[chip], send.at[k], recv.at[k],
            device_id=(dest, core, ten), device_id_type=MESH)
        cp.start()
        copies.append(cp)
    loads = [pltpu.make_async_copy(src, dst, load_sem.at[i]) for i, (src, dst) in enumerate(
        ((rows_hbm, rows_ref), (w_hbm, w_ref), (wo_hbm, wo_ref), (gate_hbm, gate_ref),
         (up_hbm, up_ref)))]
    for ld in loads:
        ld.start()
    for ld in loads:
        ld.wait()

    def one_tile(i, carry):
        rows = pl.ds(pl.multiple_of(i * tile, tile), tile)
        acc = jnp.zeros((tile, gate_ref.shape[1]), jnp.float32)
        for r in range(w_ref.shape[0]):
            acc += jnp.dot(rows_ref[r, core, rows, :], w_ref[r],
                           preferred_element_type=jnp.float32)
            acc += jnp.dot(rows_ref[r, 1 - core, rows, :], wo_ref[r],
                           preferred_element_type=jnp.float32)
        gate_wide = gate_ref[rows, :].astype(jnp.float32)
        up_wide = up_ref[rows, :].astype(jnp.float32)
        sigmoid_gate = jax.nn.sigmoid(gate_wide)
        activated = gate_wide * sigmoid_gate
        gate_out[rows, :] = (
            acc * up_wide * sigmoid_gate * (1.0 + gate_wide * (1.0 - sigmoid_gate))
        ).astype(gate_out.dtype)
        up_out[rows, :] = (acc * activated).astype(up_out.dtype)
        return carry

    lax.fori_loop(0, gate_ref.shape[0] // tile, one_tile, 0)

    own.wait()
    for cp in copies:
        cp.wait_send()
        cp.wait_recv()


def _params(cid):
    return pltpu.CompilerParams(collective_id=cid, has_side_effects=True)


def body(out_grad, gate_act, up_act, w_down):
    seq_rows, ff = gate_act.shape
    width = w_down.shape[0]
    n_chip = lax.axis_size("chip")
    n_core = lax.axis_size("core")
    n_ten = lax.axis_size("tensor")
    core = lax.axis_index("core")
    grad_scale = 1.0 / math.sqrt(seq_rows * n_chip * n_core)
    gate_wide = gate_act.astype(jnp.float32)
    up_wide = up_act.astype(jnp.float32)
    sigmoid_gate = jax.nn.sigmoid(gate_wide)
    activated = gate_wide * sigmoid_gate
    hidden = (activated * up_wide).astype(jnp.bfloat16)

    n_lo = n_core
    n_plane = n_ten // n_lo
    vmem = pl.BlockSpec(memory_space=pltpu.VMEM)
    rows_g, w_own, rows_other, w_other, hidden_other, partial = pl.pallas_call(
        lambda *refs: _gather_kernel(n_chip, n_lo, *refs),
        out_shape=(
            jax.ShapeDtypeStruct((n_plane, n_lo, seq_rows, out_grad.shape[1]), out_grad.dtype),
            jax.ShapeDtypeStruct((n_chip, width, ff), w_down.dtype),
            jax.ShapeDtypeStruct((n_plane, seq_rows, out_grad.shape[1]), out_grad.dtype),
            jax.ShapeDtypeStruct((n_chip, width, ff), w_down.dtype),
            jax.ShapeDtypeStruct(hidden.shape, hidden.dtype),
            jax.ShapeDtypeStruct((n_chip, width, ff), jnp.bfloat16),
        ),
        in_specs=[ANY, ANY, ANY],
        out_specs=(ANY, ANY, ANY, ANY, ANY, vmem),
        scratch_shapes=[pltpu.SemaphoreType.DMA((1,)), pltpu.SemaphoreType.DMA((1,)),
                        pltpu.SemaphoreType.DMA((n_plane // 2,)),
                        pltpu.SemaphoreType.DMA((n_plane // 2,)),
                        pltpu.SemaphoreType.DMA((n_plane // 2,)),
                        pltpu.SemaphoreType.DMA((n_plane // 2,)),
                        pltpu.SemaphoreType.DMA((n_chip,)), pltpu.SemaphoreType.DMA((n_chip,)),
                        pltpu.SemaphoreType.DMA((1,)), pltpu.SemaphoreType.DMA((1,)),
                        pltpu.SemaphoreType.DMA((n_chip,)), pltpu.SemaphoreType.DMA((n_chip,)),
                        pltpu.SemaphoreType.DMA((n_plane,)), pltpu.SemaphoreType.DMA((n_plane,)),
                        pltpu.SemaphoreType.DMA((2,)),
                        pltpu.VMEM((n_plane, seq_rows, out_grad.shape[1]), out_grad.dtype),
                        pltpu.VMEM((n_plane, seq_rows, out_grad.shape[1]), out_grad.dtype),
                        pltpu.VMEM(hidden.shape, hidden.dtype),
                        pltpu.VMEM(hidden.shape, hidden.dtype),
                        pltpu.SemaphoreType.DMA((n_plane + 3,))],
        compiler_params=_params(0),
    )(out_grad, w_down, hidden)

    received, gate_grad, up_grad = pl.pallas_call(
        lambda *refs: _scatter_kernel(n_chip, min(128, seq_rows), *refs),
        out_shape=(
            jax.ShapeDtypeStruct(partial.shape, jnp.bfloat16),
            jax.ShapeDtypeStruct(gate_act.shape, jnp.bfloat16),
            jax.ShapeDtypeStruct(up_act.shape, jnp.bfloat16),
        ),
        in_specs=[vmem, ANY, ANY, ANY, ANY, ANY],
        out_specs=(ANY, vmem, vmem),
        scratch_shapes=[pltpu.SemaphoreType.DMA((n_chip,)), pltpu.SemaphoreType.DMA((n_chip,)),
                        pltpu.SemaphoreType.DMA((1,)),
                        pltpu.VMEM(rows_g.shape, rows_g.dtype),
                        pltpu.VMEM(w_own.shape, w_own.dtype),
                        pltpu.VMEM(w_other.shape, w_other.dtype),
                        pltpu.VMEM(gate_act.shape, gate_act.dtype),
                        pltpu.VMEM(up_act.shape, up_act.dtype),
                        pltpu.SemaphoreType.DMA((5,))],
        compiler_params=_params(2),
    )(partial, rows_g, w_own, w_other, gate_act, up_act)
    summed = jnp.sum(received.astype(jnp.float32), axis=0)
    down_grad = (summed * grad_scale).astype(jnp.bfloat16)
    return (gate_grad, up_grad, down_grad)


def solution(mesh):
    n_dp = mesh.shape["dp"]
    n_tensor = mesh.shape["tensor"]
    devices = np.asarray(mesh.devices).reshape(n_dp // 2, 2, n_tensor)
    split = Mesh(devices, ("chip", "core", "tensor"))
    placed = P(("chip", "core"), "tensor")
    return jax.shard_map(
        body,
        mesh=split,
        in_specs=(placed, placed, placed, placed),
        out_specs=(placed, placed, placed),
        check_vma=False,
    )
```

```python
import math

import jax
import jax.numpy as jnp
import numpy as np
from jax import lax
from jax.experimental import pallas as pl
from jax.experimental.pallas import tpu as pltpu
from jax.sharding import Mesh
from jax.sharding import PartitionSpec as P

MESH = pl.DeviceIdType.MESH
ANY = pl.BlockSpec(memory_space=pl.ANY)


def _where():
    return lax.axis_index("chip"), lax.axis_index("core"), lax.axis_index("tensor")


def _gather_kernel(n_chip, n_lo, og_ref, w_ref, hid_ref, rows_out, w_out, w_other, part_out,
                   x_send, x_recv, r_send, r_recv, l_send, l_recv, w_send, w_recv,
                   f_send, f_recv, fw_send, fw_recv, fr_send, fr_recv, own_sem,
                   rows_v, ro_v, hid_v, ho_v, load_sem):
    chip, core, ten = _where()
    n_plane = rows_out.shape[0]
    plane, lo = ten // n_lo, ten % n_lo
    right = ((plane + 1) % n_plane) * n_lo + lo
    left = ((plane + n_plane - 1) % n_plane) * n_lo + lo
    side = plane * n_lo + (1 - lo)
    other = (chip, 1 - core, ten)
    barrier = pltpu.get_barrier_semaphore()
    for t in (right, left, side):
        pl.semaphore_signal(barrier, inc=1, device_id=(chip, core, t), device_id_type=MESH)
    for k in range(1, n_chip):
        pl.semaphore_signal(barrier, inc=1, device_id=((chip + k) % n_chip, core, ten),
                            device_id_type=MESH)
    pl.semaphore_signal(barrier, inc=1, device_id=other, device_id_type=MESH)
    pl.semaphore_wait(barrier, 3 + (n_chip - 1) + 1)

    side_cp = pltpu.make_async_remote_copy(
        og_ref, rows_out.at[plane, lo], x_send.at[0], x_recv.at[0],
        device_id=(chip, core, side), device_id_type=MESH)
    side_cp.start()
    own_r = pltpu.make_async_copy(og_ref, rows_out.at[plane, lo], own_sem.at[0])
    own_w = pltpu.make_async_copy(w_ref, w_out.at[chip], own_sem.at[1])
    own_r.start()
    own_w.start()
    hid_cp = pltpu.make_async_remote_copy(hid_ref, ho_v, f_send.at[0], f_recv.at[0],
                                          device_id=other, device_id_type=MESH)
    hid_cp.start()
    hid_ld = pltpu.make_async_copy(hid_ref, hid_v, load_sem.at[n_plane])
    hid_ld.start()
    forwards = [hid_cp]
    w_fwds = []
    rows_fwd = {}
    rows_ld = {}

    def fwd_w(k):
        r = (chip + n_chip - k) % n_chip
        src = w_ref if k == 0 else w_out.at[r]
        cp = pltpu.make_async_remote_copy(src, w_other.at[r], fw_send.at[k], fw_recv.at[k],
                                          device_id=other, device_id_type=MESH)
        cp.start()
        forwards.append(cp)
        w_fwds.append(cp)

    def arrived(d):
        p = (plane + d) % n_plane
        cp = pltpu.make_async_remote_copy(rows_out.at[p, 1 - core], ro_v.at[p],
                                          fr_send.at[d], fr_recv.at[d],
                                          device_id=other, device_id_type=MESH)
        cp.start()
        forwards.append(cp)
        rows_fwd[d] = cp
        ld = pltpu.make_async_copy(rows_out.at[p, core], rows_v.at[p], load_sem.at[d])
        ld.start()
        rows_ld[d] = ld

    def partial(d):
        p = (plane + d) % n_plane
        rows_ld[d].wait()
        rows_fwd[d].wait_recv()
        part = lax.dot_general(rows_v[p], hid_v[...], (((0,), (0,)), ((), ())),
                               preferred_element_type=jnp.float32)
        part += lax.dot_general(ro_v[p], ho_v[...], (((0,), (0,)), ((), ())),
                                preferred_element_type=jnp.float32)
        part_out[p] = part.astype(part_out.dtype)

    fwd_w(0)
    own_r.wait()
    side_cp.wait_send()
    side_cp.wait_recv()
    arrived(0)

    n_steps = n_plane // 2
    ring = {}
    for s in range(n_steps):
        for d, sends, recvs, to, src_plane, half in (
            ("r", r_send, r_recv, right, (plane + n_plane - s) % n_plane, 0),
            ("l", l_send, l_recv, left, (plane + s) % n_plane, 1),
        ):
            block = rows_out.at[src_plane]
            if s == n_steps - 1:
                block = rows_out.at[src_plane, half]
            ring[(d, s)] = pltpu.make_async_remote_copy(
                block, block, sends.at[s], recvs.at[s],
                device_id=(chip, core, to), device_id_type=MESH)
    for d in ("r", "l"):
        ring[(d, 0)].start()
    w_copies = []
    for k in range(1, n_chip):
        cp = pltpu.make_async_remote_copy(
            w_ref, w_out.at[chip], w_send.at[k], w_recv.at[k],
            device_id=((chip + k) % n_chip, core, ten), device_id_type=MESH)
        cp.start()
        w_copies.append(cp)
    hid_ld.wait()
    hid_cp.wait_recv()
    pending = [0]
    for s in range(1, n_steps):
        for d in ("r", "l"):
            ring[(d, s - 1)].wait_recv()
            ring[(d, s)].start()
        arrived(n_plane - s)
        arrived(s)
        for d in pending:
            partial(d)
        pending = [n_plane - s, s]
    for d in ("r", "l"):
        ring[(d, n_steps - 1)].wait_recv()
        for s in range(n_steps):
            ring[(d, s)].wait_send()
    arrived(n_steps)
    for d in pending + [n_steps]:
        partial(d)

    for k in range(1, n_chip):
        w_copies[k - 1].wait_recv()
        fwd_w(k)
    own_w.wait()
    for cp in w_copies:
        cp.wait_send()
    for cp in forwards:
        cp.wait_send()
    for cp in w_fwds:
        cp.wait_recv()


def _scatter_kernel(n_chip, tile, part_ref, rows_hbm, w_hbm, wo_hbm, gate_hbm, up_hbm,
                    recv_out, gate_out, up_out, send, recv, own_sem,
                    rows_ref, w_ref, wo_ref, gate_ref, up_ref, load_sem):
    chip, core, ten = _where()
    barrier = pltpu.get_barrier_semaphore()
    for k in range(1, n_chip):
        pl.semaphore_signal(barrier, inc=1, device_id=((chip + k) % n_chip, core, ten),
                            device_id_type=MESH)
    pl.semaphore_wait(barrier, n_chip - 1)
    own = pltpu.make_async_copy(part_ref.at[chip], recv_out.at[chip], own_sem.at[0])
    own.start()
    copies = []
    for k in range(1, n_chip):
        dest = (chip + k) % n_chip
        cp = pltpu.make_async_remote_copy(
            part_ref.at[dest], recv_out.at[chip], send.at[k], recv.at[k],
            device_id=(dest, core, ten), device_id_type=MESH)
        cp.start()
        copies.append(cp)
    loads = [pltpu.make_async_copy(src, dst, load_sem.at[i]) for i, (src, dst) in enumerate(
        ((rows_hbm, rows_ref), (w_hbm, w_ref), (wo_hbm, wo_ref), (gate_hbm, gate_ref),
         (up_hbm, up_ref)))]
    for ld in loads:
        ld.start()
    for ld in loads:
        ld.wait()

    def one_tile(i, carry):
        rows = pl.ds(pl.multiple_of(i * tile, tile), tile)
        acc = jnp.zeros((tile, gate_ref.shape[1]), jnp.float32)
        for r in range(w_ref.shape[0]):
            acc += jnp.dot(rows_ref[r, core, rows, :], w_ref[r],
                           preferred_element_type=jnp.float32)
            acc += jnp.dot(rows_ref[r, 1 - core, rows, :], wo_ref[r],
                           preferred_element_type=jnp.float32)
        gate_wide = gate_ref[rows, :].astype(jnp.float32)
        up_wide = up_ref[rows, :].astype(jnp.float32)
        sigmoid_gate = jax.nn.sigmoid(gate_wide)
        activated = gate_wide * sigmoid_gate
        gate_out[rows, :] = (
            acc * up_wide * sigmoid_gate * (1.0 + gate_wide * (1.0 - sigmoid_gate))
        ).astype(gate_out.dtype)
        up_out[rows, :] = (acc * activated).astype(up_out.dtype)
        return carry

    lax.fori_loop(0, gate_ref.shape[0] // tile, one_tile, 0)

    own.wait()
    for cp in copies:
        cp.wait_send()
        cp.wait_recv()


def _params(cid):
    return pltpu.CompilerParams(collective_id=cid, has_side_effects=True)


def body(out_grad, gate_act, up_act, w_down):
    seq_rows, ff = gate_act.shape
    width = w_down.shape[0]
    n_chip = lax.axis_size("chip")
    n_core = lax.axis_size("core")
    n_ten = lax.axis_size("tensor")
    core = lax.axis_index("core")
    grad_scale = 1.0 / math.sqrt(seq_rows * n_chip * n_core)
    gate_wide = gate_act.astype(jnp.float32)
    up_wide = up_act.astype(jnp.float32)
    sigmoid_gate = jax.nn.sigmoid(gate_wide)
    activated = gate_wide * sigmoid_gate
    hidden = (activated * up_wide).astype(jnp.bfloat16)

    n_lo = n_core
    n_plane = n_ten // n_lo
    vmem = pl.BlockSpec(memory_space=pltpu.VMEM)
    rows_g, w_own, w_other, partial = pl.pallas_call(
        lambda *refs: _gather_kernel(n_chip, n_lo, *refs),
        out_shape=(
            jax.ShapeDtypeStruct((n_plane, n_lo, seq_rows, out_grad.shape[1]), out_grad.dtype),
            jax.ShapeDtypeStruct((n_chip, width, ff), w_down.dtype),
            jax.ShapeDtypeStruct((n_chip, width, ff), w_down.dtype),
            jax.ShapeDtypeStruct((n_chip, width, ff), jnp.bfloat16),
        ),
        in_specs=[ANY, ANY, ANY],
        out_specs=(ANY, ANY, ANY, vmem),
        scratch_shapes=[pltpu.SemaphoreType.DMA((1,)), pltpu.SemaphoreType.DMA((1,)),
                        pltpu.SemaphoreType.DMA((n_plane // 2,)),
                        pltpu.SemaphoreType.DMA((n_plane // 2,)),
                        pltpu.SemaphoreType.DMA((n_plane // 2,)),
                        pltpu.SemaphoreType.DMA((n_plane // 2,)),
                        pltpu.SemaphoreType.DMA((n_chip,)), pltpu.SemaphoreType.DMA((n_chip,)),
                        pltpu.SemaphoreType.DMA((1,)), pltpu.SemaphoreType.DMA((1,)),
                        pltpu.SemaphoreType.DMA((n_chip,)), pltpu.SemaphoreType.DMA((n_chip,)),
                        pltpu.SemaphoreType.DMA((n_plane,)), pltpu.SemaphoreType.DMA((n_plane,)),
                        pltpu.SemaphoreType.DMA((2,)),
                        pltpu.VMEM((n_plane, seq_rows, out_grad.shape[1]), out_grad.dtype),
                        pltpu.VMEM((n_plane, seq_rows, out_grad.shape[1]), out_grad.dtype),
                        pltpu.VMEM(hidden.shape, hidden.dtype),
                        pltpu.VMEM(hidden.shape, hidden.dtype),
                        pltpu.SemaphoreType.DMA((n_plane + 1,))],
        compiler_params=_params(0),
    )(out_grad, w_down, hidden)

    received, gate_grad, up_grad = pl.pallas_call(
        lambda *refs: _scatter_kernel(n_chip, min(128, seq_rows), *refs),
        out_shape=(
            jax.ShapeDtypeStruct(partial.shape, jnp.bfloat16),
            jax.ShapeDtypeStruct(gate_act.shape, jnp.bfloat16),
            jax.ShapeDtypeStruct(up_act.shape, jnp.bfloat16),
        ),
        in_specs=[vmem, ANY, ANY, ANY, ANY, ANY],
        out_specs=(ANY, vmem, vmem),
        scratch_shapes=[pltpu.SemaphoreType.DMA((n_chip,)), pltpu.SemaphoreType.DMA((n_chip,)),
                        pltpu.SemaphoreType.DMA((1,)),
                        pltpu.VMEM(rows_g.shape, rows_g.dtype),
                        pltpu.VMEM(w_own.shape, w_own.dtype),
                        pltpu.VMEM(w_other.shape, w_other.dtype),
                        pltpu.VMEM(gate_act.shape, gate_act.dtype),
                        pltpu.VMEM(up_act.shape, up_act.dtype),
                        pltpu.SemaphoreType.DMA((5,))],
        compiler_params=_params(2),
    )(partial, rows_g, w_own, w_other, gate_act, up_act)
    summed = jnp.sum(received.astype(jnp.float32), axis=0)
    down_grad = (summed * grad_scale).astype(jnp.bfloat16)
    return (gate_grad, up_grad, down_grad)


def solution(mesh):
    n_dp = mesh.shape["dp"]
    n_tensor = mesh.shape["tensor"]
    devices = np.asarray(mesh.devices).reshape(n_dp // 2, 2, n_tensor)
    split = Mesh(devices, ("chip", "core", "tensor"))
    placed = P(("chip", "core"), "tensor")
    return jax.shard_map(
        body,
        mesh=split,
        in_specs=(placed, placed, placed, placed),
        out_specs=(placed, placed, placed),
        check_vma=False,
    )
```

```python
import math

import jax
import jax.numpy as jnp
import numpy as np
from jax import lax
from jax.experimental import pallas as pl
from jax.experimental.pallas import tpu as pltpu
from jax.sharding import Mesh
from jax.sharding import PartitionSpec as P

MESH = pl.DeviceIdType.MESH
ANY = pl.BlockSpec(memory_space=pl.ANY)


def _where():
    return lax.axis_index("chip"), lax.axis_index("core"), lax.axis_index("tensor")


def _fused_kernel(n_chip, n_lo, tile, grad_scale, og_ref, w_ref, hid_ref, gate_hbm, up_hbm,
                  gate_out, up_out, down_out, rows_out, w_out, w_other,
                  x_send, x_recv, r_send, r_recv, l_send, l_recv, w_send, w_recv,
                  f_send, f_recv, fw_send, fw_recv, fr_send, fr_recv, own_sem,
                  rows_v, ro_v, hid_v, ho_v, load_sem, part_v, recv_v, s_send, s_recv,
                  wv, wov, rows2_v, gate_v, up_v, late_sem):
    chip, core, ten = _where()
    n_plane = rows_out.shape[0]
    plane, lo = ten // n_lo, ten % n_lo
    right = ((plane + 1) % n_plane) * n_lo + lo
    left = ((plane + n_plane - 1) % n_plane) * n_lo + lo
    side = plane * n_lo + (1 - lo)
    other = (chip, 1 - core, ten)
    barrier = pltpu.get_barrier_semaphore()
    for t in (right, left, side):
        pl.semaphore_signal(barrier, inc=1, device_id=(chip, core, t), device_id_type=MESH)
    for k in range(1, n_chip):
        pl.semaphore_signal(barrier, inc=1, device_id=((chip + k) % n_chip, core, ten),
                            device_id_type=MESH)
    pl.semaphore_signal(barrier, inc=1, device_id=other, device_id_type=MESH)
    pl.semaphore_wait(barrier, 3 + (n_chip - 1) + 1)

    side_cp = pltpu.make_async_remote_copy(
        og_ref, rows_out.at[plane, lo], x_send.at[0], x_recv.at[0],
        device_id=(chip, core, side), device_id_type=MESH)
    side_cp.start()
    own_r = pltpu.make_async_copy(og_ref, rows_out.at[plane, lo], own_sem.at[0])
    own_w = pltpu.make_async_copy(w_ref, w_out.at[chip], own_sem.at[1])
    own_r.start()
    own_w.start()
    hid_cp = pltpu.make_async_remote_copy(hid_ref, ho_v, f_send.at[0], f_recv.at[0],
                                          device_id=other, device_id_type=MESH)
    hid_cp.start()
    hid_ld = pltpu.make_async_copy(hid_ref, hid_v, load_sem.at[n_plane])
    hid_ld.start()
    forwards = [hid_cp]
    outgoing = {}
    w_fwds = []
    rows_fwd = {}
    rows_ld = {}

    def fwd_w(k):
        r = (chip + n_chip - k) % n_chip
        src = w_ref if k == 0 else w_out.at[r]
        cp = pltpu.make_async_remote_copy(src, w_other.at[r], fw_send.at[k], fw_recv.at[k],
                                          device_id=other, device_id_type=MESH)
        cp.start()
        forwards.append(cp)
        w_fwds.append(cp)

    def arrived(d):
        p = (plane + d) % n_plane
        cp = pltpu.make_async_remote_copy(rows_out.at[p, 1 - core], ro_v.at[p],
                                          fr_send.at[d], fr_recv.at[d],
                                          device_id=other, device_id_type=MESH)
        cp.start()
        forwards.append(cp)
        rows_fwd[d] = cp
        ld = pltpu.make_async_copy(rows_out.at[p, core], rows_v.at[p], load_sem.at[d])
        ld.start()
        rows_ld[d] = ld

    def partial(d):
        p = (plane + d) % n_plane
        rows_ld[d].wait()
        rows_fwd[d].wait_recv()
        part = lax.dot_general(rows_v[p], hid_v[...], (((0,), (0,)), ((), ())),
                               preferred_element_type=jnp.float32)
        part += lax.dot_general(ro_v[p], ho_v[...], (((0,), (0,)), ((), ())),
                                preferred_element_type=jnp.float32)
        part_v[p] = part.astype(part_v.dtype)
        k = (p - chip + n_chip) % n_chip
        send = pltpu.make_async_remote_copy(
            part_v.at[p], recv_v.at[chip], s_send.at[d], s_recv.at[k],
            device_id=(p, core, ten), device_id_type=MESH)
        outgoing[d] = (p, send)

        @pl.when(p != chip)
        def _():
            send.start()

    fwd_w(0)
    own_r.wait()
    side_cp.wait_send()
    side_cp.wait_recv()
    arrived(0)

    n_steps = n_plane // 2
    ring = {}
    for s in range(n_steps):
        for d, sends, recvs, to, src_plane, half in (
            ("r", r_send, r_recv, right, (plane + n_plane - s) % n_plane, 0),
            ("l", l_send, l_recv, left, (plane + s) % n_plane, 1),
        ):
            block = rows_out.at[src_plane]
            if s == n_steps - 1:
                block = rows_out.at[src_plane, half]
            ring[(d, s)] = pltpu.make_async_remote_copy(
                block, block, sends.at[s], recvs.at[s],
                device_id=(chip, core, to), device_id_type=MESH)
    for d in ("r", "l"):
        ring[(d, 0)].start()
    w_copies = []
    for k in range(1, n_chip):
        cp = pltpu.make_async_remote_copy(
            w_ref, w_out.at[chip], w_send.at[k], w_recv.at[k],
            device_id=((chip + k) % n_chip, core, ten), device_id_type=MESH)
        cp.start()
        w_copies.append(cp)
    hid_ld.wait()
    hid_cp.wait_recv()
    pending = [0]
    for s in range(1, n_steps):
        for d in ("r", "l"):
            ring[(d, s - 1)].wait_recv()
            ring[(d, s)].start()
        arrived(n_plane - s)
        arrived(s)
        for d in pending:
            partial(d)
        pending = [n_plane - s, s]
    for d in ("r", "l"):
        ring[(d, n_steps - 1)].wait_recv()
        for s in range(n_steps):
            ring[(d, s)].wait_send()
    arrived(n_steps)
    for d in pending + [n_steps]:
        partial(d)

    for k in range(1, n_chip):
        w_copies[k - 1].wait_recv()
        fwd_w(k)
    own_w.wait()
    for cp in w_copies:
        cp.wait_send()
    for cp in forwards:
        cp.wait_send()
    for cp in w_fwds:
        cp.wait_recv()

    loads = [pltpu.make_async_copy(src, dst, late_sem.at[i]) for i, (src, dst) in enumerate(
        ((w_out, wv), (w_other, wov), (gate_hbm, gate_v), (up_hbm, up_v)))]
    loads += [pltpu.make_async_copy(rows_out.at[r, 1 - core], rows2_v.at[r],
                                    late_sem.at[4 + r]) for r in range(n_plane)]
    for ld in loads:
        ld.start()
    for ld in loads:
        ld.wait()

    def one_tile(i, carry):
        rows = pl.ds(pl.multiple_of(i * tile, tile), tile)
        acc = jnp.zeros((tile, gate_v.shape[1]), jnp.float32)
        for r in range(n_plane):
            acc += jnp.dot(rows_v[r, rows, :], wv[r], preferred_element_type=jnp.float32)
            acc += jnp.dot(rows2_v[r, rows, :], wov[r], preferred_element_type=jnp.float32)
        gate_wide = gate_v[rows, :].astype(jnp.float32)
        up_wide = up_v[rows, :].astype(jnp.float32)
        sigmoid_gate = jax.nn.sigmoid(gate_wide)
        activated = gate_wide * sigmoid_gate
        gate_out[rows, :] = (
            acc * up_wide * sigmoid_gate * (1.0 + gate_wide * (1.0 - sigmoid_gate))
        ).astype(gate_out.dtype)
        up_out[rows, :] = (acc * activated).astype(up_out.dtype)
        return carry

    lax.fori_loop(0, gate_v.shape[0] // tile, one_tile, 0)

    for d in range(n_plane):
        p, send = outgoing[d]

        @pl.when(p != chip)
        def _():
            send.wait_send()
            send.wait_recv()

    total = part_v[chip].astype(jnp.float32)
    for k in range(1, n_chip):
        total += recv_v[(chip + k) % n_chip].astype(jnp.float32)
    down_out[...] = (total * grad_scale).astype(down_out.dtype)


def body(out_grad, gate_act, up_act, w_down):
    seq_rows, ff = gate_act.shape
    width = w_down.shape[0]
    n_chip = lax.axis_size("chip")
    n_core = lax.axis_size("core")
    n_ten = lax.axis_size("tensor")
    core = lax.axis_index("core")
    grad_scale = 1.0 / math.sqrt(seq_rows * n_chip * n_core)
    gate_wide = gate_act.astype(jnp.float32)
    up_wide = up_act.astype(jnp.float32)
    sigmoid_gate = jax.nn.sigmoid(gate_wide)
    activated = gate_wide * sigmoid_gate
    hidden = (activated * up_wide).astype(jnp.bfloat16)

    n_lo = n_core
    n_plane = n_ten // n_lo
    vmem = pl.BlockSpec(memory_space=pltpu.VMEM)
    rows_shape = (n_plane, seq_rows, out_grad.shape[1])
    gate_grad, up_grad, down_grad, _, _, _ = pl.pallas_call(
        lambda *refs: _fused_kernel(n_chip, n_lo, min(128, seq_rows), grad_scale, *refs),
        out_shape=(
            jax.ShapeDtypeStruct(gate_act.shape, jnp.bfloat16),
            jax.ShapeDtypeStruct(up_act.shape, jnp.bfloat16),
            jax.ShapeDtypeStruct(w_down.shape, jnp.bfloat16),
            jax.ShapeDtypeStruct((n_plane, n_lo, seq_rows, out_grad.shape[1]), out_grad.dtype),
            jax.ShapeDtypeStruct((n_chip, width, ff), w_down.dtype),
            jax.ShapeDtypeStruct((n_chip, width, ff), w_down.dtype),
        ),
        in_specs=[ANY, ANY, ANY, ANY, ANY],
        out_specs=(vmem, vmem, vmem, ANY, ANY, ANY),
        scratch_shapes=[pltpu.SemaphoreType.DMA((1,)), pltpu.SemaphoreType.DMA((1,)),
                        pltpu.SemaphoreType.DMA((n_plane // 2,)),
                        pltpu.SemaphoreType.DMA((n_plane // 2,)),
                        pltpu.SemaphoreType.DMA((n_plane // 2,)),
                        pltpu.SemaphoreType.DMA((n_plane // 2,)),
                        pltpu.SemaphoreType.DMA((n_chip,)), pltpu.SemaphoreType.DMA((n_chip,)),
                        pltpu.SemaphoreType.DMA((1,)), pltpu.SemaphoreType.DMA((1,)),
                        pltpu.SemaphoreType.DMA((n_chip,)), pltpu.SemaphoreType.DMA((n_chip,)),
                        pltpu.SemaphoreType.DMA((n_plane,)), pltpu.SemaphoreType.DMA((n_plane,)),
                        pltpu.SemaphoreType.DMA((2,)),
                        pltpu.VMEM(rows_shape, out_grad.dtype),
                        pltpu.VMEM(rows_shape, out_grad.dtype),
                        pltpu.VMEM(hidden.shape, hidden.dtype),
                        pltpu.VMEM(hidden.shape, hidden.dtype),
                        pltpu.SemaphoreType.DMA((n_plane + 1,)),
                        pltpu.VMEM((n_chip, width, ff), jnp.bfloat16),
                        pltpu.VMEM((n_chip, width, ff), jnp.bfloat16),
                        pltpu.SemaphoreType.DMA((n_plane,)), pltpu.SemaphoreType.DMA((n_chip,)),
                        pltpu.VMEM((n_chip, width, ff), w_down.dtype),
                        pltpu.VMEM((n_chip, width, ff), w_down.dtype),
                        pltpu.VMEM(rows_shape, out_grad.dtype),
                        pltpu.VMEM(gate_act.shape, gate_act.dtype),
                        pltpu.VMEM(up_act.shape, up_act.dtype),
                        pltpu.SemaphoreType.DMA((4 + n_plane,))],
        compiler_params=pltpu.CompilerParams(collective_id=0, has_side_effects=True,
                                             vmem_limit_bytes=56 * 1024 * 1024),
    )(out_grad, w_down, hidden, gate_act, up_act)
    return (gate_grad, up_grad, down_grad)


def solution(mesh):
    n_dp = mesh.shape["dp"]
    n_tensor = mesh.shape["tensor"]
    devices = np.asarray(mesh.devices).reshape(n_dp // 2, 2, n_tensor)
    split = Mesh(devices, ("chip", "core", "tensor"))
    placed = P(("chip", "core"), "tensor")
    return jax.shard_map(
        body,
        mesh=split,
        in_specs=(placed, placed, placed, placed),
        out_specs=(placed, placed, placed),
        check_vma=False,
    )
```

```python
import math

import jax
import jax.numpy as jnp
import numpy as np
from jax import lax
from jax.experimental import pallas as pl
from jax.experimental.pallas import tpu as pltpu
from jax.sharding import Mesh
from jax.sharding import PartitionSpec as P

MESH = pl.DeviceIdType.MESH
ANY = pl.BlockSpec(memory_space=pl.ANY)


def _where():
    return lax.axis_index("chip"), lax.axis_index("core"), lax.axis_index("tensor")


def _fused_kernel(n_chip, n_lo, tile, grad_scale, og_ref, w_ref, hid_ref, gate_hbm, up_hbm,
                  gate_out, up_out, down_out, rows_out, w_out, w_other,
                  x_send, x_recv, r_send, r_recv, l_send, l_recv, w_send, w_recv,
                  f_send, f_recv, fw_send, fw_recv, fr_send, fr_recv, own_sem,
                  rows_v, ro_v, hid_v, ho_v, load_sem, part_v, recv_v, s_send, s_recv,
                  wv, wov, rows2_v, gate_v, up_v, late_sem):
    chip, core, ten = _where()
    n_plane = rows_out.shape[0]
    plane, lo = ten // n_lo, ten % n_lo
    right = ((plane + 1) % n_plane) * n_lo + lo
    left = ((plane + n_plane - 1) % n_plane) * n_lo + lo
    side = plane * n_lo + (1 - lo)
    other = (chip, 1 - core, ten)
    barrier = pltpu.get_barrier_semaphore()
    for t in (right, left, side):
        pl.semaphore_signal(barrier, inc=1, device_id=(chip, core, t), device_id_type=MESH)
    for k in range(1, n_chip):
        pl.semaphore_signal(barrier, inc=1, device_id=((chip + k) % n_chip, core, ten),
                            device_id_type=MESH)
    pl.semaphore_signal(barrier, inc=1, device_id=other, device_id_type=MESH)
    pl.semaphore_wait(barrier, 3 + (n_chip - 1) + 1)

    side_cp = pltpu.make_async_remote_copy(
        og_ref, rows_out.at[plane, lo], x_send.at[0], x_recv.at[0],
        device_id=(chip, core, side), device_id_type=MESH)
    side_cp.start()
    own_r = pltpu.make_async_copy(og_ref, rows_out.at[plane, lo], own_sem.at[0])
    own_w = pltpu.make_async_copy(w_ref, w_out.at[chip], own_sem.at[1])
    own_r.start()
    own_w.start()
    hid_cp = pltpu.make_async_remote_copy(hid_ref, ho_v, f_send.at[0], f_recv.at[0],
                                          device_id=other, device_id_type=MESH)
    hid_cp.start()
    hid_ld = pltpu.make_async_copy(hid_ref, hid_v, load_sem.at[n_plane])
    hid_ld.start()
    forwards = [hid_cp]
    outgoing = {}
    w_fwds = []
    rows_fwd = {}
    rows_ld = {}

    def fwd_w(k):
        r = (chip + n_chip - k) % n_chip
        src = w_ref if k == 0 else w_out.at[r]
        cp = pltpu.make_async_remote_copy(src, w_other.at[r], fw_send.at[k], fw_recv.at[k],
                                          device_id=other, device_id_type=MESH)
        cp.start()
        forwards.append(cp)
        w_fwds.append(cp)

    def arrived(d):
        p = (plane + d) % n_plane
        cp = pltpu.make_async_remote_copy(rows_out.at[p, 1 - core], ro_v.at[p],
                                          fr_send.at[d], fr_recv.at[d],
                                          device_id=other, device_id_type=MESH)
        cp.start()
        forwards.append(cp)
        rows_fwd[d] = cp
        ld = pltpu.make_async_copy(rows_out.at[p, core], rows_v.at[p], load_sem.at[d])
        ld.start()
        rows_ld[d] = ld

    def partial(d):
        p = (plane + d) % n_plane
        rows_ld[d].wait()
        rows_fwd[d].wait_recv()
        part = lax.dot_general(rows_v[p], hid_v[...], (((0,), (0,)), ((), ())),
                               preferred_element_type=jnp.float32)
        part += lax.dot_general(ro_v[p], ho_v[...], (((0,), (0,)), ((), ())),
                                preferred_element_type=jnp.float32)
        part_v[p] = part.astype(part_v.dtype)
        k = (p - chip + n_chip) % n_chip
        send = pltpu.make_async_remote_copy(
            part_v.at[p], recv_v.at[chip], s_send.at[d], s_recv.at[k],
            device_id=(p, core, ten), device_id_type=MESH)
        outgoing[d] = (p, send)

    fwd_w(0)
    own_r.wait()
    side_cp.wait_send()
    side_cp.wait_recv()
    arrived(0)

    n_steps = n_plane // 2
    ring = {}
    for s in range(n_steps):
        for d, sends, recvs, to, src_plane, half in (
            ("r", r_send, r_recv, right, (plane + n_plane - s) % n_plane, 0),
            ("l", l_send, l_recv, left, (plane + s) % n_plane, 1),
        ):
            block = rows_out.at[src_plane]
            if s == n_steps - 1:
                block = rows_out.at[src_plane, half]
            ring[(d, s)] = pltpu.make_async_remote_copy(
                block, block, sends.at[s], recvs.at[s],
                device_id=(chip, core, to), device_id_type=MESH)
    for d in ("r", "l"):
        ring[(d, 0)].start()
    w_copies = []
    for k in range(1, n_chip):
        cp = pltpu.make_async_remote_copy(
            w_ref, w_out.at[chip], w_send.at[k], w_recv.at[k],
            device_id=((chip + k) % n_chip, core, ten), device_id_type=MESH)
        cp.start()
        w_copies.append(cp)
    hid_ld.wait()
    hid_cp.wait_recv()
    pending = [0]
    for s in range(1, n_steps):
        for d in ("r", "l"):
            ring[(d, s - 1)].wait_recv()
            ring[(d, s)].start()
        arrived(n_plane - s)
        arrived(s)
        for d in pending:
            partial(d)
        pending = [n_plane - s, s]
    for d in ("r", "l"):
        ring[(d, n_steps - 1)].wait_recv()
        for s in range(n_steps):
            ring[(d, s)].wait_send()
    arrived(n_steps)
    for d in pending + [n_steps]:
        partial(d)

    for k in range(1, n_chip):
        w_copies[k - 1].wait_recv()
        fwd_w(k)
    for d in range(n_plane):
        p, send = outgoing[d]

        @pl.when(p != chip)
        def _():
            send.start()

    own_w.wait()
    for cp in w_copies:
        cp.wait_send()
    for cp in forwards:
        cp.wait_send()
    for cp in w_fwds:
        cp.wait_recv()

    loads = [pltpu.make_async_copy(src, dst, late_sem.at[i]) for i, (src, dst) in enumerate(
        ((w_out, wv), (w_other, wov), (gate_hbm, gate_v), (up_hbm, up_v)))]
    loads += [pltpu.make_async_copy(rows_out.at[r, 1 - core], rows2_v.at[r],
                                    late_sem.at[4 + r]) for r in range(n_plane)]
    for ld in loads:
        ld.start()
    for ld in loads:
        ld.wait()

    def one_tile(i, carry):
        rows = pl.ds(pl.multiple_of(i * tile, tile), tile)
        acc = jnp.zeros((tile, gate_v.shape[1]), jnp.float32)
        for r in range(n_plane):
            acc += jnp.dot(rows_v[r, rows, :], wv[r], preferred_element_type=jnp.float32)
            acc += jnp.dot(rows2_v[r, rows, :], wov[r], preferred_element_type=jnp.float32)
        gate_wide = gate_v[rows, :].astype(jnp.float32)
        up_wide = up_v[rows, :].astype(jnp.float32)
        sigmoid_gate = jax.nn.sigmoid(gate_wide)
        activated = gate_wide * sigmoid_gate
        gate_out[rows, :] = (
            acc * up_wide * sigmoid_gate * (1.0 + gate_wide * (1.0 - sigmoid_gate))
        ).astype(gate_out.dtype)
        up_out[rows, :] = (acc * activated).astype(up_out.dtype)
        return carry

    lax.fori_loop(0, gate_v.shape[0] // tile, one_tile, 0)

    for d in range(n_plane):
        p, send = outgoing[d]

        @pl.when(p != chip)
        def _():
            send.wait_send()
            send.wait_recv()

    total = part_v[chip].astype(jnp.float32)
    for k in range(1, n_chip):
        total += recv_v[(chip + k) % n_chip].astype(jnp.float32)
    down_out[...] = (total * grad_scale).astype(down_out.dtype)


def body(out_grad, gate_act, up_act, w_down):
    seq_rows, ff = gate_act.shape
    width = w_down.shape[0]
    n_chip = lax.axis_size("chip")
    n_core = lax.axis_size("core")
    n_ten = lax.axis_size("tensor")
    core = lax.axis_index("core")
    grad_scale = 1.0 / math.sqrt(seq_rows * n_chip * n_core)
    gate_wide = gate_act.astype(jnp.float32)
    up_wide = up_act.astype(jnp.float32)
    sigmoid_gate = jax.nn.sigmoid(gate_wide)
    activated = gate_wide * sigmoid_gate
    hidden = (activated * up_wide).astype(jnp.bfloat16)

    n_lo = n_core
    n_plane = n_ten // n_lo
    vmem = pl.BlockSpec(memory_space=pltpu.VMEM)
    rows_shape = (n_plane, seq_rows, out_grad.shape[1])
    gate_grad, up_grad, down_grad, _, _, _ = pl.pallas_call(
        lambda *refs: _fused_kernel(n_chip, n_lo, min(128, seq_rows), grad_scale, *refs),
        out_shape=(
            jax.ShapeDtypeStruct(gate_act.shape, jnp.bfloat16),
            jax.ShapeDtypeStruct(up_act.shape, jnp.bfloat16),
            jax.ShapeDtypeStruct(w_down.shape, jnp.bfloat16),
            jax.ShapeDtypeStruct((n_plane, n_lo, seq_rows, out_grad.shape[1]), out_grad.dtype),
            jax.ShapeDtypeStruct((n_chip, width, ff), w_down.dtype),
            jax.ShapeDtypeStruct((n_chip, width, ff), w_down.dtype),
        ),
        in_specs=[ANY, ANY, ANY, ANY, ANY],
        out_specs=(vmem, vmem, vmem, ANY, ANY, ANY),
        scratch_shapes=[pltpu.SemaphoreType.DMA((1,)), pltpu.SemaphoreType.DMA((1,)),
                        pltpu.SemaphoreType.DMA((n_plane // 2,)),
                        pltpu.SemaphoreType.DMA((n_plane // 2,)),
                        pltpu.SemaphoreType.DMA((n_plane // 2,)),
                        pltpu.SemaphoreType.DMA((n_plane // 2,)),
                        pltpu.SemaphoreType.DMA((n_chip,)), pltpu.SemaphoreType.DMA((n_chip,)),
                        pltpu.SemaphoreType.DMA((1,)), pltpu.SemaphoreType.DMA((1,)),
                        pltpu.SemaphoreType.DMA((n_chip,)), pltpu.SemaphoreType.DMA((n_chip,)),
                        pltpu.SemaphoreType.DMA((n_plane,)), pltpu.SemaphoreType.DMA((n_plane,)),
                        pltpu.SemaphoreType.DMA((2,)),
                        pltpu.VMEM(rows_shape, out_grad.dtype),
                        pltpu.VMEM(rows_shape, out_grad.dtype),
                        pltpu.VMEM(hidden.shape, hidden.dtype),
                        pltpu.VMEM(hidden.shape, hidden.dtype),
                        pltpu.SemaphoreType.DMA((n_plane + 1,)),
                        pltpu.VMEM((n_chip, width, ff), jnp.bfloat16),
                        pltpu.VMEM((n_chip, width, ff), jnp.bfloat16),
                        pltpu.SemaphoreType.DMA((n_plane,)), pltpu.SemaphoreType.DMA((n_chip,)),
                        pltpu.VMEM((n_chip, width, ff), w_down.dtype),
                        pltpu.VMEM((n_chip, width, ff), w_down.dtype),
                        pltpu.VMEM(rows_shape, out_grad.dtype),
                        pltpu.VMEM(gate_act.shape, gate_act.dtype),
                        pltpu.VMEM(up_act.shape, up_act.dtype),
                        pltpu.SemaphoreType.DMA((4 + n_plane,))],
        compiler_params=pltpu.CompilerParams(collective_id=0, has_side_effects=True,
                                             vmem_limit_bytes=56 * 1024 * 1024),
    )(out_grad, w_down, hidden, gate_act, up_act)
    return (gate_grad, up_grad, down_grad)


def solution(mesh):
    n_dp = mesh.shape["dp"]
    n_tensor = mesh.shape["tensor"]
    devices = np.asarray(mesh.devices).reshape(n_dp // 2, 2, n_tensor)
    split = Mesh(devices, ("chip", "core", "tensor"))
    placed = P(("chip", "core"), "tensor")
    return jax.shard_map(
        body,
        mesh=split,
        in_specs=(placed, placed, placed, placed),
        out_specs=(placed, placed, placed),
        check_vma=False,
    )
```

```python
import math

import jax
import jax.numpy as jnp
import numpy as np
from jax import lax
from jax.experimental import pallas as pl
from jax.experimental.pallas import tpu as pltpu
from jax.sharding import Mesh
from jax.sharding import PartitionSpec as P

MESH = pl.DeviceIdType.MESH
ANY = pl.BlockSpec(memory_space=pl.ANY)


def _where():
    return lax.axis_index("chip"), lax.axis_index("core"), lax.axis_index("tensor")


def _fused_kernel(n_chip, n_lo, tile, grad_scale, og_ref, w_ref, hid_ref, gate_hbm, up_hbm,
                  gate_out, up_out, down_out, rows_out, w_out, w_other,
                  x_send, x_recv, r_send, r_recv, l_send, l_recv, w_send, w_recv,
                  f_send, f_recv, fw_send, fw_recv, fr_send, fr_recv, own_sem,
                  rows_v, ro_v, hid_v, ho_v, load_sem, part_v, recv_own, recv_agg, recv_x,
                  agg_v, s_send, s_recv, x2_send, x2_recv,
                  wv, wov, rows2_v, gate_v, up_v, late_sem):
    chip, core, ten = _where()
    n_plane = rows_out.shape[0]
    plane, lo = ten // n_lo, ten % n_lo
    right = ((plane + 1) % n_plane) * n_lo + lo
    left = ((plane + n_plane - 1) % n_plane) * n_lo + lo
    side = plane * n_lo + (1 - lo)
    other = (chip, 1 - core, ten)
    barrier = pltpu.get_barrier_semaphore()
    for t in (right, left, side):
        pl.semaphore_signal(barrier, inc=1, device_id=(chip, core, t), device_id_type=MESH)
    for k in range(1, n_chip):
        pl.semaphore_signal(barrier, inc=1, device_id=((chip + k) % n_chip, core, ten),
                            device_id_type=MESH)
    pl.semaphore_signal(barrier, inc=1, device_id=other, device_id_type=MESH)
    pl.semaphore_wait(barrier, 3 + (n_chip - 1) + 1)

    side_cp = pltpu.make_async_remote_copy(
        og_ref, rows_out.at[plane, lo], x_send.at[0], x_recv.at[0],
        device_id=(chip, core, side), device_id_type=MESH)
    side_cp.start()
    own_r = pltpu.make_async_copy(og_ref, rows_out.at[plane, lo], own_sem.at[0])
    own_w = pltpu.make_async_copy(w_ref, w_out.at[chip], own_sem.at[1])
    own_r.start()
    own_w.start()
    hid_cp = pltpu.make_async_remote_copy(hid_ref, ho_v, f_send.at[0], f_recv.at[0],
                                          device_id=other, device_id_type=MESH)
    hid_cp.start()
    hid_ld = pltpu.make_async_copy(hid_ref, hid_v, load_sem.at[n_plane])
    hid_ld.start()
    forwards = [hid_cp]
    w_fwds = []
    rows_fwd = {}
    rows_ld = {}

    def fwd_w(k):
        r = (chip + n_chip - k) % n_chip
        src = w_ref if k == 0 else w_out.at[r]
        cp = pltpu.make_async_remote_copy(src, w_other.at[r], fw_send.at[k], fw_recv.at[k],
                                          device_id=other, device_id_type=MESH)
        cp.start()
        forwards.append(cp)
        w_fwds.append(cp)

    def arrived(d):
        p = (plane + d) % n_plane
        cp = pltpu.make_async_remote_copy(rows_out.at[p, 1 - core], ro_v.at[p],
                                          fr_send.at[d], fr_recv.at[d],
                                          device_id=other, device_id_type=MESH)
        cp.start()
        forwards.append(cp)
        rows_fwd[d] = cp
        ld = pltpu.make_async_copy(rows_out.at[p, core], rows_v.at[p], load_sem.at[d])
        ld.start()
        rows_ld[d] = ld

    def partial(d):
        p = (plane + d) % n_plane
        rows_ld[d].wait()
        rows_fwd[d].wait_recv()
        part = lax.dot_general(rows_v[p], hid_v[...], (((0,), (0,)), ((), ())),
                               preferred_element_type=jnp.float32)
        part += lax.dot_general(ro_v[p], ho_v[...], (((0,), (0,)), ((), ())),
                                preferred_element_type=jnp.float32)
        part_v[p] = part.astype(part_v.dtype)

    fwd_w(0)
    own_r.wait()
    side_cp.wait_send()
    side_cp.wait_recv()
    arrived(0)

    n_steps = n_plane // 2
    ring = {}
    for s in range(n_steps):
        for d, sends, recvs, to, src_plane, half in (
            ("r", r_send, r_recv, right, (plane + n_plane - s) % n_plane, 0),
            ("l", l_send, l_recv, left, (plane + s) % n_plane, 1),
        ):
            block = rows_out.at[src_plane]
            if s == n_steps - 1:
                block = rows_out.at[src_plane, half]
            ring[(d, s)] = pltpu.make_async_remote_copy(
                block, block, sends.at[s], recvs.at[s],
                device_id=(chip, core, to), device_id_type=MESH)
    for d in ("r", "l"):
        ring[(d, 0)].start()
    w_copies = []
    for k in range(1, n_chip):
        cp = pltpu.make_async_remote_copy(
            w_ref, w_out.at[chip], w_send.at[k], w_recv.at[k],
            device_id=((chip + k) % n_chip, core, ten), device_id_type=MESH)
        cp.start()
        w_copies.append(cp)
    hid_ld.wait()
    hid_cp.wait_recv()
    pending = [0]
    for s in range(1, n_steps):
        for d in ("r", "l"):
            ring[(d, s - 1)].wait_recv()
            ring[(d, s)].start()
        arrived(n_plane - s)
        arrived(s)
        for d in pending:
            partial(d)
        pending = [n_plane - s, s]
    for d in ("r", "l"):
        ring[(d, n_steps - 1)].wait_recv()
        for s in range(n_steps):
            ring[(d, s)].wait_send()
    arrived(n_steps)
    for d in pending + [n_steps]:
        partial(d)

    for k in range(1, n_chip):
        w_copies[k - 1].wait_recv()
        fwd_w(k)
    n_y = n_chip // 2
    half, y = chip // n_y, chip % n_y
    across = (1 - half) * n_y + y
    stage = []
    for ky in range(1, n_y):
        to_y = (y + ky) % n_y
        for kind, (block, slot) in enumerate(((half * n_y + to_y, recv_own),
                                              ((1 - half) * n_y + to_y, recv_agg))):
            cp = pltpu.make_async_remote_copy(
                part_v.at[block], slot.at[y], s_send.at[2 * ky + kind],
                s_recv.at[2 * ky + kind],
                device_id=(half * n_y + to_y, core, ten), device_id_type=MESH)
            cp.start()
            stage.append((kind, cp))
    agg = part_v[across].astype(jnp.float32)
    for kind, cp in stage:
        if kind == 1:
            cp.wait_recv()
    for ky in range(1, n_y):
        agg += recv_agg[(y + n_y - ky) % n_y].astype(jnp.float32)
    agg_v[...] = agg
    cross = pltpu.make_async_remote_copy(agg_v, recv_x, x2_send.at[0], x2_recv.at[0],
                                         device_id=(across, core, ten), device_id_type=MESH)
    cross.start()

    own_w.wait()
    for cp in w_copies:
        cp.wait_send()
    for cp in forwards:
        cp.wait_send()
    for cp in w_fwds:
        cp.wait_recv()

    loads = [pltpu.make_async_copy(src, dst, late_sem.at[i]) for i, (src, dst) in enumerate(
        ((w_out, wv), (w_other, wov), (gate_hbm, gate_v), (up_hbm, up_v)))]
    loads += [pltpu.make_async_copy(rows_out.at[r, 1 - core], rows2_v.at[r],
                                    late_sem.at[4 + r]) for r in range(n_plane)]
    for ld in loads:
        ld.start()
    for ld in loads:
        ld.wait()

    def one_tile(i, carry):
        rows = pl.ds(pl.multiple_of(i * tile, tile), tile)
        acc = jnp.zeros((tile, gate_v.shape[1]), jnp.float32)
        for r in range(n_plane):
            acc += jnp.dot(rows_v[r, rows, :], wv[r], preferred_element_type=jnp.float32)
            acc += jnp.dot(rows2_v[r, rows, :], wov[r], preferred_element_type=jnp.float32)
        gate_wide = gate_v[rows, :].astype(jnp.float32)
        up_wide = up_v[rows, :].astype(jnp.float32)
        sigmoid_gate = jax.nn.sigmoid(gate_wide)
        activated = gate_wide * sigmoid_gate
        gate_out[rows, :] = (
            acc * up_wide * sigmoid_gate * (1.0 + gate_wide * (1.0 - sigmoid_gate))
        ).astype(gate_out.dtype)
        up_out[rows, :] = (acc * activated).astype(up_out.dtype)
        return carry

    lax.fori_loop(0, gate_v.shape[0] // tile, one_tile, 0)

    for kind, cp in stage:
        cp.wait_send()
        if kind == 0:
            cp.wait_recv()
    cross.wait_send()
    cross.wait_recv()
    total = part_v[chip].astype(jnp.float32) + recv_x[...]
    for ky in range(1, n_y):
        total += recv_own[(y + n_y - ky) % n_y].astype(jnp.float32)
    down_out[...] = (total * grad_scale).astype(down_out.dtype)


def body(out_grad, gate_act, up_act, w_down):
    seq_rows, ff = gate_act.shape
    width = w_down.shape[0]
    n_chip = lax.axis_size("chip")
    n_core = lax.axis_size("core")
    n_ten = lax.axis_size("tensor")
    core = lax.axis_index("core")
    grad_scale = 1.0 / math.sqrt(seq_rows * n_chip * n_core)
    gate_wide = gate_act.astype(jnp.float32)
    up_wide = up_act.astype(jnp.float32)
    sigmoid_gate = jax.nn.sigmoid(gate_wide)
    activated = gate_wide * sigmoid_gate
    hidden = (activated * up_wide).astype(jnp.bfloat16)

    n_lo = n_core
    n_plane = n_ten // n_lo
    vmem = pl.BlockSpec(memory_space=pltpu.VMEM)
    rows_shape = (n_plane, seq_rows, out_grad.shape[1])
    gate_grad, up_grad, down_grad, _, _, _ = pl.pallas_call(
        lambda *refs: _fused_kernel(n_chip, n_lo, min(128, seq_rows), grad_scale, *refs),
        out_shape=(
            jax.ShapeDtypeStruct(gate_act.shape, jnp.bfloat16),
            jax.ShapeDtypeStruct(up_act.shape, jnp.bfloat16),
            jax.ShapeDtypeStruct(w_down.shape, jnp.bfloat16),
            jax.ShapeDtypeStruct((n_plane, n_lo, seq_rows, out_grad.shape[1]), out_grad.dtype),
            jax.ShapeDtypeStruct((n_chip, width, ff), w_down.dtype),
            jax.ShapeDtypeStruct((n_chip, width, ff), w_down.dtype),
        ),
        in_specs=[ANY, ANY, ANY, ANY, ANY],
        out_specs=(vmem, vmem, vmem, ANY, ANY, ANY),
        scratch_shapes=[pltpu.SemaphoreType.DMA((1,)), pltpu.SemaphoreType.DMA((1,)),
                        pltpu.SemaphoreType.DMA((n_plane // 2,)),
                        pltpu.SemaphoreType.DMA((n_plane // 2,)),
                        pltpu.SemaphoreType.DMA((n_plane // 2,)),
                        pltpu.SemaphoreType.DMA((n_plane // 2,)),
                        pltpu.SemaphoreType.DMA((n_chip,)), pltpu.SemaphoreType.DMA((n_chip,)),
                        pltpu.SemaphoreType.DMA((1,)), pltpu.SemaphoreType.DMA((1,)),
                        pltpu.SemaphoreType.DMA((n_chip,)), pltpu.SemaphoreType.DMA((n_chip,)),
                        pltpu.SemaphoreType.DMA((n_plane,)), pltpu.SemaphoreType.DMA((n_plane,)),
                        pltpu.SemaphoreType.DMA((2,)),
                        pltpu.VMEM(rows_shape, out_grad.dtype),
                        pltpu.VMEM(rows_shape, out_grad.dtype),
                        pltpu.VMEM(hidden.shape, hidden.dtype),
                        pltpu.VMEM(hidden.shape, hidden.dtype),
                        pltpu.SemaphoreType.DMA((n_plane + 1,)),
                        pltpu.VMEM((n_chip, width, ff), jnp.bfloat16),
                        pltpu.VMEM((n_chip // 2, width, ff), jnp.bfloat16),
                        pltpu.VMEM((n_chip // 2, width, ff), jnp.bfloat16),
                        pltpu.VMEM((width, ff), jnp.float32),
                        pltpu.VMEM((width, ff), jnp.float32),
                        pltpu.SemaphoreType.DMA((n_chip,)), pltpu.SemaphoreType.DMA((n_chip,)),
                        pltpu.SemaphoreType.DMA((1,)), pltpu.SemaphoreType.DMA((1,)),
                        pltpu.VMEM((n_chip, width, ff), w_down.dtype),
                        pltpu.VMEM((n_chip, width, ff), w_down.dtype),
                        pltpu.VMEM(rows_shape, out_grad.dtype),
                        pltpu.VMEM(gate_act.shape, gate_act.dtype),
                        pltpu.VMEM(up_act.shape, up_act.dtype),
                        pltpu.SemaphoreType.DMA((4 + n_plane,))],
        compiler_params=pltpu.CompilerParams(collective_id=0, has_side_effects=True,
                                             vmem_limit_bytes=56 * 1024 * 1024),
    )(out_grad, w_down, hidden, gate_act, up_act)
    return (gate_grad, up_grad, down_grad)


def solution(mesh):
    n_dp = mesh.shape["dp"]
    n_tensor = mesh.shape["tensor"]
    devices = np.asarray(mesh.devices).reshape(n_dp // 2, 2, n_tensor)
    split = Mesh(devices, ("chip", "core", "tensor"))
    placed = P(("chip", "core"), "tensor")
    return jax.shard_map(
        body,
        mesh=split,
        in_specs=(placed, placed, placed, placed),
        out_specs=(placed, placed, placed),
        check_vma=False,
    )
```

```python
import math

import jax
import jax.numpy as jnp
import numpy as np
from jax import lax
from jax.experimental import pallas as pl
from jax.experimental.pallas import tpu as pltpu
from jax.sharding import Mesh
from jax.sharding import PartitionSpec as P

MESH = pl.DeviceIdType.MESH
ANY = pl.BlockSpec(memory_space=pl.ANY)


def _where():
    return lax.axis_index("chip"), lax.axis_index("core"), lax.axis_index("tensor")


def _fused_kernel(n_chip, n_lo, tile, grad_scale, og_ref, w_ref, gate_hbm, up_hbm,
                  gate_out, up_out, down_out, rows_out, w_out, w_other,
                  x_send, x_recv, r_send, r_recv, l_send, l_recv, w_send, w_recv,
                  f_send, f_recv, fw_send, fw_recv, fr_send, fr_recv, own_sem,
                  rows_v, ro_v, hid_v, ho_v, load_sem, part_v, recv_v, s_send, s_recv,
                  wv, wov, rows2_v, gate_v, up_v, late_sem):
    chip, core, ten = _where()
    n_plane = rows_out.shape[0]
    plane, lo = ten // n_lo, ten % n_lo
    right = ((plane + 1) % n_plane) * n_lo + lo
    left = ((plane + n_plane - 1) % n_plane) * n_lo + lo
    side = plane * n_lo + (1 - lo)
    other = (chip, 1 - core, ten)
    barrier = pltpu.get_barrier_semaphore()
    for t in (right, left, side):
        pl.semaphore_signal(barrier, inc=1, device_id=(chip, core, t), device_id_type=MESH)
    for k in range(1, n_chip):
        pl.semaphore_signal(barrier, inc=1, device_id=((chip + k) % n_chip, core, ten),
                            device_id_type=MESH)
    pl.semaphore_signal(barrier, inc=1, device_id=other, device_id_type=MESH)
    pl.semaphore_wait(barrier, 3 + (n_chip - 1) + 1)

    side_cp = pltpu.make_async_remote_copy(
        og_ref, rows_out.at[plane, lo], x_send.at[0], x_recv.at[0],
        device_id=(chip, core, side), device_id_type=MESH)
    side_cp.start()
    own_r = pltpu.make_async_copy(og_ref, rows_out.at[plane, lo], own_sem.at[0])
    own_w = pltpu.make_async_copy(w_ref, w_out.at[chip], own_sem.at[1])
    own_r.start()
    own_w.start()
    act_ld = [pltpu.make_async_copy(gate_hbm, gate_v, late_sem.at[2]),
              pltpu.make_async_copy(up_hbm, up_v, late_sem.at[3])]
    for ld in act_ld:
        ld.start()
    hid_cp = pltpu.make_async_remote_copy(hid_v, ho_v, f_send.at[0], f_recv.at[0],
                                          device_id=other, device_id_type=MESH)
    forwards = [hid_cp]
    outgoing = {}
    w_fwds = []
    rows_fwd = {}
    rows_ld = {}

    def fwd_w(k):
        r = (chip + n_chip - k) % n_chip
        src = w_ref if k == 0 else w_out.at[r]
        cp = pltpu.make_async_remote_copy(src, w_other.at[r], fw_send.at[k], fw_recv.at[k],
                                          device_id=other, device_id_type=MESH)
        cp.start()
        forwards.append(cp)
        w_fwds.append(cp)

    def arrived(d):
        p = (plane + d) % n_plane
        cp = pltpu.make_async_remote_copy(rows_out.at[p, 1 - core], ro_v.at[p],
                                          fr_send.at[d], fr_recv.at[d],
                                          device_id=other, device_id_type=MESH)
        cp.start()
        forwards.append(cp)
        rows_fwd[d] = cp
        ld = pltpu.make_async_copy(rows_out.at[p, core], rows_v.at[p], load_sem.at[d])
        ld.start()
        rows_ld[d] = ld

    def partial(d):
        p = (plane + d) % n_plane
        rows_ld[d].wait()
        rows_fwd[d].wait_recv()
        part = lax.dot_general(rows_v[p], hid_v[...], (((0,), (0,)), ((), ())),
                               preferred_element_type=jnp.float32)
        part += lax.dot_general(ro_v[p], ho_v[...], (((0,), (0,)), ((), ())),
                                preferred_element_type=jnp.float32)
        part_v[p] = part.astype(part_v.dtype)
        k = (p - chip + n_chip) % n_chip
        send = pltpu.make_async_remote_copy(
            part_v.at[p], recv_v.at[chip], s_send.at[d], s_recv.at[k],
            device_id=(p, core, ten), device_id_type=MESH)
        outgoing[d] = (p, send)

    fwd_w(0)
    own_r.wait()
    side_cp.wait_send()
    side_cp.wait_recv()
    arrived(0)

    n_steps = n_plane // 2
    ring = {}
    for s in range(n_steps):
        for d, sends, recvs, to, src_plane, half in (
            ("r", r_send, r_recv, right, (plane + n_plane - s) % n_plane, 0),
            ("l", l_send, l_recv, left, (plane + s) % n_plane, 1),
        ):
            block = rows_out.at[src_plane]
            if s == n_steps - 1:
                block = rows_out.at[src_plane, half]
            ring[(d, s)] = pltpu.make_async_remote_copy(
                block, block, sends.at[s], recvs.at[s],
                device_id=(chip, core, to), device_id_type=MESH)
    for d in ("r", "l"):
        ring[(d, 0)].start()
    w_copies = []
    for k in range(1, n_chip):
        cp = pltpu.make_async_remote_copy(
            w_ref, w_out.at[chip], w_send.at[k], w_recv.at[k],
            device_id=((chip + k) % n_chip, core, ten), device_id_type=MESH)
        cp.start()
        w_copies.append(cp)
    for ld in act_ld:
        ld.wait()
    gate_wide = gate_v[...].astype(jnp.float32)
    sigmoid_gate = jax.nn.sigmoid(gate_wide)
    hid_v[...] = (gate_wide * sigmoid_gate * up_v[...].astype(jnp.float32)).astype(hid_v.dtype)
    hid_cp.start()
    hid_cp.wait_recv()
    pending = [0]
    for s in range(1, n_steps):
        for d in ("r", "l"):
            ring[(d, s - 1)].wait_recv()
            ring[(d, s)].start()
        arrived(n_plane - s)
        arrived(s)
        for d in pending:
            partial(d)
        pending = [n_plane - s, s]
    for d in ("r", "l"):
        ring[(d, n_steps - 1)].wait_recv()
        for s in range(n_steps):
            ring[(d, s)].wait_send()
    arrived(n_steps)
    for d in pending + [n_steps]:
        partial(d)

    for k in range(1, n_chip):
        w_copies[k - 1].wait_recv()
        fwd_w(k)
    for d in range(n_plane):
        p, send = outgoing[d]

        @pl.when(p != chip)
        def _():
            send.start()

    own_w.wait()
    for cp in w_copies:
        cp.wait_send()
    for cp in forwards:
        cp.wait_send()
    for cp in w_fwds:
        cp.wait_recv()

    loads = [pltpu.make_async_copy(src, dst, late_sem.at[i]) for i, (src, dst) in enumerate(
        ((w_out, wv), (w_other, wov)))]
    loads += [pltpu.make_async_copy(rows_out.at[r, 1 - core], rows2_v.at[r],
                                    late_sem.at[4 + r]) for r in range(n_plane)]
    for ld in loads:
        ld.start()
    for ld in loads:
        ld.wait()

    def one_tile(i, carry):
        rows = pl.ds(pl.multiple_of(i * tile, tile), tile)
        acc = jnp.zeros((tile, gate_v.shape[1]), jnp.float32)
        for r in range(n_plane):
            acc += jnp.dot(rows_v[r, rows, :], wv[r], preferred_element_type=jnp.float32)
            acc += jnp.dot(rows2_v[r, rows, :], wov[r], preferred_element_type=jnp.float32)
        gate_wide = gate_v[rows, :].astype(jnp.float32)
        up_wide = up_v[rows, :].astype(jnp.float32)
        sigmoid_gate = jax.nn.sigmoid(gate_wide)
        activated = gate_wide * sigmoid_gate
        gate_out[rows, :] = (
            acc * up_wide * sigmoid_gate * (1.0 + gate_wide * (1.0 - sigmoid_gate))
        ).astype(gate_out.dtype)
        up_out[rows, :] = (acc * activated).astype(up_out.dtype)
        return carry

    lax.fori_loop(0, gate_v.shape[0] // tile, one_tile, 0)

    for d in range(n_plane):
        p, send = outgoing[d]

        @pl.when(p != chip)
        def _():
            send.wait_send()
            send.wait_recv()

    total = part_v[chip].astype(jnp.float32)
    for k in range(1, n_chip):
        total += recv_v[(chip + k) % n_chip].astype(jnp.float32)
    down_out[...] = (total * grad_scale).astype(down_out.dtype)


def body(out_grad, gate_act, up_act, w_down):
    seq_rows, ff = gate_act.shape
    width = w_down.shape[0]
    n_chip = lax.axis_size("chip")
    n_core = lax.axis_size("core")
    n_ten = lax.axis_size("tensor")
    core = lax.axis_index("core")
    grad_scale = 1.0 / math.sqrt(seq_rows * n_chip * n_core)
    hidden = jax.ShapeDtypeStruct(gate_act.shape, jnp.bfloat16)

    n_lo = n_core
    n_plane = n_ten // n_lo
    vmem = pl.BlockSpec(memory_space=pltpu.VMEM)
    rows_shape = (n_plane, seq_rows, out_grad.shape[1])
    gate_grad, up_grad, down_grad, _, _, _ = pl.pallas_call(
        lambda *refs: _fused_kernel(n_chip, n_lo, min(128, seq_rows), grad_scale, *refs),
        out_shape=(
            jax.ShapeDtypeStruct(gate_act.shape, jnp.bfloat16),
            jax.ShapeDtypeStruct(up_act.shape, jnp.bfloat16),
            jax.ShapeDtypeStruct(w_down.shape, jnp.bfloat16),
            jax.ShapeDtypeStruct((n_plane, n_lo, seq_rows, out_grad.shape[1]), out_grad.dtype),
            jax.ShapeDtypeStruct((n_chip, width, ff), w_down.dtype),
            jax.ShapeDtypeStruct((n_chip, width, ff), w_down.dtype),
        ),
        in_specs=[ANY, ANY, ANY, ANY],
        out_specs=(vmem, vmem, vmem, ANY, ANY, ANY),
        scratch_shapes=[pltpu.SemaphoreType.DMA((1,)), pltpu.SemaphoreType.DMA((1,)),
                        pltpu.SemaphoreType.DMA((n_plane // 2,)),
                        pltpu.SemaphoreType.DMA((n_plane // 2,)),
                        pltpu.SemaphoreType.DMA((n_plane // 2,)),
                        pltpu.SemaphoreType.DMA((n_plane // 2,)),
                        pltpu.SemaphoreType.DMA((n_chip,)), pltpu.SemaphoreType.DMA((n_chip,)),
                        pltpu.SemaphoreType.DMA((1,)), pltpu.SemaphoreType.DMA((1,)),
                        pltpu.SemaphoreType.DMA((n_chip,)), pltpu.SemaphoreType.DMA((n_chip,)),
                        pltpu.SemaphoreType.DMA((n_plane,)), pltpu.SemaphoreType.DMA((n_plane,)),
                        pltpu.SemaphoreType.DMA((2,)),
                        pltpu.VMEM(rows_shape, out_grad.dtype),
                        pltpu.VMEM(rows_shape, out_grad.dtype),
                        pltpu.VMEM(hidden.shape, hidden.dtype),
                        pltpu.VMEM(hidden.shape, hidden.dtype),
                        pltpu.SemaphoreType.DMA((n_plane + 1,)),
                        pltpu.VMEM((n_chip, width, ff), jnp.bfloat16),
                        pltpu.VMEM((n_chip, width, ff), jnp.bfloat16),
                        pltpu.SemaphoreType.DMA((n_plane,)), pltpu.SemaphoreType.DMA((n_chip,)),
                        pltpu.VMEM((n_chip, width, ff), w_down.dtype),
                        pltpu.VMEM((n_chip, width, ff), w_down.dtype),
                        pltpu.VMEM(rows_shape, out_grad.dtype),
                        pltpu.VMEM(gate_act.shape, gate_act.dtype),
                        pltpu.VMEM(up_act.shape, up_act.dtype),
                        pltpu.SemaphoreType.DMA((4 + n_plane,))],
        compiler_params=pltpu.CompilerParams(collective_id=0, has_side_effects=True,
                                             vmem_limit_bytes=56 * 1024 * 1024),
    )(out_grad, w_down, gate_act, up_act)
    return (gate_grad, up_grad, down_grad)


def solution(mesh):
    n_dp = mesh.shape["dp"]
    n_tensor = mesh.shape["tensor"]
    devices = np.asarray(mesh.devices).reshape(n_dp // 2, 2, n_tensor)
    split = Mesh(devices, ("chip", "core", "tensor"))
    placed = P(("chip", "core"), "tensor")
    return jax.shard_map(
        body,
        mesh=split,
        in_specs=(placed, placed, placed, placed),
        out_specs=(placed, placed, placed),
        check_vma=False,
    )
```

```python
import math

import jax
import jax.numpy as jnp
import numpy as np
from jax import lax
from jax.experimental import pallas as pl
from jax.experimental.pallas import tpu as pltpu
from jax.sharding import Mesh
from jax.sharding import PartitionSpec as P

MESH = pl.DeviceIdType.MESH
ANY = pl.BlockSpec(memory_space=pl.ANY)


def _where():
    return lax.axis_index("chip"), lax.axis_index("core"), lax.axis_index("tensor")


def _fused_kernel(n_chip, n_lo, tile, grad_scale, og_ref, w_ref, gate_hbm, up_hbm,
                  gate_out, up_out, down_out, rows_out, w_out, w_other,
                  x_send, x_recv, r_send, r_recv, l_send, l_recv, w_send, w_recv,
                  f_send, f_recv, fw_send, fw_recv, fr_send, fr_recv, own_sem,
                  rows_v, ro_v, hid_v, ho_v, load_sem, part_v, recv_v, s_send, s_recv,
                  wv, wov, rows2_v, gate_v, up_v, late_sem):
    chip, core, ten = _where()
    n_plane = rows_out.shape[0]
    plane, lo = ten // n_lo, ten % n_lo
    right = ((plane + 1) % n_plane) * n_lo + lo
    left = ((plane + n_plane - 1) % n_plane) * n_lo + lo
    side = plane * n_lo + (1 - lo)
    other = (chip, 1 - core, ten)
    barrier = pltpu.get_barrier_semaphore()
    for t in (right, left, side):
        pl.semaphore_signal(barrier, inc=1, device_id=(chip, core, t), device_id_type=MESH)
    for k in range(1, n_chip):
        pl.semaphore_signal(barrier, inc=1, device_id=((chip + k) % n_chip, core, ten),
                            device_id_type=MESH)
    pl.semaphore_signal(barrier, inc=1, device_id=other, device_id_type=MESH)
    pl.semaphore_wait(barrier, 3 + (n_chip - 1) + 1)

    side_cp = pltpu.make_async_remote_copy(
        og_ref, rows_out.at[plane, lo], x_send.at[0], x_recv.at[0],
        device_id=(chip, core, side), device_id_type=MESH)
    side_cp.start()
    own_r = pltpu.make_async_copy(og_ref, rows_out.at[plane, lo], own_sem.at[0])
    own_w = pltpu.make_async_copy(w_ref, w_out.at[chip], own_sem.at[1])
    own_r.start()
    own_w.start()
    act_ld = [pltpu.make_async_copy(gate_hbm, gate_v, late_sem.at[2]),
              pltpu.make_async_copy(up_hbm, up_v, late_sem.at[3])]
    for ld in act_ld:
        ld.start()
    hid_cp = pltpu.make_async_remote_copy(hid_v, ho_v, f_send.at[0], f_recv.at[0],
                                          device_id=other, device_id_type=MESH)
    forwards = [hid_cp]
    w_fwds = []
    rows_fwd = {}
    rows_ld = {}

    def fwd_w(k):
        r = (chip + n_chip - k) % n_chip
        src = w_ref if k == 0 else w_out.at[r]
        cp = pltpu.make_async_remote_copy(src, w_other.at[r], fw_send.at[k], fw_recv.at[k],
                                          device_id=other, device_id_type=MESH)
        cp.start()
        forwards.append(cp)
        w_fwds.append(cp)

    def arrived(d):
        p = (plane + d) % n_plane
        cp = pltpu.make_async_remote_copy(rows_out.at[p, 1 - core], ro_v.at[p],
                                          fr_send.at[d], fr_recv.at[d],
                                          device_id=other, device_id_type=MESH)
        cp.start()
        forwards.append(cp)
        rows_fwd[d] = cp
        ld = pltpu.make_async_copy(rows_out.at[p, core], rows_v.at[p], load_sem.at[d])
        ld.start()
        rows_ld[d] = ld

    def partial(d):
        p = (plane + d) % n_plane
        rows_ld[d].wait()
        rows_fwd[d].wait_recv()
        part = lax.dot_general(rows_v[p], hid_v[...], (((0,), (0,)), ((), ())),
                               preferred_element_type=jnp.float32)
        part += lax.dot_general(ro_v[p], ho_v[...], (((0,), (0,)), ((), ())),
                                preferred_element_type=jnp.float32)
        part_v[p] = part.astype(part_v.dtype)

    fwd_w(0)
    own_r.wait()
    side_cp.wait_send()
    side_cp.wait_recv()
    arrived(0)

    n_steps = n_plane // 2
    ring = {}
    for s in range(n_steps):
        for d, sends, recvs, to, src_plane, half in (
            ("r", r_send, r_recv, right, (plane + n_plane - s) % n_plane, 0),
            ("l", l_send, l_recv, left, (plane + s) % n_plane, 1),
        ):
            block = rows_out.at[src_plane]
            if s == n_steps - 1:
                block = rows_out.at[src_plane, half]
            ring[(d, s)] = pltpu.make_async_remote_copy(
                block, block, sends.at[s], recvs.at[s],
                device_id=(chip, core, to), device_id_type=MESH)
    for d in ("r", "l"):
        ring[(d, 0)].start()
    w_copies = []
    for k in range(1, n_chip):
        cp = pltpu.make_async_remote_copy(
            w_ref, w_out.at[chip], w_send.at[k], w_recv.at[k],
            device_id=((chip + k) % n_chip, core, ten), device_id_type=MESH)
        cp.start()
        w_copies.append(cp)
    for ld in act_ld:
        ld.wait()
    gate_wide = gate_v[...].astype(jnp.float32)
    sigmoid_gate = jax.nn.sigmoid(gate_wide)
    hid_v[...] = (gate_wide * sigmoid_gate * up_v[...].astype(jnp.float32)).astype(hid_v.dtype)
    hid_cp.start()
    hid_cp.wait_recv()
    pending = [0]
    for s in range(1, n_steps):
        for d in ("r", "l"):
            ring[(d, s - 1)].wait_recv()
            ring[(d, s)].start()
        arrived(n_plane - s)
        arrived(s)
        for d in pending:
            partial(d)
        pending = [n_plane - s, s]
    for d in ("r", "l"):
        ring[(d, n_steps - 1)].wait_recv()
        for s in range(n_steps):
            ring[(d, s)].wait_send()
    arrived(n_steps)
    for d in pending + [n_steps]:
        partial(d)

    for k in range(1, n_chip):
        w_copies[k - 1].wait_recv()
        fwd_w(k)
    order = sorted(range(1, n_chip), key=lambda k: abs(k - n_chip // 2))
    outgoing = []
    for k in order:
        p = (chip + k) % n_chip
        send = pltpu.make_async_remote_copy(
            part_v.at[p], recv_v.at[chip], s_send.at[k], s_recv.at[k],
            device_id=(p, core, ten), device_id_type=MESH)
        send.start()
        outgoing.append(send)

    own_w.wait()
    for cp in w_copies:
        cp.wait_send()
    for cp in forwards:
        cp.wait_send()
    for cp in w_fwds:
        cp.wait_recv()

    loads = [pltpu.make_async_copy(src, dst, late_sem.at[i]) for i, (src, dst) in enumerate(
        ((w_out, wv), (w_other, wov)))]
    loads += [pltpu.make_async_copy(rows_out.at[r, 1 - core], rows2_v.at[r],
                                    late_sem.at[4 + r]) for r in range(n_plane)]
    for ld in loads:
        ld.start()
    for ld in loads:
        ld.wait()

    def one_tile(i, carry):
        rows = pl.ds(pl.multiple_of(i * tile, tile), tile)
        acc = jnp.zeros((tile, gate_v.shape[1]), jnp.float32)
        for r in range(n_plane):
            acc += jnp.dot(rows_v[r, rows, :], wv[r], preferred_element_type=jnp.float32)
            acc += jnp.dot(rows2_v[r, rows, :], wov[r], preferred_element_type=jnp.float32)
        gate_wide = gate_v[rows, :].astype(jnp.float32)
        up_wide = up_v[rows, :].astype(jnp.float32)
        sigmoid_gate = jax.nn.sigmoid(gate_wide)
        activated = gate_wide * sigmoid_gate
        gate_out[rows, :] = (
            acc * up_wide * sigmoid_gate * (1.0 + gate_wide * (1.0 - sigmoid_gate))
        ).astype(gate_out.dtype)
        up_out[rows, :] = (acc * activated).astype(up_out.dtype)
        return carry

    lax.fori_loop(0, gate_v.shape[0] // tile, one_tile, 0)

    for send in outgoing:
        send.wait_send()
        send.wait_recv()

    total = part_v[chip].astype(jnp.float32)
    for k in range(1, n_chip):
        total += recv_v[(chip + k) % n_chip].astype(jnp.float32)
    down_out[...] = (total * grad_scale).astype(down_out.dtype)


def body(out_grad, gate_act, up_act, w_down):
    seq_rows, ff = gate_act.shape
    width = w_down.shape[0]
    n_chip = lax.axis_size("chip")
    n_core = lax.axis_size("core")
    n_ten = lax.axis_size("tensor")
    core = lax.axis_index("core")
    grad_scale = 1.0 / math.sqrt(seq_rows * n_chip * n_core)
    hidden = jax.ShapeDtypeStruct(gate_act.shape, jnp.bfloat16)

    n_lo = n_core
    n_plane = n_ten // n_lo
    vmem = pl.BlockSpec(memory_space=pltpu.VMEM)
    rows_shape = (n_plane, seq_rows, out_grad.shape[1])
    gate_grad, up_grad, down_grad, _, _, _ = pl.pallas_call(
        lambda *refs: _fused_kernel(n_chip, n_lo, min(128, seq_rows), grad_scale, *refs),
        out_shape=(
            jax.ShapeDtypeStruct(gate_act.shape, jnp.bfloat16),
            jax.ShapeDtypeStruct(up_act.shape, jnp.bfloat16),
            jax.ShapeDtypeStruct(w_down.shape, jnp.bfloat16),
            jax.ShapeDtypeStruct((n_plane, n_lo, seq_rows, out_grad.shape[1]), out_grad.dtype),
            jax.ShapeDtypeStruct((n_chip, width, ff), w_down.dtype),
            jax.ShapeDtypeStruct((n_chip, width, ff), w_down.dtype),
        ),
        in_specs=[ANY, ANY, ANY, ANY],
        out_specs=(vmem, vmem, vmem, ANY, ANY, ANY),
        scratch_shapes=[pltpu.SemaphoreType.DMA((1,)), pltpu.SemaphoreType.DMA((1,)),
                        pltpu.SemaphoreType.DMA((n_plane // 2,)),
                        pltpu.SemaphoreType.DMA((n_plane // 2,)),
                        pltpu.SemaphoreType.DMA((n_plane // 2,)),
                        pltpu.SemaphoreType.DMA((n_plane // 2,)),
                        pltpu.SemaphoreType.DMA((n_chip,)), pltpu.SemaphoreType.DMA((n_chip,)),
                        pltpu.SemaphoreType.DMA((1,)), pltpu.SemaphoreType.DMA((1,)),
                        pltpu.SemaphoreType.DMA((n_chip,)), pltpu.SemaphoreType.DMA((n_chip,)),
                        pltpu.SemaphoreType.DMA((n_plane,)), pltpu.SemaphoreType.DMA((n_plane,)),
                        pltpu.SemaphoreType.DMA((2,)),
                        pltpu.VMEM(rows_shape, out_grad.dtype),
                        pltpu.VMEM(rows_shape, out_grad.dtype),
                        pltpu.VMEM(hidden.shape, hidden.dtype),
                        pltpu.VMEM(hidden.shape, hidden.dtype),
                        pltpu.SemaphoreType.DMA((n_plane + 1,)),
                        pltpu.VMEM((n_chip, width, ff), jnp.bfloat16),
                        pltpu.VMEM((n_chip, width, ff), jnp.bfloat16),
                        pltpu.SemaphoreType.DMA((n_plane,)), pltpu.SemaphoreType.DMA((n_chip,)),
                        pltpu.VMEM((n_chip, width, ff), w_down.dtype),
                        pltpu.VMEM((n_chip, width, ff), w_down.dtype),
                        pltpu.VMEM(rows_shape, out_grad.dtype),
                        pltpu.VMEM(gate_act.shape, gate_act.dtype),
                        pltpu.VMEM(up_act.shape, up_act.dtype),
                        pltpu.SemaphoreType.DMA((4 + n_plane,))],
        compiler_params=pltpu.CompilerParams(collective_id=0, has_side_effects=True,
                                             vmem_limit_bytes=56 * 1024 * 1024),
    )(out_grad, w_down, gate_act, up_act)
    return (gate_grad, up_grad, down_grad)


def solution(mesh):
    n_dp = mesh.shape["dp"]
    n_tensor = mesh.shape["tensor"]
    devices = np.asarray(mesh.devices).reshape(n_dp // 2, 2, n_tensor)
    split = Mesh(devices, ("chip", "core", "tensor"))
    placed = P(("chip", "core"), "tensor")
    return jax.shard_map(
        body,
        mesh=split,
        in_specs=(placed, placed, placed, placed),
        out_specs=(placed, placed, placed),
        check_vma=False,
    )
```

```python
import math

import jax
import jax.numpy as jnp
import numpy as np
from jax import lax
from jax.experimental import pallas as pl
from jax.experimental.pallas import tpu as pltpu
from jax.sharding import Mesh
from jax.sharding import PartitionSpec as P

MESH = pl.DeviceIdType.MESH
ANY = pl.BlockSpec(memory_space=pl.ANY)


def _where():
    return lax.axis_index("chip"), lax.axis_index("core"), lax.axis_index("tensor")


def _fused_kernel(n_chip, n_lo, tile, grad_scale, og_ref, w_ref, gate_hbm, up_hbm,
                  gate_out, up_out, down_out, rows_out, w_out, w_other,
                  x_send, x_recv, r_send, r_recv, l_send, l_recv, w_send, w_recv,
                  f_send, f_recv, fw_send, fw_recv, fr_send, fr_recv, own_sem,
                  rows_v, ro_v, hid_v, ho_v, load_sem, part_v, recv_v, s_send, s_recv,
                  wv, wov, rows2_v, gate_v, up_v, late_sem):
    chip, core, ten = _where()
    n_plane = rows_out.shape[0]
    plane, lo = ten // n_lo, ten % n_lo
    right = ((plane + 1) % n_plane) * n_lo + lo
    left = ((plane + n_plane - 1) % n_plane) * n_lo + lo
    side = plane * n_lo + (1 - lo)
    other = (chip, 1 - core, ten)
    barrier = pltpu.get_barrier_semaphore()
    for t in (right, left, side):
        pl.semaphore_signal(barrier, inc=1, device_id=(chip, core, t), device_id_type=MESH)
    for k in range(1, n_chip):
        pl.semaphore_signal(barrier, inc=1, device_id=((chip + k) % n_chip, core, ten),
                            device_id_type=MESH)
    pl.semaphore_signal(barrier, inc=1, device_id=other, device_id_type=MESH)
    pl.semaphore_wait(barrier, 3 + (n_chip - 1) + 1)

    side_cp = pltpu.make_async_remote_copy(
        og_ref, rows_out.at[plane, lo], x_send.at[0], x_recv.at[0],
        device_id=(chip, core, side), device_id_type=MESH)
    side_cp.start()
    own_r = pltpu.make_async_copy(og_ref, rows_out.at[plane, lo], own_sem.at[0])
    own_w = pltpu.make_async_copy(w_ref, w_out.at[chip], own_sem.at[1])
    own_r.start()
    own_w.start()
    act_ld = [pltpu.make_async_copy(gate_hbm, gate_v, late_sem.at[2]),
              pltpu.make_async_copy(up_hbm, up_v, late_sem.at[3])]
    for ld in act_ld:
        ld.start()
    hid_cp = pltpu.make_async_remote_copy(hid_v, ho_v, f_send.at[0], f_recv.at[0],
                                          device_id=other, device_id_type=MESH)
    forwards = [hid_cp]
    w_fwds = []
    rows_fwd = {}
    rows_ld = {}

    def fwd_w(k):
        r = (chip + n_chip - k) % n_chip
        src = w_ref if k == 0 else w_out.at[r]
        cp = pltpu.make_async_remote_copy(src, w_other.at[r], fw_send.at[k], fw_recv.at[k],
                                          device_id=other, device_id_type=MESH)
        cp.start()
        forwards.append(cp)
        w_fwds.append(cp)

    def arrived(d):
        p = (plane + d) % n_plane
        cp = pltpu.make_async_remote_copy(rows_out.at[p, 1 - core], ro_v.at[p],
                                          fr_send.at[d], fr_recv.at[d],
                                          device_id=other, device_id_type=MESH)
        cp.start()
        forwards.append(cp)
        rows_fwd[d] = cp
        ld = pltpu.make_async_copy(rows_out.at[p, core], rows_v.at[p], load_sem.at[d])
        ld.start()
        rows_ld[d] = ld

    def partial(d):
        p = (plane + d) % n_plane
        rows_ld[d].wait()
        rows_fwd[d].wait_recv()
        part = lax.dot_general(rows_v[p], hid_v[...], (((0,), (0,)), ((), ())),
                               preferred_element_type=jnp.float32)
        part += lax.dot_general(ro_v[p], ho_v[...], (((0,), (0,)), ((), ())),
                                preferred_element_type=jnp.float32)
        part_v[p] = part.astype(part_v.dtype)

    fwd_w(0)
    own_r.wait()
    side_cp.wait_send()
    side_cp.wait_recv()
    arrived(0)

    n_steps = n_plane // 2
    ring = {}
    for s in range(n_steps):
        for d, sends, recvs, to, src_plane, half in (
            ("r", r_send, r_recv, right, (plane + n_plane - s) % n_plane, 0),
            ("l", l_send, l_recv, left, (plane + s) % n_plane, 1),
        ):
            block = rows_out.at[src_plane]
            if s == n_steps - 1:
                block = rows_out.at[src_plane, half]
            ring[(d, s)] = pltpu.make_async_remote_copy(
                block, block, sends.at[s], recvs.at[s],
                device_id=(chip, core, to), device_id_type=MESH)
    for d in ("r", "l"):
        ring[(d, 0)].start()
    order = sorted(range(1, n_chip), key=lambda k: abs(k - n_chip // 2))
    w_copies = {}
    for k in order:
        cp = pltpu.make_async_remote_copy(
            w_ref, w_out.at[chip], w_send.at[k], w_recv.at[k],
            device_id=((chip + k) % n_chip, core, ten), device_id_type=MESH)
        cp.start()
        w_copies[k] = cp
    for ld in act_ld:
        ld.wait()
    gate_wide = gate_v[...].astype(jnp.float32)
    sigmoid_gate = jax.nn.sigmoid(gate_wide)
    hid_v[...] = (gate_wide * sigmoid_gate * up_v[...].astype(jnp.float32)).astype(hid_v.dtype)
    hid_cp.start()
    hid_cp.wait_recv()
    pending = [0]
    for s in range(1, n_steps):
        for d in ("r", "l"):
            ring[(d, s - 1)].wait_recv()
            ring[(d, s)].start()
        arrived(n_plane - s)
        arrived(s)
        for d in pending:
            partial(d)
        pending = [n_plane - s, s]
    for d in ("r", "l"):
        ring[(d, n_steps - 1)].wait_recv()
        for s in range(n_steps):
            ring[(d, s)].wait_send()
    arrived(n_steps)
    for d in pending + [n_steps]:
        partial(d)

    for k in order:
        w_copies[k].wait_recv()
        fwd_w(k)
    outgoing = []
    for k in order:
        p = (chip + k) % n_chip
        send = pltpu.make_async_remote_copy(
            part_v.at[p], recv_v.at[chip], s_send.at[k], s_recv.at[k],
            device_id=(p, core, ten), device_id_type=MESH)
        send.start()
        outgoing.append(send)

    own_w.wait()
    for k in order:
        w_copies[k].wait_send()
    for cp in forwards:
        cp.wait_send()
    for cp in w_fwds:
        cp.wait_recv()

    loads = [pltpu.make_async_copy(src, dst, late_sem.at[i]) for i, (src, dst) in enumerate(
        ((w_out, wv), (w_other, wov)))]
    loads += [pltpu.make_async_copy(rows_out.at[r, 1 - core], rows2_v.at[r],
                                    late_sem.at[4 + r]) for r in range(n_plane)]
    for ld in loads:
        ld.start()
    for ld in loads:
        ld.wait()

    def one_tile(i, carry):
        rows = pl.ds(pl.multiple_of(i * tile, tile), tile)
        acc = jnp.zeros((tile, gate_v.shape[1]), jnp.float32)
        for r in range(n_plane):
            acc += jnp.dot(rows_v[r, rows, :], wv[r], preferred_element_type=jnp.float32)
            acc += jnp.dot(rows2_v[r, rows, :], wov[r], preferred_element_type=jnp.float32)
        gate_wide = gate_v[rows, :].astype(jnp.float32)
        up_wide = up_v[rows, :].astype(jnp.float32)
        sigmoid_gate = jax.nn.sigmoid(gate_wide)
        activated = gate_wide * sigmoid_gate
        gate_out[rows, :] = (
            acc * up_wide * sigmoid_gate * (1.0 + gate_wide * (1.0 - sigmoid_gate))
        ).astype(gate_out.dtype)
        up_out[rows, :] = (acc * activated).astype(up_out.dtype)
        return carry

    lax.fori_loop(0, gate_v.shape[0] // tile, one_tile, 0)

    for send in outgoing:
        send.wait_send()
        send.wait_recv()

    total = part_v[chip].astype(jnp.float32)
    for k in range(1, n_chip):
        total += recv_v[(chip + k) % n_chip].astype(jnp.float32)
    down_out[...] = (total * grad_scale).astype(down_out.dtype)


def body(out_grad, gate_act, up_act, w_down):
    seq_rows, ff = gate_act.shape
    width = w_down.shape[0]
    n_chip = lax.axis_size("chip")
    n_core = lax.axis_size("core")
    n_ten = lax.axis_size("tensor")
    core = lax.axis_index("core")
    grad_scale = 1.0 / math.sqrt(seq_rows * n_chip * n_core)
    hidden = jax.ShapeDtypeStruct(gate_act.shape, jnp.bfloat16)

    n_lo = n_core
    n_plane = n_ten // n_lo
    vmem = pl.BlockSpec(memory_space=pltpu.VMEM)
    rows_shape = (n_plane, seq_rows, out_grad.shape[1])
    gate_grad, up_grad, down_grad, _, _, _ = pl.pallas_call(
        lambda *refs: _fused_kernel(n_chip, n_lo, min(128, seq_rows), grad_scale, *refs),
        out_shape=(
            jax.ShapeDtypeStruct(gate_act.shape, jnp.bfloat16),
            jax.ShapeDtypeStruct(up_act.shape, jnp.bfloat16),
            jax.ShapeDtypeStruct(w_down.shape, jnp.bfloat16),
            jax.ShapeDtypeStruct((n_plane, n_lo, seq_rows, out_grad.shape[1]), out_grad.dtype),
            jax.ShapeDtypeStruct((n_chip, width, ff), w_down.dtype),
            jax.ShapeDtypeStruct((n_chip, width, ff), w_down.dtype),
        ),
        in_specs=[ANY, ANY, ANY, ANY],
        out_specs=(vmem, vmem, vmem, ANY, ANY, ANY),
        scratch_shapes=[pltpu.SemaphoreType.DMA((1,)), pltpu.SemaphoreType.DMA((1,)),
                        pltpu.SemaphoreType.DMA((n_plane // 2,)),
                        pltpu.SemaphoreType.DMA((n_plane // 2,)),
                        pltpu.SemaphoreType.DMA((n_plane // 2,)),
                        pltpu.SemaphoreType.DMA((n_plane // 2,)),
                        pltpu.SemaphoreType.DMA((n_chip,)), pltpu.SemaphoreType.DMA((n_chip,)),
                        pltpu.SemaphoreType.DMA((1,)), pltpu.SemaphoreType.DMA((1,)),
                        pltpu.SemaphoreType.DMA((n_chip,)), pltpu.SemaphoreType.DMA((n_chip,)),
                        pltpu.SemaphoreType.DMA((n_plane,)), pltpu.SemaphoreType.DMA((n_plane,)),
                        pltpu.SemaphoreType.DMA((2,)),
                        pltpu.VMEM(rows_shape, out_grad.dtype),
                        pltpu.VMEM(rows_shape, out_grad.dtype),
                        pltpu.VMEM(hidden.shape, hidden.dtype),
                        pltpu.VMEM(hidden.shape, hidden.dtype),
                        pltpu.SemaphoreType.DMA((n_plane + 1,)),
                        pltpu.VMEM((n_chip, width, ff), jnp.bfloat16),
                        pltpu.VMEM((n_chip, width, ff), jnp.bfloat16),
                        pltpu.SemaphoreType.DMA((n_plane,)), pltpu.SemaphoreType.DMA((n_chip,)),
                        pltpu.VMEM((n_chip, width, ff), w_down.dtype),
                        pltpu.VMEM((n_chip, width, ff), w_down.dtype),
                        pltpu.VMEM(rows_shape, out_grad.dtype),
                        pltpu.VMEM(gate_act.shape, gate_act.dtype),
                        pltpu.VMEM(up_act.shape, up_act.dtype),
                        pltpu.SemaphoreType.DMA((4 + n_plane,))],
        compiler_params=pltpu.CompilerParams(collective_id=0, has_side_effects=True,
                                             vmem_limit_bytes=56 * 1024 * 1024),
    )(out_grad, w_down, gate_act, up_act)
    return (gate_grad, up_grad, down_grad)


def solution(mesh):
    n_dp = mesh.shape["dp"]
    n_tensor = mesh.shape["tensor"]
    devices = np.asarray(mesh.devices).reshape(n_dp // 2, 2, n_tensor)
    split = Mesh(devices, ("chip", "core", "tensor"))
    placed = P(("chip", "core"), "tensor")
    return jax.shard_map(
        body,
        mesh=split,
        in_specs=(placed, placed, placed, placed),
        out_specs=(placed, placed, placed),
        check_vma=False,
    )
```

```python
import math

import jax
import jax.numpy as jnp
import numpy as np
from jax import lax
from jax.experimental import pallas as pl
from jax.experimental.pallas import tpu as pltpu
from jax.sharding import Mesh
from jax.sharding import PartitionSpec as P

MESH = pl.DeviceIdType.MESH
ANY = pl.BlockSpec(memory_space=pl.ANY)


def _where():
    return lax.axis_index("chip"), lax.axis_index("core"), lax.axis_index("tensor")


def _fused_kernel(n_chip, n_lo, tile, grad_scale, og_ref, w_ref, gate_hbm, up_hbm,
                  gate_out, up_out, down_out, rows_out,
                  x_send, x_recv, r_send, r_recv, l_send, l_recv, w_send, w_recv,
                  f_send, f_recv, fw_send, fw_recv, fr_send, fr_recv, own_sem,
                  rows_v, ro_v, hid_v, ho_v, load_sem, part_v, recv_v, s_send, s_recv,
                  wv, wov, rows2_v, gate_v, up_v, late_sem):
    chip, core, ten = _where()
    n_plane = rows_out.shape[0]
    plane, lo = ten // n_lo, ten % n_lo
    right = ((plane + 1) % n_plane) * n_lo + lo
    left = ((plane + n_plane - 1) % n_plane) * n_lo + lo
    side = plane * n_lo + (1 - lo)
    other = (chip, 1 - core, ten)
    barrier = pltpu.get_barrier_semaphore()
    for t in (right, left, side):
        pl.semaphore_signal(barrier, inc=1, device_id=(chip, core, t), device_id_type=MESH)
    for k in range(1, n_chip):
        pl.semaphore_signal(barrier, inc=1, device_id=((chip + k) % n_chip, core, ten),
                            device_id_type=MESH)
    pl.semaphore_signal(barrier, inc=1, device_id=other, device_id_type=MESH)
    pl.semaphore_wait(barrier, 3 + (n_chip - 1) + 1)

    side_cp = pltpu.make_async_remote_copy(
        og_ref, rows_out.at[plane, lo], x_send.at[0], x_recv.at[0],
        device_id=(chip, core, side), device_id_type=MESH)
    side_cp.start()
    own_r = pltpu.make_async_copy(og_ref, rows_out.at[plane, lo], own_sem.at[0])
    own_w = pltpu.make_async_copy(w_ref, wv.at[chip], own_sem.at[1])
    own_r.start()
    own_w.start()
    act_ld = [pltpu.make_async_copy(gate_hbm, gate_v, late_sem.at[2]),
              pltpu.make_async_copy(up_hbm, up_v, late_sem.at[3])]
    for ld in act_ld:
        ld.start()
    hid_cp = pltpu.make_async_remote_copy(hid_v, ho_v, f_send.at[0], f_recv.at[0],
                                          device_id=other, device_id_type=MESH)
    forwards = [hid_cp]
    w_fwds = []
    rows_fwd = {}
    rows_ld = {}

    def fwd_w(k):
        r = (chip + n_chip - k) % n_chip
        src = w_ref if k == 0 else wv.at[r]
        cp = pltpu.make_async_remote_copy(src, wov.at[r], fw_send.at[k], fw_recv.at[k],
                                          device_id=other, device_id_type=MESH)
        cp.start()
        forwards.append(cp)
        w_fwds.append(cp)

    def arrived(d):
        p = (plane + d) % n_plane
        cp = pltpu.make_async_remote_copy(rows_out.at[p, 1 - core], ro_v.at[p],
                                          fr_send.at[d], fr_recv.at[d],
                                          device_id=other, device_id_type=MESH)
        cp.start()
        forwards.append(cp)
        rows_fwd[d] = cp
        ld = pltpu.make_async_copy(rows_out.at[p, core], rows_v.at[p], load_sem.at[d])
        ld.start()
        rows_ld[d] = ld

    def partial(d):
        p = (plane + d) % n_plane
        rows_ld[d].wait()
        rows_fwd[d].wait_recv()
        part = lax.dot_general(rows_v[p], hid_v[...], (((0,), (0,)), ((), ())),
                               preferred_element_type=jnp.float32)
        part += lax.dot_general(ro_v[p], ho_v[...], (((0,), (0,)), ((), ())),
                                preferred_element_type=jnp.float32)
        part_v[p] = part.astype(part_v.dtype)

    fwd_w(0)
    own_r.wait()
    side_cp.wait_send()
    side_cp.wait_recv()
    arrived(0)

    n_steps = n_plane // 2
    ring = {}
    for s in range(n_steps):
        for d, sends, recvs, to, src_plane, half in (
            ("r", r_send, r_recv, right, (plane + n_plane - s) % n_plane, 0),
            ("l", l_send, l_recv, left, (plane + s) % n_plane, 1),
        ):
            block = rows_out.at[src_plane]
            if s == n_steps - 1:
                block = rows_out.at[src_plane, half]
            ring[(d, s)] = pltpu.make_async_remote_copy(
                block, block, sends.at[s], recvs.at[s],
                device_id=(chip, core, to), device_id_type=MESH)
    for d in ("r", "l"):
        ring[(d, 0)].start()
    order = sorted(range(1, n_chip), key=lambda k: abs(k - n_chip // 2))
    w_copies = {}
    for k in order:
        cp = pltpu.make_async_remote_copy(
            w_ref, wv.at[chip], w_send.at[k], w_recv.at[k],
            device_id=((chip + k) % n_chip, core, ten), device_id_type=MESH)
        cp.start()
        w_copies[k] = cp
    for ld in act_ld:
        ld.wait()
    gate_wide = gate_v[...].astype(jnp.float32)
    sigmoid_gate = jax.nn.sigmoid(gate_wide)
    hid_v[...] = (gate_wide * sigmoid_gate * up_v[...].astype(jnp.float32)).astype(hid_v.dtype)
    hid_cp.start()
    hid_cp.wait_recv()
    pending = [0]
    for s in range(1, n_steps):
        for d in ("r", "l"):
            ring[(d, s - 1)].wait_recv()
            ring[(d, s)].start()
        arrived(n_plane - s)
        arrived(s)
        for d in pending:
            partial(d)
        pending = [n_plane - s, s]
    for d in ("r", "l"):
        ring[(d, n_steps - 1)].wait_recv()
        for s in range(n_steps):
            ring[(d, s)].wait_send()
    arrived(n_steps)
    loads = [pltpu.make_async_copy(rows_out.at[r, 1 - core], rows2_v.at[r],
                                   late_sem.at[4 + r]) for r in range(n_plane)]
    for ld in loads:
        ld.start()
    for d in pending + [n_steps]:
        partial(d)

    for k in order:
        w_copies[k].wait_recv()
        fwd_w(k)
    outgoing = []
    for k in order:
        p = (chip + k) % n_chip
        send = pltpu.make_async_remote_copy(
            part_v.at[p], recv_v.at[chip], s_send.at[k], s_recv.at[k],
            device_id=(p, core, ten), device_id_type=MESH)
        send.start()
        outgoing.append(send)

    own_w.wait()
    for k in order:
        w_copies[k].wait_send()
    for cp in forwards:
        cp.wait_send()
    for cp in w_fwds:
        cp.wait_recv()

    for ld in loads:
        ld.wait()

    def one_tile(i, carry):
        rows = pl.ds(pl.multiple_of(i * tile, tile), tile)
        acc = jnp.zeros((tile, gate_v.shape[1]), jnp.float32)
        for r in range(n_plane):
            acc += jnp.dot(rows_v[r, rows, :], wv[r], preferred_element_type=jnp.float32)
            acc += jnp.dot(rows2_v[r, rows, :], wov[r], preferred_element_type=jnp.float32)
        gate_wide = gate_v[rows, :].astype(jnp.float32)
        up_wide = up_v[rows, :].astype(jnp.float32)
        sigmoid_gate = jax.nn.sigmoid(gate_wide)
        activated = gate_wide * sigmoid_gate
        gate_out[rows, :] = (
            acc * up_wide * sigmoid_gate * (1.0 + gate_wide * (1.0 - sigmoid_gate))
        ).astype(gate_out.dtype)
        up_out[rows, :] = (acc * activated).astype(up_out.dtype)
        return carry

    lax.fori_loop(0, gate_v.shape[0] // tile, one_tile, 0)

    for send in outgoing:
        send.wait_send()
        send.wait_recv()

    total = part_v[chip].astype(jnp.float32)
    for k in range(1, n_chip):
        total += recv_v[(chip + k) % n_chip].astype(jnp.float32)
    down_out[...] = (total * grad_scale).astype(down_out.dtype)


def body(out_grad, gate_act, up_act, w_down):
    seq_rows, ff = gate_act.shape
    width = w_down.shape[0]
    n_chip = lax.axis_size("chip")
    n_core = lax.axis_size("core")
    n_ten = lax.axis_size("tensor")
    core = lax.axis_index("core")
    grad_scale = 1.0 / math.sqrt(seq_rows * n_chip * n_core)
    hidden = jax.ShapeDtypeStruct(gate_act.shape, jnp.bfloat16)

    n_lo = n_core
    n_plane = n_ten // n_lo
    vmem = pl.BlockSpec(memory_space=pltpu.VMEM)
    rows_shape = (n_plane, seq_rows, out_grad.shape[1])
    gate_grad, up_grad, down_grad, _ = pl.pallas_call(
        lambda *refs: _fused_kernel(n_chip, n_lo, min(128, seq_rows), grad_scale, *refs),
        out_shape=(
            jax.ShapeDtypeStruct(gate_act.shape, jnp.bfloat16),
            jax.ShapeDtypeStruct(up_act.shape, jnp.bfloat16),
            jax.ShapeDtypeStruct(w_down.shape, jnp.bfloat16),
            jax.ShapeDtypeStruct((n_plane, n_lo, seq_rows, out_grad.shape[1]), out_grad.dtype),
        ),
        in_specs=[ANY, ANY, ANY, ANY],
        out_specs=(vmem, vmem, vmem, ANY),
        scratch_shapes=[pltpu.SemaphoreType.DMA((1,)), pltpu.SemaphoreType.DMA((1,)),
                        pltpu.SemaphoreType.DMA((n_plane // 2,)),
                        pltpu.SemaphoreType.DMA((n_plane // 2,)),
                        pltpu.SemaphoreType.DMA((n_plane // 2,)),
                        pltpu.SemaphoreType.DMA((n_plane // 2,)),
                        pltpu.SemaphoreType.DMA((n_chip,)), pltpu.SemaphoreType.DMA((n_chip,)),
                        pltpu.SemaphoreType.DMA((1,)), pltpu.SemaphoreType.DMA((1,)),
                        pltpu.SemaphoreType.DMA((n_chip,)), pltpu.SemaphoreType.DMA((n_chip,)),
                        pltpu.SemaphoreType.DMA((n_plane,)), pltpu.SemaphoreType.DMA((n_plane,)),
                        pltpu.SemaphoreType.DMA((2,)),
                        pltpu.VMEM(rows_shape, out_grad.dtype),
                        pltpu.VMEM(rows_shape, out_grad.dtype),
                        pltpu.VMEM(hidden.shape, hidden.dtype),
                        pltpu.VMEM(hidden.shape, hidden.dtype),
                        pltpu.SemaphoreType.DMA((n_plane + 1,)),
                        pltpu.VMEM((n_chip, width, ff), jnp.bfloat16),
                        pltpu.VMEM((n_chip, width, ff), jnp.bfloat16),
                        pltpu.SemaphoreType.DMA((n_plane,)), pltpu.SemaphoreType.DMA((n_chip,)),
                        pltpu.VMEM((n_chip, width, ff), w_down.dtype),
                        pltpu.VMEM((n_chip, width, ff), w_down.dtype),
                        pltpu.VMEM(rows_shape, out_grad.dtype),
                        pltpu.VMEM(gate_act.shape, gate_act.dtype),
                        pltpu.VMEM(up_act.shape, up_act.dtype),
                        pltpu.SemaphoreType.DMA((4 + n_plane,))],
        compiler_params=pltpu.CompilerParams(collective_id=0, has_side_effects=True,
                                             vmem_limit_bytes=56 * 1024 * 1024),
    )(out_grad, w_down, gate_act, up_act)
    return (gate_grad, up_grad, down_grad)


def solution(mesh):
    n_dp = mesh.shape["dp"]
    n_tensor = mesh.shape["tensor"]
    devices = np.asarray(mesh.devices).reshape(n_dp // 2, 2, n_tensor)
    split = Mesh(devices, ("chip", "core", "tensor"))
    placed = P(("chip", "core"), "tensor")
    return jax.shard_map(
        body,
        mesh=split,
        in_specs=(placed, placed, placed, placed),
        out_specs=(placed, placed, placed),
        check_vma=False,
    )
```

```python
import math

import jax
import jax.numpy as jnp
import numpy as np
from jax import lax
from jax.experimental import pallas as pl
from jax.experimental.pallas import tpu as pltpu
from jax.sharding import Mesh
from jax.sharding import PartitionSpec as P

MESH = pl.DeviceIdType.MESH
ANY = pl.BlockSpec(memory_space=pl.ANY)


def _where():
    return lax.axis_index("chip"), lax.axis_index("core"), lax.axis_index("tensor")


def _fused_kernel(n_chip, n_lo, tile, grad_scale, og_ref, w_ref, gate_hbm, up_hbm,
                  gate_out, up_out, down_out, rows_out,
                  x_send, x_recv, r_send, r_recv, l_send, l_recv, w_send, w_recv,
                  f_send, f_recv, fw_send, fw_recv, fr_send, fr_recv, own_sem,
                  rows_v, ro_v, hid_v, ho_v, load_sem, part_v, recv_v, s_send, s_recv,
                  wv, wov, rows2_v, gate_v, up_v, late_sem, gate_res, up_res, down_res,
                  out_sem):
    chip, core, ten = _where()
    n_plane = rows_out.shape[0]
    plane, lo = ten // n_lo, ten % n_lo
    right = ((plane + 1) % n_plane) * n_lo + lo
    left = ((plane + n_plane - 1) % n_plane) * n_lo + lo
    side = plane * n_lo + (1 - lo)
    other = (chip, 1 - core, ten)
    barrier = pltpu.get_barrier_semaphore()
    for t in (right, left, side):
        pl.semaphore_signal(barrier, inc=1, device_id=(chip, core, t), device_id_type=MESH)
    for k in range(1, n_chip):
        pl.semaphore_signal(barrier, inc=1, device_id=((chip + k) % n_chip, core, ten),
                            device_id_type=MESH)
    pl.semaphore_signal(barrier, inc=1, device_id=other, device_id_type=MESH)
    pl.semaphore_wait(barrier, 3 + (n_chip - 1) + 1)

    side_cp = pltpu.make_async_remote_copy(
        og_ref, rows_out.at[plane, lo], x_send.at[0], x_recv.at[0],
        device_id=(chip, core, side), device_id_type=MESH)
    side_cp.start()
    own_r = pltpu.make_async_copy(og_ref, rows_out.at[plane, lo], own_sem.at[0])
    own_w = pltpu.make_async_copy(w_ref, wv.at[chip], own_sem.at[1])
    own_r.start()
    own_w.start()
    act_ld = [pltpu.make_async_copy(gate_hbm, gate_v, late_sem.at[2]),
              pltpu.make_async_copy(up_hbm, up_v, late_sem.at[3])]
    for ld in act_ld:
        ld.start()
    hid_cp = pltpu.make_async_remote_copy(hid_v, ho_v, f_send.at[0], f_recv.at[0],
                                          device_id=other, device_id_type=MESH)
    forwards = [hid_cp]
    w_fwds = []
    rows_fwd = {}
    rows_ld = {}

    def fwd_w(k):
        r = (chip + n_chip - k) % n_chip
        src = w_ref if k == 0 else wv.at[r]
        cp = pltpu.make_async_remote_copy(src, wov.at[r], fw_send.at[k], fw_recv.at[k],
                                          device_id=other, device_id_type=MESH)
        cp.start()
        forwards.append(cp)
        w_fwds.append(cp)

    def arrived(d):
        p = (plane + d) % n_plane
        cp = pltpu.make_async_remote_copy(rows_out.at[p, 1 - core], ro_v.at[p],
                                          fr_send.at[d], fr_recv.at[d],
                                          device_id=other, device_id_type=MESH)
        cp.start()
        forwards.append(cp)
        rows_fwd[d] = cp
        ld = pltpu.make_async_copy(rows_out.at[p, core], rows_v.at[p], load_sem.at[d])
        ld.start()
        rows_ld[d] = ld

    def partial(d):
        p = (plane + d) % n_plane
        rows_ld[d].wait()
        rows_fwd[d].wait_recv()
        part = lax.dot_general(rows_v[p], hid_v[...], (((0,), (0,)), ((), ())),
                               preferred_element_type=jnp.float32)
        part += lax.dot_general(ro_v[p], ho_v[...], (((0,), (0,)), ((), ())),
                                preferred_element_type=jnp.float32)
        part_v[p] = part.astype(part_v.dtype)

    fwd_w(0)
    own_r.wait()
    side_cp.wait_send()
    side_cp.wait_recv()
    arrived(0)

    n_steps = n_plane // 2
    ring = {}
    for s in range(n_steps):
        for d, sends, recvs, to, src_plane, half in (
            ("r", r_send, r_recv, right, (plane + n_plane - s) % n_plane, 0),
            ("l", l_send, l_recv, left, (plane + s) % n_plane, 1),
        ):
            block = rows_out.at[src_plane]
            if s == n_steps - 1:
                block = rows_out.at[src_plane, half]
            ring[(d, s)] = pltpu.make_async_remote_copy(
                block, block, sends.at[s], recvs.at[s],
                device_id=(chip, core, to), device_id_type=MESH)
    for d in ("r", "l"):
        ring[(d, 0)].start()
    order = sorted(range(1, n_chip), key=lambda k: abs(k - n_chip // 2))
    w_copies = {}
    for k in order:
        cp = pltpu.make_async_remote_copy(
            w_ref, wv.at[chip], w_send.at[k], w_recv.at[k],
            device_id=((chip + k) % n_chip, core, ten), device_id_type=MESH)
        cp.start()
        w_copies[k] = cp
    for ld in act_ld:
        ld.wait()
    gate_wide = gate_v[...].astype(jnp.float32)
    sigmoid_gate = jax.nn.sigmoid(gate_wide)
    hid_v[...] = (gate_wide * sigmoid_gate * up_v[...].astype(jnp.float32)).astype(hid_v.dtype)
    hid_cp.start()
    hid_cp.wait_recv()
    pending = [0]
    for s in range(1, n_steps):
        for d in ("r", "l"):
            ring[(d, s - 1)].wait_recv()
            ring[(d, s)].start()
        arrived(n_plane - s)
        arrived(s)
        for d in pending:
            partial(d)
        pending = [n_plane - s, s]
    for d in ("r", "l"):
        ring[(d, n_steps - 1)].wait_recv()
        for s in range(n_steps):
            ring[(d, s)].wait_send()
    arrived(n_steps)
    loads = [pltpu.make_async_copy(rows_out.at[r, 1 - core], rows2_v.at[r],
                                   late_sem.at[4 + r]) for r in range(n_plane)]
    for ld in loads:
        ld.start()
    for d in pending + [n_steps]:
        partial(d)

    for k in order:
        w_copies[k].wait_recv()
        fwd_w(k)
    outgoing = []
    for k in order:
        p = (chip + k) % n_chip
        send = pltpu.make_async_remote_copy(
            part_v.at[p], recv_v.at[chip], s_send.at[k], s_recv.at[k],
            device_id=(p, core, ten), device_id_type=MESH)
        send.start()
        outgoing.append(send)

    own_w.wait()
    for k in order:
        w_copies[k].wait_send()
    for cp in forwards:
        cp.wait_send()
    for cp in w_fwds:
        cp.wait_recv()

    for ld in loads:
        ld.wait()

    def one_tile(i, carry):
        rows = pl.ds(pl.multiple_of(i * tile, tile), tile)
        acc = jnp.zeros((tile, gate_v.shape[1]), jnp.float32)
        for r in range(n_plane):
            acc += jnp.dot(rows_v[r, rows, :], wv[r], preferred_element_type=jnp.float32)
            acc += jnp.dot(rows2_v[r, rows, :], wov[r], preferred_element_type=jnp.float32)
        gate_wide = gate_v[rows, :].astype(jnp.float32)
        up_wide = up_v[rows, :].astype(jnp.float32)
        sigmoid_gate = jax.nn.sigmoid(gate_wide)
        activated = gate_wide * sigmoid_gate
        gate_res[rows, :] = (
            acc * up_wide * sigmoid_gate * (1.0 + gate_wide * (1.0 - sigmoid_gate))
        ).astype(gate_res.dtype)
        up_res[rows, :] = (acc * activated).astype(up_res.dtype)
        return carry

    lax.fori_loop(0, gate_v.shape[0] // tile, one_tile, 0)
    results = [pltpu.make_async_copy(gate_res, gate_out, out_sem.at[0]),
               pltpu.make_async_copy(up_res, up_out, out_sem.at[1])]
    for cp in results:
        cp.start()

    for send in outgoing:
        send.wait_send()
        send.wait_recv()

    total = part_v[chip].astype(jnp.float32)
    for k in range(1, n_chip):
        total += recv_v[(chip + k) % n_chip].astype(jnp.float32)
    down_res[...] = (total * grad_scale).astype(down_res.dtype)
    results.append(pltpu.make_async_copy(down_res, down_out, out_sem.at[2]))
    results[-1].start()
    for cp in results:
        cp.wait()


def body(out_grad, gate_act, up_act, w_down):
    seq_rows, ff = gate_act.shape
    width = w_down.shape[0]
    n_chip = lax.axis_size("chip")
    n_core = lax.axis_size("core")
    n_ten = lax.axis_size("tensor")
    core = lax.axis_index("core")
    grad_scale = 1.0 / math.sqrt(seq_rows * n_chip * n_core)
    hidden = jax.ShapeDtypeStruct(gate_act.shape, jnp.bfloat16)

    n_lo = n_core
    n_plane = n_ten // n_lo
    vmem = pl.BlockSpec(memory_space=pltpu.VMEM)
    rows_shape = (n_plane, seq_rows, out_grad.shape[1])
    gate_grad, up_grad, down_grad, _ = pl.pallas_call(
        lambda *refs: _fused_kernel(n_chip, n_lo, min(128, seq_rows), grad_scale, *refs),
        out_shape=(
            jax.ShapeDtypeStruct(gate_act.shape, jnp.bfloat16),
            jax.ShapeDtypeStruct(up_act.shape, jnp.bfloat16),
            jax.ShapeDtypeStruct(w_down.shape, jnp.bfloat16),
            jax.ShapeDtypeStruct((n_plane, n_lo, seq_rows, out_grad.shape[1]), out_grad.dtype),
        ),
        in_specs=[ANY, ANY, ANY, ANY],
        out_specs=(ANY, ANY, ANY, ANY),
        scratch_shapes=[pltpu.SemaphoreType.DMA((1,)), pltpu.SemaphoreType.DMA((1,)),
                        pltpu.SemaphoreType.DMA((n_plane // 2,)),
                        pltpu.SemaphoreType.DMA((n_plane // 2,)),
                        pltpu.SemaphoreType.DMA((n_plane // 2,)),
                        pltpu.SemaphoreType.DMA((n_plane // 2,)),
                        pltpu.SemaphoreType.DMA((n_chip,)), pltpu.SemaphoreType.DMA((n_chip,)),
                        pltpu.SemaphoreType.DMA((1,)), pltpu.SemaphoreType.DMA((1,)),
                        pltpu.SemaphoreType.DMA((n_chip,)), pltpu.SemaphoreType.DMA((n_chip,)),
                        pltpu.SemaphoreType.DMA((n_plane,)), pltpu.SemaphoreType.DMA((n_plane,)),
                        pltpu.SemaphoreType.DMA((2,)),
                        pltpu.VMEM(rows_shape, out_grad.dtype),
                        pltpu.VMEM(rows_shape, out_grad.dtype),
                        pltpu.VMEM(hidden.shape, hidden.dtype),
                        pltpu.VMEM(hidden.shape, hidden.dtype),
                        pltpu.SemaphoreType.DMA((n_plane + 1,)),
                        pltpu.VMEM((n_chip, width, ff), jnp.bfloat16),
                        pltpu.VMEM((n_chip, width, ff), jnp.bfloat16),
                        pltpu.SemaphoreType.DMA((n_plane,)), pltpu.SemaphoreType.DMA((n_chip,)),
                        pltpu.VMEM((n_chip, width, ff), w_down.dtype),
                        pltpu.VMEM((n_chip, width, ff), w_down.dtype),
                        pltpu.VMEM(rows_shape, out_grad.dtype),
                        pltpu.VMEM(gate_act.shape, gate_act.dtype),
                        pltpu.VMEM(up_act.shape, up_act.dtype),
                        pltpu.SemaphoreType.DMA((4 + n_plane,)),
                        pltpu.VMEM(gate_act.shape, jnp.bfloat16),
                        pltpu.VMEM(up_act.shape, jnp.bfloat16),
                        pltpu.VMEM(w_down.shape, jnp.bfloat16),
                        pltpu.SemaphoreType.DMA((3,))],
        compiler_params=pltpu.CompilerParams(collective_id=0, has_side_effects=True,
                                             vmem_limit_bytes=56 * 1024 * 1024),
    )(out_grad, w_down, gate_act, up_act)
    return (gate_grad, up_grad, down_grad)


def solution(mesh):
    n_dp = mesh.shape["dp"]
    n_tensor = mesh.shape["tensor"]
    devices = np.asarray(mesh.devices).reshape(n_dp // 2, 2, n_tensor)
    split = Mesh(devices, ("chip", "core", "tensor"))
    placed = P(("chip", "core"), "tensor")
    return jax.shard_map(
        body,
        mesh=split,
        in_specs=(placed, placed, placed, placed),
        out_specs=(placed, placed, placed),
        check_vma=False,
    )
```

```python
import math

import jax
import jax.numpy as jnp
import numpy as np
from jax import lax
from jax.experimental import pallas as pl
from jax.experimental.pallas import tpu as pltpu
from jax.sharding import Mesh
from jax.sharding import PartitionSpec as P

MESH = pl.DeviceIdType.MESH
ANY = pl.BlockSpec(memory_space=pl.ANY)


def _where():
    return lax.axis_index("chip"), lax.axis_index("core"), lax.axis_index("tensor")


def _fused_kernel(n_chip, n_lo, tile, grad_scale, og_ref, w_ref, gate_hbm, up_hbm,
                  gate_out, up_out, down_out, rows_out, w_out, w_other,
                  x_send, x_recv, r_send, r_recv, l_send, l_recv, w_send, w_recv,
                  f_send, f_recv, fw_send, fw_recv, fr_send, fr_recv, own_sem,
                  rows_v, ro_v, hid_v, ho_v, load_sem, part_v, recv_v, s_send, s_recv,
                  wv, wov, rows2_v, gate_v, up_v, late_sem):
    chip, core, ten = _where()
    n_plane = rows_out.shape[0]
    plane, lo = ten // n_lo, ten % n_lo
    right = ((plane + 1) % n_plane) * n_lo + lo
    left = ((plane + n_plane - 1) % n_plane) * n_lo + lo
    side = plane * n_lo + (1 - lo)
    other = (chip, 1 - core, ten)
    barrier = pltpu.get_barrier_semaphore()
    for t in (right, left, side):
        pl.semaphore_signal(barrier, inc=1, device_id=(chip, core, t), device_id_type=MESH)
    for k in range(1, n_chip):
        pl.semaphore_signal(barrier, inc=1, device_id=((chip + k) % n_chip, core, ten),
                            device_id_type=MESH)
    pl.semaphore_signal(barrier, inc=1, device_id=other, device_id_type=MESH)
    pl.semaphore_wait(barrier, 3 + (n_chip - 1) + 1)

    side_cp = pltpu.make_async_remote_copy(
        og_ref, rows_out.at[plane, lo], x_send.at[0], x_recv.at[0],
        device_id=(chip, core, side), device_id_type=MESH)
    side_cp.start()
    own_r = pltpu.make_async_copy(og_ref, rows_out.at[plane, lo], own_sem.at[0])
    own_w = pltpu.make_async_copy(w_ref, w_out.at[chip], own_sem.at[1])
    own_r.start()
    own_w.start()
    act_ld = [pltpu.make_async_copy(gate_hbm, gate_v, late_sem.at[2]),
              pltpu.make_async_copy(up_hbm, up_v, late_sem.at[3])]
    for ld in act_ld:
        ld.start()
    hid_cp = pltpu.make_async_remote_copy(hid_v, ho_v, f_send.at[0], f_recv.at[0],
                                          device_id=other, device_id_type=MESH)
    forwards = [hid_cp]
    w_fwds = []
    rows_fwd = {}
    rows_ld = {}

    def fwd_w(k):
        r = (chip + n_chip - k) % n_chip
        src = w_ref if k == 0 else w_out.at[r]
        cp = pltpu.make_async_remote_copy(src, w_other.at[r], fw_send.at[k], fw_recv.at[k],
                                          device_id=other, device_id_type=MESH)
        cp.start()
        forwards.append(cp)
        w_fwds.append(cp)

    def arrived(d):
        p = (plane + d) % n_plane
        cp = pltpu.make_async_remote_copy(rows_out.at[p, 1 - core], ro_v.at[p],
                                          fr_send.at[d], fr_recv.at[d],
                                          device_id=other, device_id_type=MESH)
        cp.start()
        forwards.append(cp)
        rows_fwd[d] = cp
        ld = pltpu.make_async_copy(rows_out.at[p, core], rows_v.at[p], load_sem.at[d])
        ld.start()
        rows_ld[d] = ld

    def partial(d):
        p = (plane + d) % n_plane
        rows_ld[d].wait()
        rows_fwd[d].wait_recv()
        part = lax.dot_general(rows_v[p], hid_v[...], (((0,), (0,)), ((), ())),
                               preferred_element_type=jnp.float32)
        part += lax.dot_general(ro_v[p], ho_v[...], (((0,), (0,)), ((), ())),
                                preferred_element_type=jnp.float32)
        part_v[p] = part.astype(part_v.dtype)

    fwd_w(0)
    own_r.wait()
    side_cp.wait_send()
    side_cp.wait_recv()
    arrived(0)

    n_steps = n_plane // 2
    ring = {}
    for s in range(n_steps):
        for d, sends, recvs, to, src_plane, half in (
            ("r", r_send, r_recv, right, (plane + n_plane - s) % n_plane, 0),
            ("l", l_send, l_recv, left, (plane + s) % n_plane, 1),
        ):
            block = rows_out.at[src_plane]
            if s == n_steps - 1:
                block = rows_out.at[src_plane, half]
            ring[(d, s)] = pltpu.make_async_remote_copy(
                block, block, sends.at[s], recvs.at[s],
                device_id=(chip, core, to), device_id_type=MESH)
    for d in ("r", "l"):
        ring[(d, 0)].start()
    order = sorted(range(1, n_chip), key=lambda k: abs(k - n_chip // 2))
    w_copies = {}
    for k in order:
        cp = pltpu.make_async_remote_copy(
            w_ref, w_out.at[chip], w_send.at[k], w_recv.at[k],
            device_id=((chip + k) % n_chip, core, ten), device_id_type=MESH)
        cp.start()
        w_copies[k] = cp
    for ld in act_ld:
        ld.wait()
    gate_wide = gate_v[...].astype(jnp.float32)
    sigmoid_gate = jax.nn.sigmoid(gate_wide)
    hid_v[...] = (gate_wide * sigmoid_gate * up_v[...].astype(jnp.float32)).astype(hid_v.dtype)
    hid_cp.start()
    hid_cp.wait_recv()
    pending = [0]
    for s in range(1, n_steps):
        for d in ("r", "l"):
            ring[(d, s - 1)].wait_recv()
            ring[(d, s)].start()
        arrived(n_plane - s)
        arrived(s)
        for d in pending:
            partial(d)
        pending = [n_plane - s, s]
    for d in ("r", "l"):
        ring[(d, n_steps - 1)].wait_recv()
        for s in range(n_steps):
            ring[(d, s)].wait_send()
    arrived(n_steps)
    for d in pending + [n_steps]:
        partial(d)

    outgoing = []

    def send_partial(k):
        p = (chip + k) % n_chip
        send = pltpu.make_async_remote_copy(
            part_v.at[p], recv_v.at[chip], s_send.at[k], s_recv.at[k],
            device_id=(p, core, ten), device_id_type=MESH)
        send.start()
        outgoing.append(send)

    send_partial(order[0])
    for k in order:
        w_copies[k].wait_recv()
        fwd_w(k)
    for k in order[1:]:
        send_partial(k)

    own_w.wait()
    for k in order:
        w_copies[k].wait_send()
    for cp in forwards:
        cp.wait_send()
    for cp in w_fwds:
        cp.wait_recv()

    loads = [pltpu.make_async_copy(src, dst, late_sem.at[i]) for i, (src, dst) in enumerate(
        ((w_out, wv), (w_other, wov)))]
    loads += [pltpu.make_async_copy(rows_out.at[r, 1 - core], rows2_v.at[r],
                                    late_sem.at[4 + r]) for r in range(n_plane)]
    for ld in loads:
        ld.start()
    for ld in loads:
        ld.wait()

    def one_tile(i, carry):
        rows = pl.ds(pl.multiple_of(i * tile, tile), tile)
        acc = jnp.zeros((tile, gate_v.shape[1]), jnp.float32)
        for r in range(n_plane):
            acc += jnp.dot(rows_v[r, rows, :], wv[r], preferred_element_type=jnp.float32)
            acc += jnp.dot(rows2_v[r, rows, :], wov[r], preferred_element_type=jnp.float32)
        gate_wide = gate_v[rows, :].astype(jnp.float32)
        up_wide = up_v[rows, :].astype(jnp.float32)
        sigmoid_gate = jax.nn.sigmoid(gate_wide)
        activated = gate_wide * sigmoid_gate
        gate_out[rows, :] = (
            acc * up_wide * sigmoid_gate * (1.0 + gate_wide * (1.0 - sigmoid_gate))
        ).astype(gate_out.dtype)
        up_out[rows, :] = (acc * activated).astype(up_out.dtype)
        return carry

    lax.fori_loop(0, gate_v.shape[0] // tile, one_tile, 0)

    for send in outgoing:
        send.wait_send()
        send.wait_recv()

    total = part_v[chip].astype(jnp.float32)
    for k in range(1, n_chip):
        total += recv_v[(chip + k) % n_chip].astype(jnp.float32)
    down_out[...] = (total * grad_scale).astype(down_out.dtype)


def body(out_grad, gate_act, up_act, w_down):
    seq_rows, ff = gate_act.shape
    width = w_down.shape[0]
    n_chip = lax.axis_size("chip")
    n_core = lax.axis_size("core")
    n_ten = lax.axis_size("tensor")
    core = lax.axis_index("core")
    grad_scale = 1.0 / math.sqrt(seq_rows * n_chip * n_core)
    hidden = jax.ShapeDtypeStruct(gate_act.shape, jnp.bfloat16)

    n_lo = n_core
    n_plane = n_ten // n_lo
    vmem = pl.BlockSpec(memory_space=pltpu.VMEM)
    rows_shape = (n_plane, seq_rows, out_grad.shape[1])
    gate_grad, up_grad, down_grad, _, _, _ = pl.pallas_call(
        lambda *refs: _fused_kernel(n_chip, n_lo, min(128, seq_rows), grad_scale, *refs),
        out_shape=(
            jax.ShapeDtypeStruct(gate_act.shape, jnp.bfloat16),
            jax.ShapeDtypeStruct(up_act.shape, jnp.bfloat16),
            jax.ShapeDtypeStruct(w_down.shape, jnp.bfloat16),
            jax.ShapeDtypeStruct((n_plane, n_lo, seq_rows, out_grad.shape[1]), out_grad.dtype),
            jax.ShapeDtypeStruct((n_chip, width, ff), w_down.dtype),
            jax.ShapeDtypeStruct((n_chip, width, ff), w_down.dtype),
        ),
        in_specs=[ANY, ANY, ANY, ANY],
        out_specs=(vmem, vmem, vmem, ANY, ANY, ANY),
        scratch_shapes=[pltpu.SemaphoreType.DMA((1,)), pltpu.SemaphoreType.DMA((1,)),
                        pltpu.SemaphoreType.DMA((n_plane // 2,)),
                        pltpu.SemaphoreType.DMA((n_plane // 2,)),
                        pltpu.SemaphoreType.DMA((n_plane // 2,)),
                        pltpu.SemaphoreType.DMA((n_plane // 2,)),
                        pltpu.SemaphoreType.DMA((n_chip,)), pltpu.SemaphoreType.DMA((n_chip,)),
                        pltpu.SemaphoreType.DMA((1,)), pltpu.SemaphoreType.DMA((1,)),
                        pltpu.SemaphoreType.DMA((n_chip,)), pltpu.SemaphoreType.DMA((n_chip,)),
                        pltpu.SemaphoreType.DMA((n_plane,)), pltpu.SemaphoreType.DMA((n_plane,)),
                        pltpu.SemaphoreType.DMA((2,)),
                        pltpu.VMEM(rows_shape, out_grad.dtype),
                        pltpu.VMEM(rows_shape, out_grad.dtype),
                        pltpu.VMEM(hidden.shape, hidden.dtype),
                        pltpu.VMEM(hidden.shape, hidden.dtype),
                        pltpu.SemaphoreType.DMA((n_plane + 1,)),
                        pltpu.VMEM((n_chip, width, ff), jnp.bfloat16),
                        pltpu.VMEM((n_chip, width, ff), jnp.bfloat16),
                        pltpu.SemaphoreType.DMA((n_plane,)), pltpu.SemaphoreType.DMA((n_chip,)),
                        pltpu.VMEM((n_chip, width, ff), w_down.dtype),
                        pltpu.VMEM((n_chip, width, ff), w_down.dtype),
                        pltpu.VMEM(rows_shape, out_grad.dtype),
                        pltpu.VMEM(gate_act.shape, gate_act.dtype),
                        pltpu.VMEM(up_act.shape, up_act.dtype),
                        pltpu.SemaphoreType.DMA((4 + n_plane,))],
        compiler_params=pltpu.CompilerParams(collective_id=0, has_side_effects=True,
                                             vmem_limit_bytes=56 * 1024 * 1024),
    )(out_grad, w_down, gate_act, up_act)
    return (gate_grad, up_grad, down_grad)


def solution(mesh):
    n_dp = mesh.shape["dp"]
    n_tensor = mesh.shape["tensor"]
    devices = np.asarray(mesh.devices).reshape(n_dp // 2, 2, n_tensor)
    split = Mesh(devices, ("chip", "core", "tensor"))
    placed = P(("chip", "core"), "tensor")
    return jax.shard_map(
        body,
        mesh=split,
        in_specs=(placed, placed, placed, placed),
        out_specs=(placed, placed, placed),
        check_vma=False,
    )
```

```python
import math

import jax
import jax.numpy as jnp
import numpy as np
from jax import lax
from jax.experimental import pallas as pl
from jax.experimental.pallas import tpu as pltpu
from jax.sharding import Mesh
from jax.sharding import PartitionSpec as P

MESH = pl.DeviceIdType.MESH
ANY = pl.BlockSpec(memory_space=pl.ANY)


def _where():
    return lax.axis_index("chip"), lax.axis_index("core"), lax.axis_index("tensor")


def _fused_kernel(n_chip, n_lo, tile, grad_scale, og_ref, w_ref, gate_hbm, up_hbm,
                  hg_out, down_out, rows_out, w_out, w_other,
                  x_send, x_recv, r_send, r_recv, l_send, l_recv, w_send, w_recv,
                  f_send, f_recv, fw_send, fw_recv, fr_send, fr_recv, own_sem,
                  rows_v, ro_v, hid_v, ho_v, load_sem, part_v, recv_v, s_send, s_recv,
                  wv, wov, rows2_v, gate_v, up_v, late_sem):
    chip, core, ten = _where()
    n_plane = rows_out.shape[0]
    plane, lo = ten // n_lo, ten % n_lo
    right = ((plane + 1) % n_plane) * n_lo + lo
    left = ((plane + n_plane - 1) % n_plane) * n_lo + lo
    side = plane * n_lo + (1 - lo)
    other = (chip, 1 - core, ten)
    barrier = pltpu.get_barrier_semaphore()
    for t in (right, left, side):
        pl.semaphore_signal(barrier, inc=1, device_id=(chip, core, t), device_id_type=MESH)
    for k in range(1, n_chip):
        pl.semaphore_signal(barrier, inc=1, device_id=((chip + k) % n_chip, core, ten),
                            device_id_type=MESH)
    pl.semaphore_signal(barrier, inc=1, device_id=other, device_id_type=MESH)
    pl.semaphore_wait(barrier, 3 + (n_chip - 1) + 1)

    side_cp = pltpu.make_async_remote_copy(
        og_ref, rows_out.at[plane, lo], x_send.at[0], x_recv.at[0],
        device_id=(chip, core, side), device_id_type=MESH)
    side_cp.start()
    own_r = pltpu.make_async_copy(og_ref, rows_out.at[plane, lo], own_sem.at[0])
    own_w = pltpu.make_async_copy(w_ref, w_out.at[chip], own_sem.at[1])
    own_r.start()
    own_w.start()
    act_ld = [pltpu.make_async_copy(gate_hbm, gate_v, late_sem.at[2]),
              pltpu.make_async_copy(up_hbm, up_v, late_sem.at[3])]
    for ld in act_ld:
        ld.start()
    hid_cp = pltpu.make_async_remote_copy(hid_v, ho_v, f_send.at[0], f_recv.at[0],
                                          device_id=other, device_id_type=MESH)
    forwards = [hid_cp]
    w_fwds = []
    rows_fwd = {}
    rows_ld = {}

    def fwd_w(k):
        r = (chip + n_chip - k) % n_chip
        src = w_ref if k == 0 else w_out.at[r]
        cp = pltpu.make_async_remote_copy(src, w_other.at[r], fw_send.at[k], fw_recv.at[k],
                                          device_id=other, device_id_type=MESH)
        cp.start()
        forwards.append(cp)
        w_fwds.append(cp)

    def arrived(d):
        p = (plane + d) % n_plane
        cp = pltpu.make_async_remote_copy(rows_out.at[p, 1 - core], ro_v.at[p],
                                          fr_send.at[d], fr_recv.at[d],
                                          device_id=other, device_id_type=MESH)
        cp.start()
        forwards.append(cp)
        rows_fwd[d] = cp
        ld = pltpu.make_async_copy(rows_out.at[p, core], rows_v.at[p], load_sem.at[d])
        ld.start()
        rows_ld[d] = ld

    def partial(d):
        p = (plane + d) % n_plane
        rows_ld[d].wait()
        rows_fwd[d].wait_recv()
        part = lax.dot_general(rows_v[p], hid_v[...], (((0,), (0,)), ((), ())),
                               preferred_element_type=jnp.float32)
        part += lax.dot_general(ro_v[p], ho_v[...], (((0,), (0,)), ((), ())),
                                preferred_element_type=jnp.float32)
        part_v[p] = part.astype(part_v.dtype)

    fwd_w(0)
    own_r.wait()
    side_cp.wait_send()
    side_cp.wait_recv()
    arrived(0)

    n_steps = n_plane // 2
    ring = {}
    for s in range(n_steps):
        for d, sends, recvs, to, src_plane, half in (
            ("r", r_send, r_recv, right, (plane + n_plane - s) % n_plane, 0),
            ("l", l_send, l_recv, left, (plane + s) % n_plane, 1),
        ):
            block = rows_out.at[src_plane]
            if s == n_steps - 1:
                block = rows_out.at[src_plane, half]
            ring[(d, s)] = pltpu.make_async_remote_copy(
                block, block, sends.at[s], recvs.at[s],
                device_id=(chip, core, to), device_id_type=MESH)
    for d in ("r", "l"):
        ring[(d, 0)].start()
    order = sorted(range(1, n_chip), key=lambda k: abs(k - n_chip // 2))
    w_copies = {}
    for k in order:
        cp = pltpu.make_async_remote_copy(
            w_ref, w_out.at[chip], w_send.at[k], w_recv.at[k],
            device_id=((chip + k) % n_chip, core, ten), device_id_type=MESH)
        cp.start()
        w_copies[k] = cp
    for ld in act_ld:
        ld.wait()
    gate_wide = gate_v[...].astype(jnp.float32)
    sigmoid_gate = jax.nn.sigmoid(gate_wide)
    hid_v[...] = (gate_wide * sigmoid_gate * up_v[...].astype(jnp.float32)).astype(hid_v.dtype)
    hid_cp.start()
    hid_cp.wait_recv()
    pending = [0]
    for s in range(1, n_steps):
        for d in ("r", "l"):
            ring[(d, s - 1)].wait_recv()
            ring[(d, s)].start()
        arrived(n_plane - s)
        arrived(s)
        for d in pending:
            partial(d)
        pending = [n_plane - s, s]
    for d in ("r", "l"):
        ring[(d, n_steps - 1)].wait_recv()
        for s in range(n_steps):
            ring[(d, s)].wait_send()
    arrived(n_steps)
    for d in pending + [n_steps]:
        partial(d)

    for k in order:
        w_copies[k].wait_recv()
        fwd_w(k)
    outgoing = []
    for k in order:
        p = (chip + k) % n_chip
        send = pltpu.make_async_remote_copy(
            part_v.at[p], recv_v.at[chip], s_send.at[k], s_recv.at[k],
            device_id=(p, core, ten), device_id_type=MESH)
        send.start()
        outgoing.append(send)

    own_w.wait()
    for k in order:
        w_copies[k].wait_send()
    for cp in forwards:
        cp.wait_send()
    for cp in w_fwds:
        cp.wait_recv()

    loads = [pltpu.make_async_copy(src, dst, late_sem.at[i]) for i, (src, dst) in enumerate(
        ((w_out, wv), (w_other, wov)))]
    loads += [pltpu.make_async_copy(rows_out.at[r, 1 - core], rows2_v.at[r],
                                    late_sem.at[4 + r]) for r in range(n_plane)]
    for ld in loads:
        ld.start()
    for ld in loads:
        ld.wait()

    def one_tile(i, carry):
        rows = pl.ds(pl.multiple_of(i * tile, tile), tile)
        acc = jnp.zeros((tile, gate_v.shape[1]), jnp.float32)
        for r in range(n_plane):
            acc += jnp.dot(rows_v[r, rows, :], wv[r], preferred_element_type=jnp.float32)
            acc += jnp.dot(rows2_v[r, rows, :], wov[r], preferred_element_type=jnp.float32)
        hg_out[rows, :] = acc
        return carry

    lax.fori_loop(0, gate_v.shape[0] // tile, one_tile, 0)

    for send in outgoing:
        send.wait_send()
        send.wait_recv()

    total = part_v[chip].astype(jnp.float32)
    for k in range(1, n_chip):
        total += recv_v[(chip + k) % n_chip].astype(jnp.float32)
    down_out[...] = (total * grad_scale).astype(down_out.dtype)


def body(out_grad, gate_act, up_act, w_down):
    seq_rows, ff = gate_act.shape
    width = w_down.shape[0]
    n_chip = lax.axis_size("chip")
    n_core = lax.axis_size("core")
    n_ten = lax.axis_size("tensor")
    core = lax.axis_index("core")
    grad_scale = 1.0 / math.sqrt(seq_rows * n_chip * n_core)
    hidden = jax.ShapeDtypeStruct(gate_act.shape, jnp.bfloat16)

    n_lo = n_core
    n_plane = n_ten // n_lo
    vmem = pl.BlockSpec(memory_space=pltpu.VMEM)
    rows_shape = (n_plane, seq_rows, out_grad.shape[1])
    hidden_grad, down_grad, _, _, _ = pl.pallas_call(
        lambda *refs: _fused_kernel(n_chip, n_lo, min(128, seq_rows), grad_scale, *refs),
        out_shape=(
            jax.ShapeDtypeStruct(gate_act.shape, jnp.float32),
            jax.ShapeDtypeStruct(w_down.shape, jnp.bfloat16),
            jax.ShapeDtypeStruct((n_plane, n_lo, seq_rows, out_grad.shape[1]), out_grad.dtype),
            jax.ShapeDtypeStruct((n_chip, width, ff), w_down.dtype),
            jax.ShapeDtypeStruct((n_chip, width, ff), w_down.dtype),
        ),
        in_specs=[ANY, ANY, ANY, ANY],
        out_specs=(vmem, vmem, ANY, ANY, ANY),
        scratch_shapes=[pltpu.SemaphoreType.DMA((1,)), pltpu.SemaphoreType.DMA((1,)),
                        pltpu.SemaphoreType.DMA((n_plane // 2,)),
                        pltpu.SemaphoreType.DMA((n_plane // 2,)),
                        pltpu.SemaphoreType.DMA((n_plane // 2,)),
                        pltpu.SemaphoreType.DMA((n_plane // 2,)),
                        pltpu.SemaphoreType.DMA((n_chip,)), pltpu.SemaphoreType.DMA((n_chip,)),
                        pltpu.SemaphoreType.DMA((1,)), pltpu.SemaphoreType.DMA((1,)),
                        pltpu.SemaphoreType.DMA((n_chip,)), pltpu.SemaphoreType.DMA((n_chip,)),
                        pltpu.SemaphoreType.DMA((n_plane,)), pltpu.SemaphoreType.DMA((n_plane,)),
                        pltpu.SemaphoreType.DMA((2,)),
                        pltpu.VMEM(rows_shape, out_grad.dtype),
                        pltpu.VMEM(rows_shape, out_grad.dtype),
                        pltpu.VMEM(hidden.shape, hidden.dtype),
                        pltpu.VMEM(hidden.shape, hidden.dtype),
                        pltpu.SemaphoreType.DMA((n_plane + 1,)),
                        pltpu.VMEM((n_chip, width, ff), jnp.bfloat16),
                        pltpu.VMEM((n_chip, width, ff), jnp.bfloat16),
                        pltpu.SemaphoreType.DMA((n_plane,)), pltpu.SemaphoreType.DMA((n_chip,)),
                        pltpu.VMEM((n_chip, width, ff), w_down.dtype),
                        pltpu.VMEM((n_chip, width, ff), w_down.dtype),
                        pltpu.VMEM(rows_shape, out_grad.dtype),
                        pltpu.VMEM(gate_act.shape, gate_act.dtype),
                        pltpu.VMEM(up_act.shape, up_act.dtype),
                        pltpu.SemaphoreType.DMA((4 + n_plane,))],
        compiler_params=pltpu.CompilerParams(collective_id=0, has_side_effects=True,
                                             vmem_limit_bytes=56 * 1024 * 1024),
    )(out_grad, w_down, gate_act, up_act)
    gate_wide = gate_act.astype(jnp.float32)
    up_wide = up_act.astype(jnp.float32)
    sigmoid_gate = jax.nn.sigmoid(gate_wide)
    activated = gate_wide * sigmoid_gate
    gate_grad = (
        hidden_grad * up_wide * sigmoid_gate * (1.0 + gate_wide * (1.0 - sigmoid_gate))
    ).astype(jnp.bfloat16)
    up_grad = (hidden_grad * activated).astype(jnp.bfloat16)
    return (gate_grad, up_grad, down_grad)


def solution(mesh):
    n_dp = mesh.shape["dp"]
    n_tensor = mesh.shape["tensor"]
    devices = np.asarray(mesh.devices).reshape(n_dp // 2, 2, n_tensor)
    split = Mesh(devices, ("chip", "core", "tensor"))
    placed = P(("chip", "core"), "tensor")
    return jax.shard_map(
        body,
        mesh=split,
        in_specs=(placed, placed, placed, placed),
        out_specs=(placed, placed, placed),
        check_vma=False,
    )
```

```python
import math

import jax
import jax.numpy as jnp
import numpy as np
from jax import lax
from jax.experimental import pallas as pl
from jax.experimental.pallas import tpu as pltpu
from jax.sharding import Mesh
from jax.sharding import PartitionSpec as P

MESH = pl.DeviceIdType.MESH
ANY = pl.BlockSpec(memory_space=pl.ANY)


def _where():
    return lax.axis_index("chip"), lax.axis_index("core"), lax.axis_index("tensor")


def _fused_kernel(n_chip, n_lo, tile, grad_scale, og_ref, w_ref, gate_hbm, up_hbm,
                  hg_out, down_out, rows_out, w_out, w_other,
                  x_send, x_recv, r_send, r_recv, l_send, l_recv, w_send, w_recv,
                  f_send, f_recv, fw_send, fw_recv, fr_send, fr_recv, own_sem,
                  rows_v, ro_v, hid_v, ho_v, load_sem, part_v, recv_v, s_send, s_recv,
                  wv, wov, rows2_v, gate_v, up_v, late_sem):
    chip, core, ten = _where()
    n_plane = rows_out.shape[0]
    plane, lo = ten // n_lo, ten % n_lo
    right = ((plane + 1) % n_plane) * n_lo + lo
    left = ((plane + n_plane - 1) % n_plane) * n_lo + lo
    side = plane * n_lo + (1 - lo)
    other = (chip, 1 - core, ten)
    barrier = pltpu.get_barrier_semaphore()
    for t in (right, left, side):
        pl.semaphore_signal(barrier, inc=1, device_id=(chip, core, t), device_id_type=MESH)
    for k in range(1, n_chip):
        pl.semaphore_signal(barrier, inc=1, device_id=((chip + k) % n_chip, core, ten),
                            device_id_type=MESH)
    pl.semaphore_signal(barrier, inc=1, device_id=other, device_id_type=MESH)
    pl.semaphore_wait(barrier, 3 + (n_chip - 1) + 1)

    side_cp = pltpu.make_async_remote_copy(
        og_ref, rows_out.at[plane, lo], x_send.at[0], x_recv.at[0],
        device_id=(chip, core, side), device_id_type=MESH)
    side_cp.start()
    own_r = pltpu.make_async_copy(og_ref, rows_out.at[plane, lo], own_sem.at[0])
    own_w = pltpu.make_async_copy(w_ref, w_out.at[chip], own_sem.at[1])
    own_r.start()
    own_w.start()
    act_ld = [pltpu.make_async_copy(gate_hbm, gate_v, late_sem.at[2]),
              pltpu.make_async_copy(up_hbm, up_v, late_sem.at[3])]
    for ld in act_ld:
        ld.start()
    hid_cp = pltpu.make_async_remote_copy(hid_v, ho_v, f_send.at[0], f_recv.at[0],
                                          device_id=other, device_id_type=MESH)
    forwards = [hid_cp]
    w_fwds = []
    rows_fwd = {}
    rows_ld = {}

    def fwd_w(k):
        r = (chip + n_chip - k) % n_chip
        src = w_ref if k == 0 else w_out.at[r]
        cp = pltpu.make_async_remote_copy(src, w_other.at[r], fw_send.at[k], fw_recv.at[k],
                                          device_id=other, device_id_type=MESH)
        cp.start()
        forwards.append(cp)
        w_fwds.append(cp)

    def arrived(d):
        p = (plane + d) % n_plane
        cp = pltpu.make_async_remote_copy(rows_out.at[p, 1 - core], ro_v.at[p],
                                          fr_send.at[d], fr_recv.at[d],
                                          device_id=other, device_id_type=MESH)
        cp.start()
        forwards.append(cp)
        rows_fwd[d] = cp
        ld = pltpu.make_async_copy(rows_out.at[p, core], rows_v.at[p], load_sem.at[d])
        ld.start()
        rows_ld[d] = ld

    def partial(d):
        p = (plane + d) % n_plane
        rows_ld[d].wait()
        rows_fwd[d].wait_recv()
        part = lax.dot_general(rows_v[p], hid_v[...], (((0,), (0,)), ((), ())),
                               preferred_element_type=jnp.float32)
        part += lax.dot_general(ro_v[p], ho_v[...], (((0,), (0,)), ((), ())),
                                preferred_element_type=jnp.float32)
        part_v[p] = part.astype(part_v.dtype)

    fwd_w(0)
    own_r.wait()
    side_cp.wait_send()
    side_cp.wait_recv()
    arrived(0)

    n_steps = n_plane // 2
    ring = {}
    for s in range(n_steps):
        for d, sends, recvs, to, src_plane, half in (
            ("r", r_send, r_recv, right, (plane + n_plane - s) % n_plane, 0),
            ("l", l_send, l_recv, left, (plane + s) % n_plane, 1),
        ):
            block = rows_out.at[src_plane]
            if s == n_steps - 1:
                block = rows_out.at[src_plane, half]
            ring[(d, s)] = pltpu.make_async_remote_copy(
                block, block, sends.at[s], recvs.at[s],
                device_id=(chip, core, to), device_id_type=MESH)
    for d in ("r", "l"):
        ring[(d, 0)].start()
    order = sorted(range(1, n_chip), key=lambda k: abs(k - n_chip // 2))
    w_copies = {}
    for k in order:
        cp = pltpu.make_async_remote_copy(
            w_ref, w_out.at[chip], w_send.at[k], w_recv.at[k],
            device_id=((chip + k) % n_chip, core, ten), device_id_type=MESH)
        cp.start()
        w_copies[k] = cp
    for ld in act_ld:
        ld.wait()
    gate_wide = gate_v[...].astype(jnp.float32)
    sigmoid_gate = jax.nn.sigmoid(gate_wide)
    hid_v[...] = (gate_wide * sigmoid_gate * up_v[...].astype(jnp.float32)).astype(hid_v.dtype)
    hid_cp.start()
    hid_cp.wait_recv()
    pending = [0]
    for s in range(1, n_steps):
        for d in ("r", "l"):
            ring[(d, s - 1)].wait_recv()
            ring[(d, s)].start()
        arrived(n_plane - s)
        arrived(s)
        for d in pending:
            partial(d)
        pending = [n_plane - s, s]
    for d in ("r", "l"):
        ring[(d, n_steps - 1)].wait_recv()
        for s in range(n_steps):
            ring[(d, s)].wait_send()
    arrived(n_steps)
    for d in pending + [n_steps]:
        partial(d)

    for k in order:
        w_copies[k].wait_recv()
        fwd_w(k)
    outgoing = []
    for k in order:
        p = (chip + k) % n_chip
        send = pltpu.make_async_remote_copy(
            part_v.at[p], recv_v.at[chip], s_send.at[k], s_recv.at[k],
            device_id=(p, core, ten), device_id_type=MESH)
        send.start()
        outgoing.append(send)

    own_w.wait()
    for k in order:
        w_copies[k].wait_send()
    for cp in forwards:
        cp.wait_send()
    for cp in w_fwds:
        cp.wait_recv()

    loads = [pltpu.make_async_copy(src, dst, late_sem.at[i]) for i, (src, dst) in enumerate(
        ((w_out, wv), (w_other, wov)))]
    loads += [pltpu.make_async_copy(rows_out.at[r, 1 - core], rows2_v.at[r],
                                    late_sem.at[4 + r]) for r in range(n_plane)]
    for ld in loads:
        ld.start()
    for ld in loads:
        ld.wait()

    def one_tile(i, carry):
        rows = pl.ds(pl.multiple_of(i * tile, tile), tile)
        acc = jnp.zeros((tile, gate_v.shape[1]), jnp.float32)
        for r in range(n_plane):
            acc += jnp.dot(rows_v[r, rows, :], wv[r], preferred_element_type=jnp.float32)
            acc += jnp.dot(rows2_v[r, rows, :], wov[r], preferred_element_type=jnp.float32)
        hg_out[rows, :] = acc
        return carry

    lax.fori_loop(0, gate_v.shape[0] // tile, one_tile, 0)

    for send in outgoing:
        send.wait_send()
        send.wait_recv()

    total = part_v[chip].astype(jnp.float32)
    for k in range(1, n_chip):
        total += recv_v[(chip + k) % n_chip].astype(jnp.float32)
    down_out[...] = total


def body(out_grad, gate_act, up_act, w_down):
    seq_rows, ff = gate_act.shape
    width = w_down.shape[0]
    n_chip = lax.axis_size("chip")
    n_core = lax.axis_size("core")
    n_ten = lax.axis_size("tensor")
    core = lax.axis_index("core")
    grad_scale = 1.0 / math.sqrt(seq_rows * n_chip * n_core)
    hidden = jax.ShapeDtypeStruct(gate_act.shape, jnp.bfloat16)

    n_lo = n_core
    n_plane = n_ten // n_lo
    vmem = pl.BlockSpec(memory_space=pltpu.VMEM)
    rows_shape = (n_plane, seq_rows, out_grad.shape[1])
    hidden_grad, summed, _, _, _ = pl.pallas_call(
        lambda *refs: _fused_kernel(n_chip, n_lo, min(128, seq_rows), grad_scale, *refs),
        out_shape=(
            jax.ShapeDtypeStruct(gate_act.shape, jnp.float32),
            jax.ShapeDtypeStruct(w_down.shape, jnp.float32),
            jax.ShapeDtypeStruct((n_plane, n_lo, seq_rows, out_grad.shape[1]), out_grad.dtype),
            jax.ShapeDtypeStruct((n_chip, width, ff), w_down.dtype),
            jax.ShapeDtypeStruct((n_chip, width, ff), w_down.dtype),
        ),
        in_specs=[ANY, ANY, ANY, ANY],
        out_specs=(vmem, vmem, ANY, ANY, ANY),
        scratch_shapes=[pltpu.SemaphoreType.DMA((1,)), pltpu.SemaphoreType.DMA((1,)),
                        pltpu.SemaphoreType.DMA((n_plane // 2,)),
                        pltpu.SemaphoreType.DMA((n_plane // 2,)),
                        pltpu.SemaphoreType.DMA((n_plane // 2,)),
                        pltpu.SemaphoreType.DMA((n_plane // 2,)),
                        pltpu.SemaphoreType.DMA((n_chip,)), pltpu.SemaphoreType.DMA((n_chip,)),
                        pltpu.SemaphoreType.DMA((1,)), pltpu.SemaphoreType.DMA((1,)),
                        pltpu.SemaphoreType.DMA((n_chip,)), pltpu.SemaphoreType.DMA((n_chip,)),
                        pltpu.SemaphoreType.DMA((n_plane,)), pltpu.SemaphoreType.DMA((n_plane,)),
                        pltpu.SemaphoreType.DMA((2,)),
                        pltpu.VMEM(rows_shape, out_grad.dtype),
                        pltpu.VMEM(rows_shape, out_grad.dtype),
                        pltpu.VMEM(hidden.shape, hidden.dtype),
                        pltpu.VMEM(hidden.shape, hidden.dtype),
                        pltpu.SemaphoreType.DMA((n_plane + 1,)),
                        pltpu.VMEM((n_chip, width, ff), jnp.bfloat16),
                        pltpu.VMEM((n_chip, width, ff), jnp.bfloat16),
                        pltpu.SemaphoreType.DMA((n_plane,)), pltpu.SemaphoreType.DMA((n_chip,)),
                        pltpu.VMEM((n_chip, width, ff), w_down.dtype),
                        pltpu.VMEM((n_chip, width, ff), w_down.dtype),
                        pltpu.VMEM(rows_shape, out_grad.dtype),
                        pltpu.VMEM(gate_act.shape, gate_act.dtype),
                        pltpu.VMEM(up_act.shape, up_act.dtype),
                        pltpu.SemaphoreType.DMA((4 + n_plane,))],
        compiler_params=pltpu.CompilerParams(collective_id=0, has_side_effects=True,
                                             vmem_limit_bytes=56 * 1024 * 1024),
    )(out_grad, w_down, gate_act, up_act)
    gate_wide = gate_act.astype(jnp.float32)
    up_wide = up_act.astype(jnp.float32)
    sigmoid_gate = jax.nn.sigmoid(gate_wide)
    activated = gate_wide * sigmoid_gate
    gate_grad = (
        hidden_grad * up_wide * sigmoid_gate * (1.0 + gate_wide * (1.0 - sigmoid_gate))
    ).astype(jnp.bfloat16)
    up_grad = (hidden_grad * activated).astype(jnp.bfloat16)
    down_grad = (summed * grad_scale).astype(jnp.bfloat16)
    return (gate_grad, up_grad, down_grad)


def solution(mesh):
    n_dp = mesh.shape["dp"]
    n_tensor = mesh.shape["tensor"]
    devices = np.asarray(mesh.devices).reshape(n_dp // 2, 2, n_tensor)
    split = Mesh(devices, ("chip", "core", "tensor"))
    placed = P(("chip", "core"), "tensor")
    return jax.shard_map(
        body,
        mesh=split,
        in_specs=(placed, placed, placed, placed),
        out_specs=(placed, placed, placed),
        check_vma=False,
    )
```
